32 devices in a mesh: parts: 1, node: 4 (over y, x), local: 8 (over z, core).
Axes of the slice: x: 2, y: 2, z: 4, core: 2. Of those that a mesh axis runs over, the one named last changes fastest.
Arguments:
- tokens: bfloat16 [2048, 4096], P(('parts', 'node', 'local')), may hold values from -6 to 6
- expert_ids: int32 [2048, 8], P(('parts', 'node', 'local')), may hold values from 0 to 15, all different within a row; in each aligned block of 64 rows (0 to 63, 64 to 127, ...) at most 40 rows name the same one
- gate_weights: float32 [2048, 8], P(('parts', 'node', 'local')), may hold values from 0.02 to 0.5
- w_gate: bfloat16 [4096, 12288], P(None, ('parts', 'node', 'local')), may hold values from -0.09375 to 0.09375
- w_up: bfloat16 [4096, 12288], P(None, ('parts', 'node', 'local')), may hold values from -0.09375 to 0.09375
- w_down: bfloat16 [12288, 4096], P(('parts', 'node', 'local')), may hold values from -0.21875 to 0.21875
Outputs:
- mixed: bfloat16 [2048, 4096], P(('parts', 'node', 'local'))
The draws below stay inside these ranges and needn't reach their ends.
Inputs may be any that keep to these rules, and one draw needn't show every extreme that they name: `expert_ids`: each token names 8 different experts; among the 64 tokens of one device no expert is named more than 40 times, and in some such block one expert is named exactly 40 times.
All inputs are finite; a program needn't handle non-finite values.
Results may differ from the reference program's by a relative error of at most 0.0058.
Values may be sent and summed in bfloat16 or wider, within the bound.
A program may use at most 128 MiB of HBM per device.

```python
import math
import jax
import jax.numpy as jnp
import numpy as np
from jax import lax

D = 4096
FF = 768
TOPK = 8
TOK_DEV = 64
EXPERTS = 16
CAP = 40
TOKENS = 2048


def levels(stream_key, extent, pieces, smallest, top_value):
    level = 1.0
    for dim, blocks in pieces:
        steps = jax.random.uniform(jax.random.fold_in(jax.random.fold_in(stream_key, 6), dim), (blocks,), jnp.float32, smallest / len(pieces), top_value / len(pieces))
        level = level * jnp.repeat(jnp.exp(steps), extent[dim] // blocks).reshape((-1,) + (1,) * (len(extent) - 1 - dim))
    return level


def routed_block(stream_key, own, number, rows, number_of, top, reach, skew):
    order = jax.random.permutation(stream_key, number_of)
    packed, usual = portions_of(number_of, rows * top, reach, skew, True), portions_of(number_of, rows * top, reach, skew, False)
    places = jnp.arange(number_of)

    def named(tallies, rotation):
        used = int((tallies > 0).sum())
        fixed = max(1, used // 4)
        passed = fixed + (places - fixed + rotation * (used - fixed)) % max(1, number_of - fixed)
        return jnp.zeros((number_of,), jnp.int32).at[order[jnp.where(places < fixed, places, passed)]].set(jnp.asarray(tallies, jnp.int32))

    tallies = jnp.where(number % 4 == 0, named(packed, number // 4), named(usual, number - number // 4 - 1))
    mixed = jax.random.permutation(jax.random.fold_in(own, 3), number_of)
    donor, receiver = mixed[0:number_of // 2 * 2:2], mixed[1:number_of // 2 * 2:2]
    margin = jnp.minimum(tallies[donor] - 1, reach - tallies[receiver]) // 2
    margin = jnp.where((donor == order[0]) | (receiver == order[0]) | (tallies[receiver] == 0), 0, jnp.maximum(margin, 0))
    passed = jax.random.randint(jax.random.fold_in(own, 4), (number_of // 2,), 0, 1 << 20) % (margin + 1)
    tallies = tallies.at[donor].add(-passed).at[receiver].add(passed)
    labels = jnp.searchsorted(jnp.cumsum(tallies), jnp.arange(rows * top), side="right").astype(jnp.int32)
    grid = labels.reshape(top, rows).T
    grid = grid[jax.random.permutation(jax.random.fold_in(own, 1), rows)]
    rotation = jax.random.randint(jax.random.fold_in(own, 2), (rows, 1), 0, top)
    return jnp.take_along_axis(grid, (jnp.arange(top)[None, :] + rotation) % top, axis=1)


def portions_of(amount, total, bound, skew, full):
    loads = [(1 << 20) // math.isqrt(standing ** skew) + 1 for standing in range(1, amount + 1)]
    largest = bound if full else min(bound, max(-(-total // amount), total * loads[0] // sum(loads)))
    least = 1 if total - largest >= amount - 1 else 0
    holding, spare = [largest] + [least] * (amount - 1), total - largest - least * (amount - 1)
    while spare > 0:
        movable = [i for i in range(1, amount) if holding[i] < largest] or [i for i in range(1, amount) if holding[i] < bound]
        whole, left = sum([loads[i] for i in movable]), spare
        for i in movable:
            more = min(bound - holding[i], max(1, left * loads[i] // whole), spare)
            holding[i] = holding[i] + more
            spare = spare - more
    return np.array(holding)


def gaussian(key, shape, width, reach, split=(), held_as=jnp.bfloat16):
    loudness = levels(key, shape, split, -0.22, 0.18) if split else 1.0
    array = jax.random.normal(key, shape, jnp.float32) * width * loudness
    return jnp.minimum(jnp.maximum(array, -reach), reach).astype(held_as)


def setup_inputs(seed: int = 0, part: int = 0) -> dict:
    streams_of = jax.random.split(jax.random.key(seed), 7)
    part_keys = jax.random.split(jax.random.fold_in(streams_of[6], part), 7)
    tokens = gaussian(part_keys[0], (TOKENS, D), 1.0, 6.0, ((0, 32),))
    expert_ids_keys = jax.random.split(jax.random.fold_in(part_keys[1], 1), TOKENS // TOK_DEV)
    expert_ids_turns = jax.random.permutation(jax.random.fold_in(part_keys[1], 3), TOKENS // TOK_DEV)
    expert_ids = jax.vmap(lambda own, number: routed_block(jax.random.fold_in(part_keys[1], 2), own, number, TOK_DEV, EXPERTS, TOPK, CAP, 2))(expert_ids_keys, expert_ids_turns).reshape((TOKENS, TOPK))
    gate_weights = jnp.clip(jnp.exp(math.log(0.5) - 3.218876 * jax.random.uniform(part_keys[2], (TOKENS, TOPK), jnp.float32) ** levels(part_keys[2], (TOKENS, TOPK), ((0, 32),), -0.2, 0.2)), 0.02, 0.5)
    w_gate = gaussian(part_keys[3], (D, EXPERTS * FF), D ** -0.5, 0.09375, ((1, 32),))
    w_up = gaussian(part_keys[4], (D, EXPERTS * FF), D ** -0.5, 0.09375, ((1, 32),))
    w_down = gaussian(part_keys[5], (EXPERTS * FF, D), FF ** -0.5, 0.21875, ((0, 32),))
    return dict(tokens=tokens, expert_ids=expert_ids, gate_weights=gate_weights, w_gate=w_gate, w_up=w_up, w_down=w_down)


def reference(tokens, expert_ids, gate_weights, w_gate, w_up, w_down):
    groups = TOKENS // TOK_DEV
    pairs = TOK_DEV * TOPK
    block_ids = expert_ids.reshape(groups, pairs)
    one_hot = (block_ids[:, :, None] == jnp.arange(EXPERTS, dtype=jnp.int32)[None, None, :]).astype(jnp.int32)
    earlier = jnp.cumsum(one_hot, axis=1) - one_hot
    slot_rank = jnp.sum(earlier * one_hot, axis=2).astype(jnp.int32)
    token_index = jnp.broadcast_to(jnp.arange(TOKENS, dtype=jnp.int32).reshape(groups, TOK_DEV, 1), (groups, TOK_DEV, TOPK)).reshape(groups, pairs)
    block_index = jnp.broadcast_to(jnp.arange(groups, dtype=jnp.int32)[:, None], (groups, pairs))
    table = jnp.zeros((EXPERTS, groups, CAP), jnp.int32).at[block_ids, block_index, slot_rank].set(token_index)
    filled = jnp.zeros((EXPERTS, groups, CAP), jnp.float32).at[block_ids, block_index, slot_rank].set(1.0)

    def expert_out(expert):
        rows = tokens[table[expert].reshape(-1)]
        rows = (rows.astype(jnp.float32) * filled[expert].reshape(-1, 1)).astype(jnp.bfloat16)
        start = (expert * FF).astype(jnp.int32)
        gate_cols = lax.dynamic_slice_in_dim(w_gate, start, FF, 1)
        up_cols = lax.dynamic_slice_in_dim(w_up, start, FF, 1)
        down_rows = lax.dynamic_slice_in_dim(w_down, start, FF, 0)
        gate = jnp.dot(rows, gate_cols, preferred_element_type=jnp.float32)
        upper = jnp.dot(rows, up_cols, preferred_element_type=jnp.float32)
        hidden = (jax.nn.silu(gate) * upper).astype(jnp.bfloat16)
        return jnp.dot(hidden, down_rows, preferred_element_type=jnp.float32).astype(jnp.bfloat16)

    outputs = lax.map(expert_out, jnp.arange(EXPERTS, dtype=jnp.int32))

    def combine(block):
        chosen_ids = lax.dynamic_index_in_dim(block_ids, block, 0, keepdims=False)
        ranks = lax.dynamic_index_in_dim(slot_rank, block, 0, keepdims=False)
        chosen = outputs[chosen_ids, block * CAP + ranks].reshape(TOK_DEV, TOPK, D)
        weights = lax.dynamic_slice_in_dim(gate_weights, (block * TOK_DEV).astype(jnp.int32), TOK_DEV, 0)
        return jnp.sum(weights[:, :, None] * chosen.astype(jnp.float32), axis=1).astype(jnp.bfloat16)

    mixed = lax.map(combine, jnp.arange(groups, dtype=jnp.int32))
    return mixed.reshape(TOKENS, D)
```

```python
import functools

import jax
import jax.numpy as jnp
from jax import lax
from jax.experimental import pallas as pl
from jax.experimental.pallas import tpu as pltpu
from jax.sharding import PartitionSpec as P

MESH = pl.DeviceIdType.MESH


def partner_2(value, axis, bit):
    mask = 2**bit
    pairs = [(source, source ^ mask) for source in range(lax.axis_size(axis))]
    return lax.ppermute(value, axis, pairs)


def by_slots(tokens, expert_ids, gate_weights, w_gate, w_up, w_down):
    node_count = lax.axis_size("node")
    local_count = lax.axis_size("local")
    devices = node_count * local_count
    experts = devices // 2
    tok_rows, top_count = expert_ids.shape
    width = tokens.shape[1]
    capacity = tok_rows * top_count * 5 // (4 * experts)
    flat_ids = expert_ids.reshape(-1)
    one_hot = (flat_ids[:, None] == jnp.arange(experts, dtype=jnp.int32)[None, :]).astype(jnp.int32)
    earlier = jnp.cumsum(one_hot, axis=0) - one_hot
    slot_rank = jnp.sum(earlier * one_hot, axis=1)
    slot_index = (flat_ids * capacity + slot_rank).reshape(tok_rows, top_count)
    slot_table = jnp.any(
        slot_index[None, :, :] == jnp.arange(experts * capacity, dtype=jnp.int32)[:, None, None],
        axis=2,
    ).astype(jnp.bfloat16)
    outgoing = jnp.dot(slot_table, tokens, preferred_element_type=jnp.float32).astype(jnp.bfloat16)
    outgoing = outgoing.reshape(devices, capacity // 2, width)
    partner = partner_2((w_gate, w_up, w_down), "local", 0)
    full_gate = jnp.concatenate([w_gate, partner[0]], axis=1)
    full_up = jnp.concatenate([w_up, partner[1]], axis=1)
    full_down = jnp.concatenate([w_down, partner[2]], axis=0)
    block = lax.all_to_all(outgoing, ("node", "local"), split_axis=0, concat_axis=0, tiled=True)
    rows = block.reshape(-1, width)
    gate = jnp.dot(rows, full_gate, preferred_element_type=jnp.float32)
    upper = jnp.dot(rows, full_up, preferred_element_type=jnp.float32)
    hidden = (jax.nn.silu(gate) * upper).astype(jnp.bfloat16)
    result = jnp.dot(hidden, full_down, preferred_element_type=jnp.float32).astype(jnp.bfloat16)
    processed = result.reshape(block.shape)
    returned = lax.all_to_all(processed, ("node", "local"), split_axis=0, concat_axis=0, tiled=True)
    results = returned.reshape(experts * capacity, width)
    chosen = results[slot_index]
    mixed = jnp.sum(gate_weights[:, :, None] * chosen.astype(jnp.float32), axis=1)
    return mixed.astype(jnp.bfloat16)


LANES = 128


def layer_kernel(
    nodes, columns, capacity,
    rows_ref, ids_ref, weights_ref, gate_ref, up_ref, down_ref, out_ref,
    ids, weights, tables, shares, picks, spreads,
    first, second, dense, halves, packed, outs, passes, acts, hidden,
    results, relays, compacts, relayed, sums, totals, finals, output,
    load_sem, swap_send, swap_recv, line_send, line_recv, list_send, list_recv,
    half_send, half_recv, note_send, note_recv, pack_send, pack_recv, pass_send, pass_recv,
    far_send, far_recv, near_send, near_recv, sum_send, sum_recv, end_send, end_recv,
):
    part, node, local = lax.axis_index("parts"), lax.axis_index("node"), lax.axis_index("local")
    column, core = local // 2, lax.rem(local, 2)
    high, low = node // 2, lax.rem(node, 2)
    count, width = rows_ref.shape
    hidden_half = gate_ref.shape[1]
    split = width // 2
    slots = 4
    bf16, f32 = jnp.bfloat16, jnp.float32
    inner = (column == 1) | (column == 2)

    def at(node_index, local_index):
        return (part, node_index, local_index)

    sides = (at(high * 2 + 1 - low, local), at((1 - high) * 2 + low, local))
    side_nodes = (high * 2 + 1 - low, (1 - high) * 2 + low)
    twin = at(node, column * 2 + 1 - core)
    low_flip = column + 1 - 2 * lax.rem(column, 2)
    beside = at(node, low_flip * 2 + core)
    across = at(node, (columns - 1 - column) * 2 + core)
    apart = at(node, (columns - 1 - low_flip) * 2 + core)
    later = jnp.where(inner, 2, 3)

    barrier = pltpu.get_barrier_semaphore()
    greeted = (*sides, twin, beside, across, apart)
    for peer in greeted:
        pl.semaphore_signal(barrier, inc=1, device_id=peer, device_id_type=MESH)
    pl.semaphore_wait(barrier, len(greeted))

    everything, inner_only = [], []

    def send(source, target, send_sem, recv_sem, peer):
        return pltpu.make_async_remote_copy(
            src_ref=source, dst_ref=target, send_sem=send_sem, recv_sem=recv_sem,
            device_id=peer, device_id_type=MESH,
        )

    def start(copy):
        copy.start()
        everything.append(copy)
        return copy

    def columns_of(side):
        return pl.ds(side * split, split)

    def own(slot):
        return pl.ds(slot * capacity, capacity)

    half_in = {}
    line_in = {}
    list_in = {}
    note_in = {}
    pack_in = {}
    pass_in = {}

    def send_halves(step, source):
        for side in (0, 1):
            half_in[step, side] = start(send(source.at[:, columns_of(side)], halves.at[step, side], half_send.at[step, side], half_recv.at[step, side], sides[side]))

    send_halves(0, rows_ref)
    line_in[1] = start(send(rows_ref, dense.at[1], line_send.at[0], line_recv.at[1], beside))
    to_across = send(rows_ref, dense.at[2], line_send.at[1], line_recv.at[2], across)
    pass_across = send(dense.at[1], dense.at[3], line_send.at[2], line_recv.at[3], across)
    pass_beside = (
        send(dense.at[2], dense.at[2], line_send.at[3], line_recv.at[2], beside),
        send(dense.at[3], dense.at[3], line_send.at[4], line_recv.at[3], beside),
    )
    line_in[2], line_in[3] = to_across, pass_across

    @pl.when(inner)
    def _():
        to_across.start()

    first_loads = [
        pltpu.make_async_copy(ids_ref, ids, load_sem.at[0]),
        pltpu.make_async_copy(weights_ref, weights, load_sem.at[1]),
        pltpu.make_async_copy(rows_ref, dense.at[0], load_sem.at[2]),
    ]
    for copy in first_loads:
        copy.start()

    def spot(target, index, by_rows, other):
        place = pl.ds((index + other) * hidden_half, hidden_half)
        return target.at[place] if by_rows else target.at[:, place]

    near = ((gate_ref, first, 0, False), (up_ref, first, 1, False), (down_ref, second, 0, True))
    swaps, loads = [], []
    for number, (source, target, index, by_rows) in enumerate(near):
        swaps.append(start(send(source, spot(target, index, by_rows, 1 if by_rows else 2), swap_send.at[number], swap_recv.at[number], twin)))
        loads.append(pltpu.make_async_copy(source, spot(target, index, by_rows, 0), load_sem.at[3 + number]))
        loads[-1].start()

    for copy in first_loads[:2]:
        copy.wait()
    experts = nodes * columns
    expert_iota = lax.broadcasted_iota(jnp.int32, (experts, count), 0)
    listed = jnp.full((experts, count), -1.0, f32)
    for choice in range(ids.shape[0]):
        listed = jnp.where(ids[pl.ds(choice, 1), :] == expert_iota, weights[pl.ds(choice, 1), :], listed)
    tables[0, 0] = jnp.full((experts, LANES), -1.0, f32)
    tables[0, 0, :, pl.ds(0, count)] = listed

    for index, peer, step in ((0, beside, 1), (1, across, later), (2, apart, later)):
        list_in[index + 1] = start(send(tables.at[0, 0], tables.at[step, 0], list_send.at[index], list_recv.at[step], peer))

    def send_notes(step):
        for side in (0, 1):
            note_in[step, side] = start(send(tables.at[step, 0], tables.at[step, 1 + side], note_send.at[step, side], note_recv.at[step, side], sides[side]))

    before = (lax.broadcasted_iota(jnp.int32, (LANES, LANES), 0) < lax.broadcasted_iota(jnp.int32, (LANES, LANES), 1)).astype(bf16)
    places = lax.broadcasted_iota(jnp.int32, (capacity, LANES), 0).astype(f32)
    mirror = (lax.broadcasted_iota(jnp.int32, (count, LANES), 0) == lax.broadcasted_iota(jnp.int32, (count, LANES), 1)).astype(bf16)
    mine = node * columns + column
    near_experts = tuple(side_node * columns + column for side_node in side_nodes)

    def prepare(step, slot, wanted):
        table = tables[step, slot]
        rank = jnp.dot((table >= 0).astype(bf16), before, preferred_element_type=f32)
        rank = jnp.where(table >= 0, rank, -1.0)
        rows_iota = lax.broadcasted_iota(jnp.int32, table.shape, 0)
        for expert, index in wanted:
            chosen = rows_iota == expert
            row = jnp.sum(jnp.where(chosen, rank, 0.0), axis=0, keepdims=True)
            pick = (places == row).astype(f32)
            if index is None or index[1]:
                value = jnp.sum(jnp.where(chosen, table, 0.0), axis=0, keepdims=True)
                share = jnp.sum(pick * value, axis=1, keepdims=True)
                shares[step, own(slot)] = jnp.broadcast_to(share, (capacity, LANES))
            if index is not None:
                picked = pick.astype(bf16)
                picks[step, index[0], pl.ds(index[2] * capacity, capacity)] = picked
                spreads[step, index[0], index[2]] = lax.dot_general(
                    mirror, picked, (((1,), (1,)), ((), ())), preferred_element_type=f32).astype(bf16)

    tile = 512

    def compress(step, index, source, targets):
        wanted = picks[step, index][:, :count]

        def body(number, carry):
            place = pl.ds(pl.multiple_of(number * tile, tile), tile)
            made = jnp.dot(wanted, source[:, place], preferred_element_type=f32).astype(bf16)
            for which, target in enumerate(targets):
                target[:, place] = made[which * capacity:(which + 1) * capacity]
            return carry

        lax.fori_loop(0, split // tile, body, 0)

    def issue(step):
        if step:
            if step == 1:
                line_in[1].wait_recv()

                @pl.when(inner)
                def _():
                    pass_across.start()
            else:
                pltpu_wait = line_in[step]
                pltpu_wait.wait_recv()

                @pl.when(inner)
                def _(step=step):
                    pass_beside[step - 2].start()
            send_halves(step, dense.at[step])
            pltpu.make_async_remote_copy(
                src_ref=tables.at[0, 0], dst_ref=tables.at[step, 0], send_sem=list_send.at[0], recv_sem=list_recv.at[step],
                device_id=beside, device_id_type=MESH,
            ).wait_recv()
        send_notes(step)
        prepare(step, 0, ((near_experts[1], (0, False, 0)), (mine, (0, True, 1)), (near_experts[0], (1, False, 0))))
        picks[step, 1, pl.ds(capacity, capacity)] = picks[step, 0, pl.ds(capacity, capacity)]
        if not step:
            first_loads[2].wait()
        for half, side in ((0, 1), (1, 0)):
            compress(step, half, dense.at[step, :, columns_of(half)], (outs.at[step, side], packed.at[step, own(0), columns_of(half)]))
            pack_in[step, side] = start(send(outs.at[step, side], packed.at[step, own(1 + side), columns_of(half)], pack_send.at[step, side], pack_recv.at[step, side], sides[side]))

    def relay(step):
        for side in (0, 1):
            other = 1 - side
            note_in[step, side].wait_recv()
            if not side:
                note_in[step, 2] = start(send(tables.at[step, 1], tables.at[step, 3], note_send.at[step, 2], note_recv.at[step, 2], sides[1]))
            prepare(step, 1 + side, ((near_experts[other], (2 + side, False, 0)), (mine, (2 + side, True, 1))))
            half_in[step, side].wait_recv()
            compress(step, 2 + side, halves.at[step, side], (passes.at[step, side], packed.at[step, own(1 + side), columns_of(side)]))
            pass_in[step, side] = start(send(passes.at[step, side], packed.at[step, own(3), columns_of(side)], pass_send.at[step, side], pass_recv.at[step, side], sides[other]))

    def compute(step):
        note_in[step, 2].wait_recv()
        prepare(step, 3, ((mine, None),))
        for side in (0, 1):
            pack_in[step, side].wait_recv()
            pass_in[step, side].wait_recv()
        if not step:
            for copy in swaps:
                copy.wait_recv()
            for copy in loads:
                copy.wait()
        wide = 2 * LANES

        def into(number, carry):
            place = pl.ds(pl.multiple_of(number * wide, wide), wide)
            acts[:, place] = jnp.dot(packed[step], first[:, place], preferred_element_type=f32)
            return carry

        lax.fori_loop(0, acts.shape[1] // wide, into, 0)
        for other in (0, 1):
            gate = acts[:, pl.ds(2 * other * hidden_half, hidden_half)]
            upper = acts[:, pl.ds((2 * other + 1) * hidden_half, hidden_half)]
            hidden[:, pl.ds(other * hidden_half, hidden_half)] = (gate / (1.0 + jnp.exp(-gate)) * upper).astype(bf16)
        share = jnp.broadcast_to(shares[step][:, :1], (slots * capacity, wide))

        def out_of(number, carry):
            place = pl.ds(pl.multiple_of(number * wide, wide), wide)
            made = jnp.dot(hidden[...], second[:, place], preferred_element_type=f32)
            results[step, :, place] = (made * share).astype(bf16)
            return carry

        lax.fori_loop(0, width // wide, out_of, 0)

    far_in, near_in, sum_in, end_in = {}, {}, {}, {}

    def hand_back(step):
        for side in (0, 1):
            far_in[step, side] = start(send(results.at[step, own(3), columns_of(side)], relays.at[step, side], far_send.at[step, side], far_recv.at[step, side], sides[side]))
        for side in (0, 1):
            near_in[step, side] = start(send(results.at[step, own(1 + side), columns_of(side)], compacts.at[step, side], near_send.at[step, side], near_recv.at[step, side], sides[side]))

    def expand(step, index, which):
        return spreads[step, index, which][:, :capacity]

    def combine(step):
        for side in (0, 1):
            other = 1 - side
            far_in[step, side].wait_recv()
            theirs = spreads[step, 2 + other, 0]
            ours = spreads[step, 2 + other, 1]

            def body(number, carry, side=side, other=other, theirs=theirs, ours=ours):
                place = pl.ds(pl.multiple_of(number * tile, tile), tile)
                shifted = pl.ds(pl.multiple_of(side * split + number * tile, tile), tile)
                made = jnp.dot(theirs, relays[step, side, :, place], preferred_element_type=f32)
                made += jnp.dot(ours, results[step, own(1 + other), shifted], preferred_element_type=f32)
                relayed[step, other, :, place] = made.astype(bf16)
                return carry

            lax.fori_loop(0, split // tile, body, 0)
            sum_in[step, other] = start(send(relayed.at[step, other], sums.at[step, other], sum_send.at[step, other], sum_recv.at[step, other], sides[other]))

    def collect(step):
        if not step:
            for index in (1, 2, 3):
                end_in[index].wait_recv()
        for side in (0, 1):
            other = 1 - side
            near_in[step, side].wait_recv()
            sum_in[step, other].wait_recv()
            theirs = spreads[step, other, 0]
            ours = spreads[step, 0, 1]

            def body(number, carry, side=side, other=other, theirs=theirs, ours=ours):
                place = pl.ds(pl.multiple_of(number * tile, tile), tile)
                shifted = pl.ds(pl.multiple_of(side * split + number * tile, tile), tile)
                made = jnp.dot(theirs, compacts[step, side, :, place], preferred_element_type=f32)
                made += jnp.dot(ours, results[step, own(0), shifted], preferred_element_type=f32)
                made += sums[step, other, :, place].astype(f32)
                if step:
                    totals[step - 1, :, shifted] = made.astype(bf16)
                else:
                    for index in range(columns - 1):
                        made += finals[index, :, shifted].astype(f32)
                    output[:, shifted] = made.astype(bf16)
                return carry

            lax.fori_loop(0, split // tile, body, 0)
        if step == 1:
            end_in[1] = start(send(totals.at[0], finals.at[0], end_send.at[0], end_recv.at[0], beside))
        elif step:
            end_in[step] = give_back[step - 2]

            @pl.when(inner)
            def _(step=step):
                give_inner[step - 2].start()

            @pl.when(jnp.logical_not(inner))
            def _(step=step):
                give_outer[step - 2].start()

    give_inner = (
        send(totals.at[1], finals.at[1], end_send.at[1], end_recv.at[1], across),
        send(totals.at[2], finals.at[1], end_send.at[2], end_recv.at[1], apart),
    )
    give_outer = (
        send(totals.at[1], finals.at[2], end_send.at[1], end_recv.at[2], apart),
        send(totals.at[2], finals.at[2], end_send.at[2], end_recv.at[2], across),
    )
    give_back = (give_inner[0], give_outer[1])

    table = {"issue": issue, "relay": relay, "compute": compute, "back": hand_back, "combine": combine, "collect": collect}
    for word in ORDER:
        table[word[:-1]](int(word[-1]))

    result = pltpu.make_async_copy(output, out_ref, load_sem.at[0])
    result.start()
    for copy in everything:
        copy.wait_send()
    for copy in give_inner:
        copy.wait_send()

    @pl.when(inner)
    def _():
        for copy in (to_across, pass_across, *pass_beside):
            copy.wait_send()

    result.wait()


ORDER = (
    "issue0", "relay0", "issue1", "compute0", "relay1", "issue2",
    "compute1", "relay2", "issue3", "compute2", "back2", "relay3",
    "combine2", "back1", "compute3", "back3", "collect2", "combine1",
    "combine3", "back0", "collect3", "collect1", "combine0", "collect0",
)


def by_rows(tokens, expert_ids, gate_weights, w_gate, w_up, w_down):
    nodes, columns = lax.axis_size("node"), lax.axis_size("local") // 2
    experts = nodes * columns
    count, width = tokens.shape
    choices = expert_ids.shape[1]
    capacity = capacity_of(count, choices, experts)
    hidden_half = w_gate.shape[1]
    split = width // 2
    dma = pltpu.SemaphoreType.DMA
    bf16, f32 = jnp.bfloat16, jnp.float32
    scratch = [
        pltpu.VMEM((choices, count), jnp.int32),
        pltpu.VMEM((choices, count), f32),
        pltpu.VMEM((columns, 4, experts, LANES), f32),
        pltpu.VMEM((columns, 4 * capacity, LANES), f32),
        pltpu.VMEM((columns, 4, 2 * capacity, LANES), bf16),
        pltpu.VMEM((columns, 4, 2, count, capacity), bf16),
        pltpu.VMEM((width, 4 * hidden_half), bf16),
        pltpu.VMEM((2 * hidden_half, width), bf16),
        pltpu.VMEM((columns, count, width), bf16),
        pltpu.VMEM((columns, 2, count, split), bf16),
        pltpu.VMEM((columns, 4 * capacity, width), bf16),
        pltpu.VMEM((columns, 2, capacity, split), bf16),
        pltpu.VMEM((columns, 2, capacity, split), bf16),
        pltpu.VMEM((4 * capacity, 4 * hidden_half), f32),
        pltpu.VMEM((4 * capacity, 2 * hidden_half), bf16),
        pltpu.VMEM((columns, 4 * capacity, width), bf16),
        pltpu.VMEM((columns, 2, capacity, split), bf16),
        pltpu.VMEM((columns, 2, capacity, split), bf16),
        pltpu.VMEM((columns, 2, count, split), bf16),
        pltpu.VMEM((columns, 2, count, split), bf16),
        pltpu.VMEM((columns - 1, count, width), bf16),
        pltpu.VMEM((columns - 1, count, width), bf16),
        pltpu.VMEM((count, width), bf16),
        dma((6,)), dma((3,)), dma((3,)), dma((5,)), dma((columns,)), dma((columns - 1,)), dma((columns,)),
        dma((columns, 2)), dma((columns, 2)), dma((columns, 3)), dma((columns, 3)),
        dma((columns, 2)), dma((columns, 2)), dma((columns, 2)), dma((columns, 2)),
        dma((columns, 2)), dma((columns, 2)), dma((columns, 2)), dma((columns, 2)),
        dma((columns, 2)), dma((columns, 2)), dma((columns - 1,)), dma((columns - 1,)),
    ]
    flops = 12 * experts * count * width * hidden_half
    return pl.pallas_call(
        functools.partial(layer_kernel, nodes, columns, capacity),
        name="moe_layer",
        out_shape=jax.ShapeDtypeStruct((count, width), bf16),
        in_specs=[pl.BlockSpec(memory_space=pl.ANY)] * 6,
        out_specs=pl.BlockSpec(memory_space=pl.ANY),
        scratch_shapes=scratch,
        cost_estimate=pl.CostEstimate(flops=flops, bytes_accessed=w_gate.size * 12, transcendentals=0),
        compiler_params=pltpu.CompilerParams(collective_id=0, has_side_effects=True, vmem_limit_bytes=60 << 20),
    )(tokens, expert_ids.T, gate_weights.T, w_gate, w_up, w_down)


def capacity_of(rows, choices, experts):
    return rows * choices * 5 // (4 * experts)


def per_device(tokens, expert_ids, *rest):
    nodes, columns = lax.axis_size("node"), lax.axis_size("local") // 2
    count = tokens.shape[0]
    capacity = capacity_of(count, expert_ids.shape[1], nodes * columns)
    if nodes == 4 and columns == 4 and count <= LANES and capacity % 8 == 0:
        return by_rows(tokens, expert_ids, *rest)
    return by_slots(tokens, expert_ids, *rest)


def solution(mesh):
    placed = (
        P(("parts", "node", "local"), None),
        P(("parts", "node", "local"), None),
        P(("parts", "node", "local"), None),
        P(None, ("parts", "node", "local")),
        P(None, ("parts", "node", "local")),
        P(("parts", "node", "local"), None),
    )
    return jax.shard_map(
        per_device,
        mesh=mesh,
        in_specs=placed,
        out_specs=P(("parts", "node", "local"), None),
        check_vma=False,
    )
```

```python
import functools

import jax
import jax.numpy as jnp
from jax import lax
from jax.experimental import pallas as pl
from jax.experimental.pallas import tpu as pltpu
from jax.sharding import PartitionSpec as P

MESH = pl.DeviceIdType.MESH


def partner_2(value, axis, bit):
    mask = 2**bit
    pairs = [(source, source ^ mask) for source in range(lax.axis_size(axis))]
    return lax.ppermute(value, axis, pairs)


def by_slots(tokens, expert_ids, gate_weights, w_gate, w_up, w_down):
    node_count = lax.axis_size("node")
    local_count = lax.axis_size("local")
    devices = node_count * local_count
    experts = devices // 2
    tok_rows, top_count = expert_ids.shape
    width = tokens.shape[1]
    capacity = tok_rows * top_count * 5 // (4 * experts)
    flat_ids = expert_ids.reshape(-1)
    one_hot = (flat_ids[:, None] == jnp.arange(experts, dtype=jnp.int32)[None, :]).astype(jnp.int32)
    earlier = jnp.cumsum(one_hot, axis=0) - one_hot
    slot_rank = jnp.sum(earlier * one_hot, axis=1)
    slot_index = (flat_ids * capacity + slot_rank).reshape(tok_rows, top_count)
    slot_table = jnp.any(
        slot_index[None, :, :] == jnp.arange(experts * capacity, dtype=jnp.int32)[:, None, None],
        axis=2,
    ).astype(jnp.bfloat16)
    outgoing = jnp.dot(slot_table, tokens, preferred_element_type=jnp.float32).astype(jnp.bfloat16)
    outgoing = outgoing.reshape(devices, capacity // 2, width)
    partner = partner_2((w_gate, w_up, w_down), "local", 0)
    full_gate = jnp.concatenate([w_gate, partner[0]], axis=1)
    full_up = jnp.concatenate([w_up, partner[1]], axis=1)
    full_down = jnp.concatenate([w_down, partner[2]], axis=0)
    block = lax.all_to_all(outgoing, ("node", "local"), split_axis=0, concat_axis=0, tiled=True)
    rows = block.reshape(-1, width)
    gate = jnp.dot(rows, full_gate, preferred_element_type=jnp.float32)
    upper = jnp.dot(rows, full_up, preferred_element_type=jnp.float32)
    hidden = (jax.nn.silu(gate) * upper).astype(jnp.bfloat16)
    result = jnp.dot(hidden, full_down, preferred_element_type=jnp.float32).astype(jnp.bfloat16)
    processed = result.reshape(block.shape)
    returned = lax.all_to_all(processed, ("node", "local"), split_axis=0, concat_axis=0, tiled=True)
    results = returned.reshape(experts * capacity, width)
    chosen = results[slot_index]
    mixed = jnp.sum(gate_weights[:, :, None] * chosen.astype(jnp.float32), axis=1)
    return mixed.astype(jnp.bfloat16)


LANES = 128


def layer_kernel(
    nodes, columns, capacity,
    rows_ref, ids_ref, weights_ref, gate_ref, up_ref, down_ref, out_ref,
    ids, weights, tables, shares, picks, spreads,
    first, second, dense, halves, packed, outs, passes, acts, hidden,
    results, relays, compacts, relayed, sums, totals, finals, output,
    load_sem, swap_send, swap_recv, line_send, line_recv, list_send, list_recv,
    half_send, half_recv, note_send, note_recv, pack_send, pack_recv, pass_send, pass_recv,
    far_send, far_recv, near_send, near_recv, sum_send, sum_recv, end_send, end_recv,
):
    part, node, local = lax.axis_index("parts"), lax.axis_index("node"), lax.axis_index("local")
    column, core = local // 2, lax.rem(local, 2)
    high, low = node // 2, lax.rem(node, 2)
    count, width = rows_ref.shape
    hidden_half = gate_ref.shape[1]
    split = width // 2
    slots = 4
    bf16, f32 = jnp.bfloat16, jnp.float32
    inner = (column == 1) | (column == 2)

    def at(node_index, local_index):
        return (part, node_index, local_index)

    sides = (at(high * 2 + 1 - low, local), at((1 - high) * 2 + low, local))
    side_nodes = (high * 2 + 1 - low, (1 - high) * 2 + low)
    twin = at(node, column * 2 + 1 - core)
    low_flip = column + 1 - 2 * lax.rem(column, 2)
    beside = at(node, low_flip * 2 + core)
    across = at(node, (columns - 1 - column) * 2 + core)
    apart = at(node, (columns - 1 - low_flip) * 2 + core)
    later = jnp.where(inner, 2, 3)

    barrier = pltpu.get_barrier_semaphore()
    greeted = (*sides, twin, beside, across, apart)
    for peer in greeted:
        pl.semaphore_signal(barrier, inc=1, device_id=peer, device_id_type=MESH)
    pl.semaphore_wait(barrier, len(greeted))

    everything, inner_only = [], []

    def send(source, target, send_sem, recv_sem, peer):
        return pltpu.make_async_remote_copy(
            src_ref=source, dst_ref=target, send_sem=send_sem, recv_sem=recv_sem,
            device_id=peer, device_id_type=MESH,
        )

    def start(copy):
        copy.start()
        everything.append(copy)
        return copy

    def columns_of(side):
        return pl.ds(side * split, split)

    def own(slot):
        return pl.ds(slot * capacity, capacity)

    half_in = {}
    line_in = {}
    list_in = {}
    note_in = {}
    pack_in = {}
    pass_in = {}

    def send_halves(step, source):
        for side in (0, 1):
            half_in[step, side] = start(send(source.at[:, columns_of(side)], halves.at[step, side], half_send.at[step, side], half_recv.at[step, side], sides[side]))

    send_halves(0, rows_ref)
    line_in[1] = start(send(rows_ref, dense.at[1], line_send.at[0], line_recv.at[1], beside))
    to_across = send(rows_ref, dense.at[2], line_send.at[1], line_recv.at[2], across)
    pass_across = send(dense.at[1], dense.at[3], line_send.at[2], line_recv.at[3], across)
    pass_beside = (
        send(dense.at[2], dense.at[2], line_send.at[3], line_recv.at[2], beside),
        send(dense.at[3], dense.at[3], line_send.at[4], line_recv.at[3], beside),
    )
    line_in[2], line_in[3] = to_across, pass_across

    @pl.when(inner)
    def _():
        to_across.start()

    first_loads = [
        pltpu.make_async_copy(ids_ref, ids, load_sem.at[0]),
        pltpu.make_async_copy(weights_ref, weights, load_sem.at[1]),
        pltpu.make_async_copy(rows_ref, dense.at[0], load_sem.at[2]),
    ]
    for copy in first_loads:
        copy.start()

    def spot(target, index, by_rows, other):
        place = pl.ds((index + other) * hidden_half, hidden_half)
        return target.at[place] if by_rows else target.at[:, place]

    near = ((gate_ref, first, 0, False), (up_ref, first, 1, False), (down_ref, second, 0, True))
    swaps, loads = [], []
    for number, (source, target, index, by_rows) in enumerate(near):
        swaps.append(start(send(source, spot(target, index, by_rows, 1 if by_rows else 2), swap_send.at[number], swap_recv.at[number], twin)))
        loads.append(pltpu.make_async_copy(source, spot(target, index, by_rows, 0), load_sem.at[3 + number]))
        loads[-1].start()

    for copy in first_loads[:2]:
        copy.wait()
    experts = nodes * columns
    expert_iota = lax.broadcasted_iota(jnp.int32, (experts, count), 0)
    listed = jnp.full((experts, count), -1.0, f32)
    for choice in range(ids.shape[0]):
        listed = jnp.where(ids[pl.ds(choice, 1), :] == expert_iota, weights[pl.ds(choice, 1), :], listed)
    tables[0, 0] = jnp.full((experts, LANES), -1.0, f32)
    tables[0, 0, :, pl.ds(0, count)] = listed

    for index, peer, step in ((0, beside, 1), (1, across, later), (2, apart, later)):
        list_in[index + 1] = start(send(tables.at[0, 0], tables.at[step, 0], list_send.at[index], list_recv.at[step], peer))

    def send_notes(step):
        for side in (0, 1):
            note_in[step, side] = start(send(tables.at[step, 0], tables.at[step, 1 + side], note_send.at[step, side], note_recv.at[step, side], sides[side]))

    before = (lax.broadcasted_iota(jnp.int32, (LANES, LANES), 0) < lax.broadcasted_iota(jnp.int32, (LANES, LANES), 1)).astype(bf16)
    places = lax.broadcasted_iota(jnp.int32, (capacity, LANES), 0).astype(f32)
    mirror = (lax.broadcasted_iota(jnp.int32, (count, LANES), 0) == lax.broadcasted_iota(jnp.int32, (count, LANES), 1)).astype(bf16)
    mine = node * columns + column
    near_experts = tuple(side_node * columns + column for side_node in side_nodes)

    def prepare(step, slot, wanted):
        table = tables[step, slot]
        rank = jnp.dot((table >= 0).astype(bf16), before, preferred_element_type=f32)
        rank = jnp.where(table >= 0, rank, -1.0)
        rows_iota = lax.broadcasted_iota(jnp.int32, table.shape, 0)
        for expert, index in wanted:
            chosen = rows_iota == expert
            row = jnp.sum(jnp.where(chosen, rank, 0.0), axis=0, keepdims=True)
            pick = (places == row).astype(f32)
            if index is None or index[1]:
                value = jnp.sum(jnp.where(chosen, table, 0.0), axis=0, keepdims=True)
                share = jnp.sum(pick * value, axis=1, keepdims=True)
                shares[step, own(slot)] = jnp.broadcast_to(share, (capacity, LANES))
            if index is not None:
                picked = pick.astype(bf16)
                picks[step, index[0], pl.ds(index[2] * capacity, capacity)] = picked
                spreads[step, index[0], index[2]] = lax.dot_general(
                    mirror, picked, (((1,), (1,)), ((), ())), preferred_element_type=f32).astype(bf16)

    tile = 512

    def compress(step, index, source, targets):
        wanted = picks[step, index][:, :count]

        def body(number, carry):
            place = pl.ds(pl.multiple_of(number * tile, tile), tile)
            made = jnp.dot(wanted, source[:, place], preferred_element_type=f32).astype(bf16)
            for which, target in enumerate(targets):
                target[:, place] = made[which * capacity:(which + 1) * capacity]
            return carry

        lax.fori_loop(0, split // tile, body, 0)

    passed = {}

    def pass_on(step):
        passed[step] = True

        @pl.when(inner)
        def _():
            line_in[step].wait_recv()
            (pass_across, *pass_beside)[step - 1].start()

    def issue(step):
        if step:
            @pl.when(jnp.logical_not(inner) | (step not in passed))
            def _():
                line_in[step].wait_recv()

            send_halves(step, dense.at[step])
            pltpu.make_async_remote_copy(
                src_ref=tables.at[0, 0], dst_ref=tables.at[step, 0], send_sem=list_send.at[0], recv_sem=list_recv.at[step],
                device_id=beside, device_id_type=MESH,
            ).wait_recv()
        send_notes(step)
        prepare(step, 0, ((near_experts[1], (0, False, 0)), (mine, (0, True, 1)), (near_experts[0], (1, False, 0))))
        picks[step, 1, pl.ds(capacity, capacity)] = picks[step, 0, pl.ds(capacity, capacity)]
        if not step:
            first_loads[2].wait()
        for half, side in ((0, 1), (1, 0)):
            compress(step, half, dense.at[step, :, columns_of(half)], (outs.at[step, side], packed.at[step, own(0), columns_of(half)]))
            pack_in[step, side] = start(send(outs.at[step, side], packed.at[step, own(1 + side), columns_of(half)], pack_send.at[step, side], pack_recv.at[step, side], sides[side]))

    def relay(step):
        for side in (0, 1):
            other = 1 - side
            note_in[step, side].wait_recv()
            if not side:
                note_in[step, 2] = start(send(tables.at[step, 1], tables.at[step, 3], note_send.at[step, 2], note_recv.at[step, 2], sides[1]))
            prepare(step, 1 + side, ((near_experts[other], (2 + side, False, 0)), (mine, (2 + side, True, 1))))
            half_in[step, side].wait_recv()
            compress(step, 2 + side, halves.at[step, side], (passes.at[step, side], packed.at[step, own(1 + side), columns_of(side)]))
            pass_in[step, side] = start(send(passes.at[step, side], packed.at[step, own(3), columns_of(side)], pass_send.at[step, side], pass_recv.at[step, side], sides[other]))

    def compute(step):
        note_in[step, 2].wait_recv()
        prepare(step, 3, ((mine, None),))
        for side in (0, 1):
            pack_in[step, side].wait_recv()
            pass_in[step, side].wait_recv()
        if not step:
            for copy in swaps:
                copy.wait_recv()
            for copy in loads:
                copy.wait()
        wide = 2 * LANES

        def into(number, carry):
            place = pl.ds(pl.multiple_of(number * wide, wide), wide)
            acts[:, place] = jnp.dot(packed[step], first[:, place], preferred_element_type=f32)
            return carry

        lax.fori_loop(0, acts.shape[1] // wide, into, 0)
        for other in (0, 1):
            gate = acts[:, pl.ds(2 * other * hidden_half, hidden_half)]
            upper = acts[:, pl.ds((2 * other + 1) * hidden_half, hidden_half)]
            hidden[:, pl.ds(other * hidden_half, hidden_half)] = (gate / (1.0 + jnp.exp(-gate)) * upper).astype(bf16)
        share = jnp.broadcast_to(shares[step][:, :1], (slots * capacity, wide))

        def out_of(number, carry):
            place = pl.ds(pl.multiple_of(number * wide, wide), wide)
            made = jnp.dot(hidden[...], second[:, place], preferred_element_type=f32)
            results[step, :, place] = (made * share).astype(bf16)
            return carry

        lax.fori_loop(0, width // wide, out_of, 0)

    far_in, near_in, sum_in, end_in = {}, {}, {}, {}

    def hand_far(step):
        for side in (0, 1):
            far_in[step, side] = start(send(results.at[step, own(3), columns_of(side)], relays.at[step, side], far_send.at[step, side], far_recv.at[step, side], sides[side]))

    def hand_near(step):
        for side in (0, 1):
            near_in[step, side] = start(send(results.at[step, own(1 + side), columns_of(side)], compacts.at[step, side], near_send.at[step, side], near_recv.at[step, side], sides[side]))

    def combine(step):
        for side in (0, 1):
            other = 1 - side
            far_in[step, side].wait_recv()
            theirs = spreads[step, 2 + other, 0]
            ours = spreads[step, 2 + other, 1]

            def body(number, carry, side=side, other=other, theirs=theirs, ours=ours):
                place = pl.ds(pl.multiple_of(number * tile, tile), tile)
                shifted = pl.ds(pl.multiple_of(side * split + number * tile, tile), tile)
                made = jnp.dot(theirs, relays[step, side, :, place], preferred_element_type=f32)
                made += jnp.dot(ours, results[step, own(1 + other), shifted], preferred_element_type=f32)
                relayed[step, other, :, place] = made.astype(bf16)
                return carry

            lax.fori_loop(0, split // tile, body, 0)
            sum_in[step, other] = start(send(relayed.at[step, other], sums.at[step, other], sum_send.at[step, other], sum_recv.at[step, other], sides[other]))

    FAR_SUM, BACK_SUM, LAST_SUM, BESIDE_SUM, ACROSS_SUM = range(5)
    routes = {
        True: {1: (beside, BESIDE_SUM), 2: (across, ACROSS_SUM), 3: (across, BACK_SUM)},
        False: {1: (beside, BESIDE_SUM), 2: (beside, LAST_SUM), 3: (beside, FAR_SUM)},
    }
    added = {
        True: {3: (FAR_SUM,), 2: (LAST_SUM,), 1: (BACK_SUM,), 0: (BESIDE_SUM, ACROSS_SUM)},
        False: {3: (), 2: (), 1: (), 0: (BESIDE_SUM,)},
    }

    def give(step, side, inside):
        peer, inbox = routes[inside][step]
        return send(totals.at[step - 1, :, columns_of(side)], finals.at[inbox, :, columns_of(side)], end_send.at[step - 1, side], end_recv.at[inbox, side], peer)

    def collect(step):
        for side in (0, 1):
            other = 1 - side
            near_in[step, side].wait_recv()
            sum_in[step, other].wait_recv()
            theirs = spreads[step, other, 0]
            ours = spreads[step, 0, 1]

            def total(inside, side=side, other=other, theirs=theirs, ours=ours):
                for inbox in added[inside][step]:
                    send(totals.at[0, :, columns_of(side)], finals.at[inbox, :, columns_of(side)], end_send.at[0, side], end_recv.at[inbox, side], beside).wait_recv()

                def body(number, carry):
                    place = pl.ds(pl.multiple_of(number * tile, tile), tile)
                    shifted = pl.ds(pl.multiple_of(side * split + number * tile, tile), tile)
                    made = jnp.dot(theirs, compacts[step, side, :, place], preferred_element_type=f32)
                    made += jnp.dot(ours, results[step, own(0), shifted], preferred_element_type=f32)
                    made += sums[step, other, :, place].astype(f32)
                    for inbox in added[inside][step]:
                        made += finals[inbox, :, shifted].astype(f32)
                    target = totals.at[step - 1] if step else output
                    target[:, shifted] = made.astype(bf16)
                    return carry

                lax.fori_loop(0, split // tile, body, 0)
                if step:
                    give(step, side, inside).start()

            @pl.when(inner)
            def _(total=total):
                total(True)

            @pl.when(jnp.logical_not(inner))
            def _(total=total):
                total(False)

    table = {
        "pass": pass_on, "issue": issue, "relay": relay, "compute": compute, "far": hand_far, "near": hand_near,
        "combine": combine, "collect": collect,
    }
    for word in ORDER:
        table[word[:-1]](int(word[-1]))

    result = pltpu.make_async_copy(output, out_ref, load_sem.at[0])
    result.start()
    for copy in everything:
        copy.wait_send()
    for step in range(1, columns):
        for side in (0, 1):
            give(step, side, True).wait_send()

    @pl.when(inner)
    def _():
        for copy in (to_across, pass_across, *pass_beside):
            copy.wait_send()

    result.wait()


ORDER = (
    "issue0", "relay0", "pass1", "pass2", "issue1", "compute0",
    "issue2", "pass3", "relay2", "issue3", "compute2", "far2",
    "relay3", "relay1", "combine2", "near2", "compute3", "far3",
    "near3", "compute1", "far1", "combine3", "far0", "near1",
    "collect2", "combine1", "collect3", "combine0", "near0", "collect1",
    "collect0",
)


def by_rows(tokens, expert_ids, gate_weights, w_gate, w_up, w_down):
    nodes, columns = lax.axis_size("node"), lax.axis_size("local") // 2
    experts = nodes * columns
    count, width = tokens.shape
    choices = expert_ids.shape[1]
    capacity = capacity_of(count, choices, experts)
    hidden_half = w_gate.shape[1]
    split = width // 2
    dma = pltpu.SemaphoreType.DMA
    bf16, f32 = jnp.bfloat16, jnp.float32
    scratch = [
        pltpu.VMEM((choices, count), jnp.int32),
        pltpu.VMEM((choices, count), f32),
        pltpu.VMEM((columns, 4, experts, LANES), f32),
        pltpu.VMEM((columns, 4 * capacity, LANES), f32),
        pltpu.VMEM((columns, 4, 2 * capacity, LANES), bf16),
        pltpu.VMEM((columns, 4, 2, count, capacity), bf16),
        pltpu.VMEM((width, 4 * hidden_half), bf16),
        pltpu.VMEM((2 * hidden_half, width), bf16),
        pltpu.VMEM((columns, count, width), bf16),
        pltpu.VMEM((columns, 2, count, split), bf16),
        pltpu.VMEM((columns, 4 * capacity, width), bf16),
        pltpu.VMEM((columns, 2, capacity, split), bf16),
        pltpu.VMEM((columns, 2, capacity, split), bf16),
        pltpu.VMEM((4 * capacity, 4 * hidden_half), f32),
        pltpu.VMEM((4 * capacity, 2 * hidden_half), bf16),
        pltpu.VMEM((columns, 4 * capacity, width), bf16),
        pltpu.VMEM((columns, 2, capacity, split), bf16),
        pltpu.VMEM((columns, 2, capacity, split), bf16),
        pltpu.VMEM((columns, 2, count, split), bf16),
        pltpu.VMEM((columns, 2, count, split), bf16),
        pltpu.VMEM((columns - 1, count, width), bf16),
        pltpu.VMEM((5, count, width), bf16),
        pltpu.VMEM((count, width), bf16),
        dma((6,)), dma((3,)), dma((3,)), dma((5,)), dma((columns,)), dma((columns - 1,)), dma((columns,)),
        dma((columns, 2)), dma((columns, 2)), dma((columns, 3)), dma((columns, 3)),
        dma((columns, 2)), dma((columns, 2)), dma((columns, 2)), dma((columns, 2)),
        dma((columns, 2)), dma((columns, 2)), dma((columns, 2)), dma((columns, 2)),
        dma((columns, 2)), dma((columns, 2)), dma((columns - 1, 2)), dma((5, 2)),
    ]
    flops = 12 * experts * count * width * hidden_half
    return pl.pallas_call(
        functools.partial(layer_kernel, nodes, columns, capacity),
        name="moe_layer",
        out_shape=jax.ShapeDtypeStruct((count, width), bf16),
        in_specs=[pl.BlockSpec(memory_space=pl.ANY)] * 6,
        out_specs=pl.BlockSpec(memory_space=pl.ANY),
        scratch_shapes=scratch,
        cost_estimate=pl.CostEstimate(flops=flops, bytes_accessed=w_gate.size * 12, transcendentals=0),
        compiler_params=pltpu.CompilerParams(collective_id=0, has_side_effects=True, vmem_limit_bytes=60 << 20),
    )(tokens, expert_ids.T, gate_weights.T, w_gate, w_up, w_down)


def capacity_of(rows, choices, experts):
    return rows * choices * 5 // (4 * experts)


def per_device(tokens, expert_ids, *rest):
    nodes, columns = lax.axis_size("node"), lax.axis_size("local") // 2
    count = tokens.shape[0]
    capacity = capacity_of(count, expert_ids.shape[1], nodes * columns)
    if nodes == 4 and columns == 4 and count <= LANES and capacity % 8 == 0:
        return by_rows(tokens, expert_ids, *rest)
    return by_slots(tokens, expert_ids, *rest)


def solution(mesh):
    placed = (
        P(("parts", "node", "local"), None),
        P(("parts", "node", "local"), None),
        P(("parts", "node", "local"), None),
        P(None, ("parts", "node", "local")),
        P(None, ("parts", "node", "local")),
        P(("parts", "node", "local"), None),
    )
    return jax.shard_map(
        per_device,
        mesh=mesh,
        in_specs=placed,
        out_specs=P(("parts", "node", "local"), None),
        check_vma=False,
    )
```

```python
import functools

import jax
import jax.numpy as jnp
from jax import lax
from jax.experimental import pallas as pl
from jax.experimental.pallas import tpu as pltpu
from jax.sharding import PartitionSpec as P

MESH = pl.DeviceIdType.MESH


def partner_2(value, axis, bit):
    mask = 2**bit
    pairs = [(source, source ^ mask) for source in range(lax.axis_size(axis))]
    return lax.ppermute(value, axis, pairs)


def by_slots(tokens, expert_ids, gate_weights, w_gate, w_up, w_down):
    node_count = lax.axis_size("node")
    local_count = lax.axis_size("local")
    devices = node_count * local_count
    experts = devices // 2
    tok_rows, top_count = expert_ids.shape
    width = tokens.shape[1]
    capacity = tok_rows * top_count * 5 // (4 * experts)
    flat_ids = expert_ids.reshape(-1)
    one_hot = (flat_ids[:, None] == jnp.arange(experts, dtype=jnp.int32)[None, :]).astype(jnp.int32)
    earlier = jnp.cumsum(one_hot, axis=0) - one_hot
    slot_rank = jnp.sum(earlier * one_hot, axis=1)
    slot_index = (flat_ids * capacity + slot_rank).reshape(tok_rows, top_count)
    slot_table = jnp.any(
        slot_index[None, :, :] == jnp.arange(experts * capacity, dtype=jnp.int32)[:, None, None],
        axis=2,
    ).astype(jnp.bfloat16)
    outgoing = jnp.dot(slot_table, tokens, preferred_element_type=jnp.float32).astype(jnp.bfloat16)
    outgoing = outgoing.reshape(devices, capacity // 2, width)
    partner = partner_2((w_gate, w_up, w_down), "local", 0)
    full_gate = jnp.concatenate([w_gate, partner[0]], axis=1)
    full_up = jnp.concatenate([w_up, partner[1]], axis=1)
    full_down = jnp.concatenate([w_down, partner[2]], axis=0)
    block = lax.all_to_all(outgoing, ("node", "local"), split_axis=0, concat_axis=0, tiled=True)
    rows = block.reshape(-1, width)
    gate = jnp.dot(rows, full_gate, preferred_element_type=jnp.float32)
    upper = jnp.dot(rows, full_up, preferred_element_type=jnp.float32)
    hidden = (jax.nn.silu(gate) * upper).astype(jnp.bfloat16)
    result = jnp.dot(hidden, full_down, preferred_element_type=jnp.float32).astype(jnp.bfloat16)
    processed = result.reshape(block.shape)
    returned = lax.all_to_all(processed, ("node", "local"), split_axis=0, concat_axis=0, tiled=True)
    results = returned.reshape(experts * capacity, width)
    chosen = results[slot_index]
    mixed = jnp.sum(gate_weights[:, :, None] * chosen.astype(jnp.float32), axis=1)
    return mixed.astype(jnp.bfloat16)


LANES = 128


def layer_kernel(
    nodes, columns, capacity, extra,
    rows_ref, ids_ref, weights_ref, gate_ref, up_ref, down_ref, out_ref,
    ids, weights, tables, shares, picks, spreads,
    first, second, dense, halves, packed, outs, passes, acts, hidden,
    results, relays, compacts, relayed, sums, totals, finals,
    edges, edge_picks, edge_spreads, dealt, gathered, merged, passed_edges, blended, edge_sums,
    load_sem, swap_send, swap_recv, line_send, line_recv, list_send, list_recv,
    half_send, half_recv, note_send, note_recv, pack_send, pack_recv, pass_send, pass_recv,
    far_send, far_recv, near_send, near_recv, sum_send, sum_recv, end_send, end_recv,
    edge_send, edge_recv, deal_send, deal_recv, ship_send, ship_recv, merge_send, merge_recv,
):
    part, node, local = lax.axis_index("parts"), lax.axis_index("node"), lax.axis_index("local")
    column, core = local // 2, lax.rem(local, 2)
    high, low = node // 2, lax.rem(node, 2)
    count, width = rows_ref.shape
    hidden_half = gate_ref.shape[1]
    body_width = width - extra
    split = body_width // 2
    slots = 4
    bf16, f32 = jnp.bfloat16, jnp.float32
    inner = (column == 1) | (column == 2)

    def at(node_index, local_index):
        return (part, node_index, local_index)

    sides = (at(high * 2 + 1 - low, local), at((1 - high) * 2 + low, local))
    side_nodes = (high * 2 + 1 - low, (1 - high) * 2 + low)
    twin = at(node, column * 2 + 1 - core)
    low_flip = column + 1 - 2 * lax.rem(column, 2)
    beside = at(node, low_flip * 2 + core)
    across = at(node, (columns - 1 - column) * 2 + core)
    apart = at(node, (columns - 1 - low_flip) * 2 + core)
    later = jnp.where(inner, 2, 3)

    barrier = pltpu.get_barrier_semaphore()
    greeted = (*sides, twin, beside, across, apart)
    for peer in greeted:
        pl.semaphore_signal(barrier, inc=1, device_id=peer, device_id_type=MESH)
    pl.semaphore_wait(barrier, len(greeted))

    everything, inner_only = [], []

    def send(source, target, send_sem, recv_sem, peer):
        return pltpu.make_async_remote_copy(
            src_ref=source, dst_ref=target, send_sem=send_sem, recv_sem=recv_sem,
            device_id=peer, device_id_type=MESH,
        )

    def start(copy):
        copy.start()
        everything.append(copy)
        return copy

    def columns_of(side):
        return pl.ds(side * split, split)

    def own(slot):
        return pl.ds(slot * capacity, capacity)

    body = pl.ds(0, body_width)
    edge = pl.ds(body_width, extra)
    edge_half = (pl.ds(0, extra // 2), pl.ds(extra // 2, extra // 2))

    half_in = {}
    line_in = {}
    list_in = {}
    note_in = {}
    pack_in = {}
    pass_in = {}

    def send_halves(step, source):
        for side in (0, 1):
            half_in[step, side] = start(send(source.at[:, columns_of(side)], halves.at[step, side], half_send.at[step, side], half_recv.at[step, side], sides[side]))

    edge_in = {}
    for side in (0, 1):
        edge_in[side] = start(send(rows_ref.at[:, edge], edges.at[1 + side], edge_send.at[side], edge_recv.at[side], sides[side]))
    send_halves(0, rows_ref)
    line_in[1] = start(send(rows_ref.at[:, body], dense.at[1], line_send.at[0], line_recv.at[1], beside))
    to_across = send(rows_ref.at[:, body], dense.at[2], line_send.at[1], line_recv.at[2], across)
    pass_across = send(dense.at[1], dense.at[3], line_send.at[2], line_recv.at[3], across)
    pass_beside = (
        send(dense.at[2], dense.at[2], line_send.at[3], line_recv.at[2], beside),
        send(dense.at[3], dense.at[3], line_send.at[4], line_recv.at[3], beside),
    )
    line_in[2], line_in[3] = to_across, pass_across

    @pl.when(inner)
    def _():
        to_across.start()

    first_loads = [
        pltpu.make_async_copy(ids_ref, ids, load_sem.at[0]),
        pltpu.make_async_copy(weights_ref, weights, load_sem.at[1]),
        pltpu.make_async_copy(rows_ref.at[:, body], dense.at[0], load_sem.at[2]),
        pltpu.make_async_copy(rows_ref.at[:, edge], edges.at[0], load_sem.at[6]),
    ]
    for copy in first_loads:
        copy.start()

    def spot(target, index, by_rows, other):
        place = pl.ds((index + other) * hidden_half, hidden_half)
        return target.at[place] if by_rows else target.at[:, place]

    near = ((gate_ref, first, 0, False), (up_ref, first, 1, False), (down_ref, second, 0, True))
    swaps, loads = [], []
    for number, (source, target, index, by_rows) in enumerate(near):
        swaps.append(start(send(source, spot(target, index, by_rows, 1 if by_rows else 2), swap_send.at[number], swap_recv.at[number], twin)))
        loads.append(pltpu.make_async_copy(source, spot(target, index, by_rows, 0), load_sem.at[3 + number]))
        loads[-1].start()

    for copy in first_loads[:2]:
        copy.wait()
    experts = nodes * columns
    expert_iota = lax.broadcasted_iota(jnp.int32, (experts, count), 0)
    listed = jnp.full((experts, count), -1.0, f32)
    for choice in range(ids.shape[0]):
        listed = jnp.where(ids[pl.ds(choice, 1), :] == expert_iota, weights[pl.ds(choice, 1), :], listed)
    tables[0, 0] = jnp.full((experts, LANES), -1.0, f32)
    tables[0, 0, :, pl.ds(0, count)] = listed

    for index, peer, step in ((0, beside, 1), (1, across, later), (2, apart, later)):
        list_in[index + 1] = start(send(tables.at[0, 0], tables.at[step, 0], list_send.at[index], list_recv.at[step], peer))

    def send_notes(step):
        for side in (0, 1):
            note_in[step, side] = start(send(tables.at[step, 0], tables.at[step, 1 + side], note_send.at[step, side], note_recv.at[step, side], sides[side]))

    before = (lax.broadcasted_iota(jnp.int32, (LANES, LANES), 0) < lax.broadcasted_iota(jnp.int32, (LANES, LANES), 1)).astype(bf16)
    places = lax.broadcasted_iota(jnp.int32, (capacity, LANES), 0).astype(f32)
    mirror = (lax.broadcasted_iota(jnp.int32, (count, LANES), 0) == lax.broadcasted_iota(jnp.int32, (count, LANES), 1)).astype(bf16)
    mine = node * columns + column
    near_experts = tuple(side_node * columns + column for side_node in side_nodes)
    line_experts = (mine, node * columns + low_flip, node * columns + (columns - 1 - column), node * columns + (columns - 1 - low_flip))

    def prepare(step, slot, wanted):
        table = tables[step, slot]
        rank = jnp.dot((table >= 0).astype(bf16), before, preferred_element_type=f32)
        rank = jnp.where(table >= 0, rank, -1.0)
        rows_iota = lax.broadcasted_iota(jnp.int32, table.shape, 0)
        for expert, index in wanted:
            chosen = rows_iota == expert
            row = jnp.sum(jnp.where(chosen, rank, 0.0), axis=0, keepdims=True)
            pick = (places == row).astype(f32)
            if index is None or index[1]:
                value = jnp.sum(jnp.where(chosen, table, 0.0), axis=0, keepdims=True)
                share = jnp.sum(pick * value, axis=1, keepdims=True)
                shares[step, own(slot)] = jnp.broadcast_to(share, (capacity, LANES))
            if index is not None:
                picked = pick.astype(bf16)
                picks[step, index[0], pl.ds(index[2] * capacity, capacity)] = picked
                spreads[step, index[0], index[2]] = lax.dot_general(
                    mirror, picked, (((1,), (1,)), ((), ())), preferred_element_type=f32).astype(bf16)

    tile = split

    def compress(step, index, source, targets):
        wanted = picks[step, index][:, :count]

        def body(number, carry):
            place = pl.ds(pl.multiple_of(number * tile, tile), tile)
            made = jnp.dot(wanted, source[:, place], preferred_element_type=f32).astype(bf16)
            for which, target in enumerate(targets):
                target[:, place] = made[which * capacity:(which + 1) * capacity]
            return carry

        lax.fori_loop(0, split // tile, body, 0)

    passed = {}

    def pass_on(step):
        passed[step] = True

        @pl.when(inner)
        def _():
            line_in[step].wait_recv()
            (pass_across, *pass_beside)[step - 1].start()

    def issue(step):
        if step:
            @pl.when(jnp.logical_not(inner) | (step not in passed))
            def _():
                line_in[step].wait_recv()

            send_halves(step, dense.at[step])
            pltpu.make_async_remote_copy(
                src_ref=tables.at[0, 0], dst_ref=tables.at[step, 0], send_sem=list_send.at[0], recv_sem=list_recv.at[step],
                device_id=beside, device_id_type=MESH,
            ).wait_recv()
        send_notes(step)
        prepare(step, 0, ((near_experts[1], (0, False, 0)), (mine, (0, True, 1)), (near_experts[0], (1, False, 0))))
        picks[step, 1, pl.ds(capacity, capacity)] = picks[step, 0, pl.ds(capacity, capacity)]
        if not step:
            first_loads[2].wait()
        for half, side in ((0, 1), (1, 0)):
            compress(step, half, dense.at[step, :, columns_of(half)], (outs.at[step, side], packed.at[step, own(0), columns_of(half)]))
            pack_in[step, side] = start(send(outs.at[step, side], packed.at[step, own(1 + side), columns_of(half)], pack_send.at[step, side], pack_recv.at[step, side], sides[side]))

    def spread_edges(step):
        for side in (0, 1):
            edge_in[side].wait_recv()
            part = edge_half[side]
            edge_in[2 + side] = start(send(edges.at[1 + side, :, part], edges.at[3, :, part], edge_send.at[2 + side], edge_recv.at[2 + side], sides[1 - side]))

    line_peers = {
        True: {1: (beside, 1), 2: (across, 2), 3: (apart, 3)},
        False: {1: (beside, 1), 2: (apart, 3), 3: (across, 2)},
    }

    def deal(step):
        first_loads[3].wait()
        note_in[0, 2].wait_recv()
        for slot in range(slots):
            table = tables[0, slot]
            rank = jnp.dot((table >= 0).astype(bf16), before, preferred_element_type=f32)
            rank = jnp.where(table >= 0, rank, -1.0)
            rows_iota = lax.broadcasted_iota(jnp.int32, table.shape, 0)
            for index, expert in enumerate(line_experts):
                row = jnp.sum(jnp.where(rows_iota == expert, rank, 0.0), axis=0, keepdims=True)
                edge_picks[slot, own(index)] = (places == row).astype(bf16)
            edge_spreads[slot] = lax.dot_general(
                mirror, edge_picks[slot], (((1,), (1,)), ((), ())), preferred_element_type=f32).astype(bf16)
        for side in (0, 1):
            edge_in[2 + side].wait_recv()
        for slot in range(slots):
            made = jnp.dot(edge_picks[slot][:, :count], edges[slot], preferred_element_type=f32).astype(bf16)
            packed[0, own(slot), edge] = made[:capacity]
            for index in (1, 2, 3):
                dealt[index - 1, own(slot)] = made[index * capacity:(index + 1) * capacity]

    def deal_out(step):
        for inside, chosen in ((True, inner), (False, jnp.logical_not(inner))):
            @pl.when(chosen)
            def _(inside=inside):
                dealing(step, inside).start()

    def dealing(step, inside):
        peer, index = line_peers[inside][step]
        target = 1 if step == 1 else later
        return send(dealt.at[index - 1], packed.at[target, :, edge], deal_send.at[index - 1], deal_recv.at[target], peer)

    def relay(step):
        for side in (0, 1):
            other = 1 - side
            note_in[step, side].wait_recv()
            if not side:
                note_in[step, 2] = start(send(tables.at[step, 1], tables.at[step, 3], note_send.at[step, 2], note_recv.at[step, 2], sides[1]))
            prepare(step, 1 + side, ((near_experts[other], (2 + side, False, 0)), (mine, (2 + side, True, 1))))
            half_in[step, side].wait_recv()
            compress(step, 2 + side, halves.at[step, side], (passes.at[step, side], packed.at[step, own(1 + side), columns_of(side)]))
            pass_in[step, side] = start(send(passes.at[step, side], packed.at[step, own(3), columns_of(side)], pass_send.at[step, side], pass_recv.at[step, side], sides[other]))

    def compute(step):
        if step:
            note_in[step, 2].wait_recv()
        prepare(step, 3, ((mine, None),))
        for side in (0, 1):
            pack_in[step, side].wait_recv()
            pass_in[step, side].wait_recv()
        if step:
            pltpu.make_async_remote_copy(
                src_ref=dealt.at[0], dst_ref=packed.at[step, :, edge], send_sem=deal_send.at[0], recv_sem=deal_recv.at[step],
                device_id=beside, device_id_type=MESH,
            ).wait_recv()
        if not step:
            for copy in swaps:
                copy.wait_recv()
            for copy in loads:
                copy.wait()
        for part in (0, 1):
            place = pl.ds(part * 2 * hidden_half, 2 * hidden_half)
            acts[:, place] = jnp.dot(packed[step], first[:, place], preferred_element_type=f32)
        for other in (0, 1):
            gate = acts[:, pl.ds(2 * other * hidden_half, hidden_half)]
            upper = acts[:, pl.ds((2 * other + 1) * hidden_half, hidden_half)]
            hidden[:, pl.ds(other * hidden_half, hidden_half)] = (gate / (1.0 + jnp.exp(-gate)) * upper).astype(bf16)
        share = shares[step][:, :1]
        wide = width // 4 if step else body_width // 2

        def out_of(number, carry):
            place = pl.ds(pl.multiple_of(number * wide, wide), wide)
            made = jnp.dot(hidden[...], second[:, place], preferred_element_type=f32)
            results[step, :, place] = (made * share).astype(bf16)
            return carry

        lax.fori_loop(0, body_width // wide if not step else width // wide, out_of, 0)
        if not step:
            made = (jnp.dot(hidden[...], second[:, edge], preferred_element_type=f32) * share).astype(bf16)
            for slot in range(slots):
                gathered[slot, pl.ds(0, capacity)] = made[slot * capacity:(slot + 1) * capacity]

    def shipment(step, slot, inside):
        peer, index = line_peers[inside][step]
        return send(results.at[step, own(slot), edge], gathered.at[slot, own(index)], ship_send.at[step - 1, slot], ship_recv.at[index - 1, slot], peer)

    def ship(step):
        for inside, chosen in ((True, inner), (False, jnp.logical_not(inner))):
            @pl.when(chosen)
            def _(inside=inside):
                for slot in range(slots):
                    shipment(step, slot, inside).start()

    def gather_edges(slot):
        for index in (1, 2, 3):
            send(results.at[1, own(slot), edge], gathered.at[slot, own(index)], ship_send.at[0, slot], ship_recv.at[index - 1, slot], beside).wait_recv()
        return jnp.dot(edge_spreads[slot], gathered[slot], preferred_element_type=f32)

    merge_in = {}

    def merge(step):
        merged[2] = gather_edges(3).astype(bf16)
        for side in (0, 1):
            merge_in["far", side] = start(send(merged.at[2, :, edge_half[side]], passed_edges.at[side], merge_send.at[0, side], merge_recv.at[0, side], sides[side]))
        for side in (0, 1):
            merged[side] = gather_edges(1 + side).astype(bf16)
            part = edge_half[side]
            merge_in["near", side] = start(send(merged.at[side, :, part], edge_sums.at[side, :, part], merge_send.at[1, side], merge_recv.at[1, side], sides[side]))

    def blend(step):
        for side in (0, 1):
            other = 1 - side
            part = edge_half[side]
            merge_in["far", side].wait_recv()
            blended[other] = (merged[other, :, part].astype(f32) + passed_edges[side].astype(f32)).astype(bf16)
            merge_in["sum", other] = start(send(blended.at[other], edge_sums.at[other, :, part], merge_send.at[2, other], merge_recv.at[2, other], sides[other]))

    def finish(step):
        made = gather_edges(0)
        for side in (0, 1):
            merge_in["near", side].wait_recv()
            merge_in["sum", side].wait_recv()
            made += edge_sums[side].astype(f32)
        out_ref[:, edge] = made.astype(bf16)

    far_in, near_in, sum_in = {}, {}, {}

    def hand_far(step):
        for side in (0, 1):
            far_in[step, side] = start(send(results.at[step, own(3), columns_of(side)], relays.at[step, side], far_send.at[step, side], far_recv.at[step, side], sides[side]))

    def hand_near(step):
        for side in (0, 1):
            near_in[step, side] = start(send(results.at[step, own(1 + side), columns_of(side)], compacts.at[step, side], near_send.at[step, side], near_recv.at[step, side], sides[side]))

    def combine(step):
        for side in (0, 1):
            other = 1 - side
            far_in[step, side].wait_recv()
            theirs = spreads[step, 2 + other, 0]
            ours = spreads[step, 2 + other, 1]

            def body(number, carry, side=side, other=other, theirs=theirs, ours=ours):
                place = pl.ds(pl.multiple_of(number * tile, tile), tile)
                shifted = pl.ds(pl.multiple_of(side * split + number * tile, tile), tile)
                made = jnp.dot(theirs, relays[step, side, :, place], preferred_element_type=f32)
                made += jnp.dot(ours, results[step, own(1 + other), shifted], preferred_element_type=f32)
                relayed[step, other, :, place] = made.astype(bf16)
                return carry

            lax.fori_loop(0, split // tile, body, 0)
            sum_in[step, other] = start(send(relayed.at[step, other], sums.at[step, other], sum_send.at[step, other], sum_recv.at[step, other], sides[other]))

    FAR_SUM, BACK_SUM, LAST_SUM, BESIDE_SUM, ACROSS_SUM = range(5)
    routes = {
        True: {1: (beside, BESIDE_SUM), 2: (across, ACROSS_SUM), 3: (across, BACK_SUM)},
        False: {1: (beside, BESIDE_SUM), 2: (beside, LAST_SUM), 3: (beside, FAR_SUM)},
    }
    added = {
        True: {3: (FAR_SUM,), 2: (LAST_SUM,), 1: (BACK_SUM,), 0: (BESIDE_SUM, ACROSS_SUM)},
        False: {3: (), 2: (), 1: (), 0: (BESIDE_SUM,)},
    }

    def give(step, side, inside):
        peer, inbox = routes[inside][step]
        return send(totals.at[step - 1, :, columns_of(side)], finals.at[inbox, :, columns_of(side)], end_send.at[step - 1, side], end_recv.at[inbox, side], peer)

    def collect(step):
        for side in (0, 1):
            other = 1 - side
            near_in[step, side].wait_recv()
            sum_in[step, other].wait_recv()
            theirs = spreads[step, other, 0]
            ours = spreads[step, 0, 1]

            def total(inside, side=side, other=other, theirs=theirs, ours=ours):
                for inbox in added[inside][step]:
                    send(totals.at[0, :, columns_of(side)], finals.at[inbox, :, columns_of(side)], end_send.at[0, side], end_recv.at[inbox, side], beside).wait_recv()

                def body(number, carry):
                    place = pl.ds(pl.multiple_of(number * tile, tile), tile)
                    shifted = pl.ds(pl.multiple_of(side * split + number * tile, tile), tile)
                    made = jnp.dot(theirs, compacts[step, side, :, place], preferred_element_type=f32)
                    made += jnp.dot(ours, results[step, own(0), shifted], preferred_element_type=f32)
                    made += sums[step, other, :, place].astype(f32)
                    for inbox in added[inside][step]:
                        made += finals[inbox, :, shifted].astype(f32)
                    target = totals.at[step - 1] if step else out_ref
                    target[:, shifted] = made.astype(bf16)
                    return carry

                lax.fori_loop(0, split // tile, body, 0)
                if step:
                    give(step, side, inside).start()

            @pl.when(inner)
            def _(total=total):
                total(True)

            @pl.when(jnp.logical_not(inner))
            def _(total=total):
                total(False)

    table = {
        "pass": pass_on, "issue": issue, "relay": relay, "compute": compute, "far": hand_far, "near": hand_near,
        "combine": combine, "collect": collect, "spread": spread_edges, "deal": deal, "dsend": deal_out, "ship": ship, "merge": merge,
        "blend": blend, "finish": finish,
    }
    for word in ORDER:
        if word == ORDER[-1]:
            settled = len(everything)
            for copy in everything[:-8]:
                copy.wait_send()
            for step in range(1, columns):
                dealing(step, True).wait_send()
                for slot in range(slots):
                    shipment(step, slot, True).wait_send()
        table[word[:-1]](int(word[-1]))

    for copy in everything[settled - 8:]:
        copy.wait_send()
    for step in range(1, columns):
        for side in (0, 1):
            give(step, side, True).wait_send()

    @pl.when(inner)
    def _():
        for copy in (to_across, pass_across, *pass_beside):
            copy.wait_send()


ORDER = (
    "issue0", "spread0", "relay0", "pass2", "pass1", "issue1",
    "deal0", "relay1", "dsend2", "pass3", "issue2", "compute0",
    "relay2", "issue3", "dsend1", "dsend3", "relay3", "compute2",
    "ship2", "far2", "near2", "compute3", "ship3", "far3",
    "combine2", "compute1", "near3", "far1", "ship1", "combine3",
    "far0", "near1", "near0", "collect2", "combine1", "merge0",
    "collect3", "combine0", "collect1", "blend0", "finish0", "collect0",
)


def by_rows(tokens, expert_ids, gate_weights, w_gate, w_up, w_down):
    nodes, columns = lax.axis_size("node"), lax.axis_size("local") // 2
    experts = nodes * columns
    count, width = tokens.shape
    choices = expert_ids.shape[1]
    capacity = capacity_of(count, choices, experts)
    hidden_half = w_gate.shape[1]
    extra = width * 3 // 16
    body_width = width - extra
    split = body_width // 2
    dma = pltpu.SemaphoreType.DMA
    bf16, f32 = jnp.bfloat16, jnp.float32
    scratch = [
        pltpu.VMEM((choices, count), jnp.int32),
        pltpu.VMEM((choices, count), f32),
        pltpu.VMEM((columns, 4, experts, LANES), f32),
        pltpu.VMEM((columns, 4 * capacity, LANES), f32),
        pltpu.VMEM((columns, 4, 2 * capacity, LANES), bf16),
        pltpu.VMEM((columns, 4, 2, count, capacity), bf16),
        pltpu.VMEM((width, 4 * hidden_half), bf16),
        pltpu.VMEM((2 * hidden_half, width), bf16),
        pltpu.VMEM((columns, count, body_width), bf16),
        pltpu.VMEM((columns, 2, count, split), bf16),
        pltpu.VMEM((columns, 4 * capacity, width), bf16),
        pltpu.VMEM((columns, 2, capacity, split), bf16),
        pltpu.VMEM((columns, 2, capacity, split), bf16),
        pltpu.VMEM((4 * capacity, 4 * hidden_half), f32),
        pltpu.VMEM((4 * capacity, 2 * hidden_half), bf16),
        pltpu.VMEM((columns, 4 * capacity, width), bf16),
        pltpu.VMEM((columns, 2, capacity, split), bf16),
        pltpu.VMEM((columns, 2, capacity, split), bf16),
        pltpu.VMEM((columns, 2, count, split), bf16),
        pltpu.VMEM((columns, 2, count, split), bf16),
        pltpu.VMEM((columns - 1, count, body_width), bf16),
        pltpu.VMEM((5, count, body_width), bf16),
        pltpu.VMEM((4, count, extra), bf16),
        pltpu.VMEM((4, columns * capacity, LANES), bf16),
        pltpu.VMEM((4, count, columns * capacity), bf16),
        pltpu.VMEM((columns - 1, 4 * capacity, extra), bf16),
        pltpu.VMEM((4, columns * capacity, extra), bf16),
        pltpu.VMEM((3, count, extra), bf16),
        pltpu.VMEM((2, count, extra // 2), bf16),
        pltpu.VMEM((2, count, extra // 2), bf16),
        pltpu.VMEM((2, count, extra), bf16),
        dma((7,)), dma((3,)), dma((3,)), dma((5,)), dma((columns,)), dma((columns - 1,)), dma((columns,)),
        dma((columns, 2)), dma((columns, 2)), dma((columns, 3)), dma((columns, 3)),
        dma((columns, 2)), dma((columns, 2)), dma((columns, 2)), dma((columns, 2)),
        dma((columns, 2)), dma((columns, 2)), dma((columns, 2)), dma((columns, 2)),
        dma((columns, 2)), dma((columns, 2)), dma((columns - 1, 2)), dma((5, 2)),
        dma((4,)), dma((4,)), dma((columns - 1,)), dma((columns,)), dma((columns - 1, 4)), dma((columns - 1, 4)),
        dma((3, 2)), dma((3, 2)),
    ]
    flops = 12 * experts * count * width * hidden_half
    return pl.pallas_call(
        functools.partial(layer_kernel, nodes, columns, capacity, extra),
        name="moe_layer",
        out_shape=pltpu.VMEM((count, width), bf16),
        in_specs=[pl.BlockSpec(memory_space=pl.ANY)] * 6,
        out_specs=pl.BlockSpec(memory_space=pltpu.VMEM),
        scratch_shapes=scratch,
        cost_estimate=pl.CostEstimate(flops=flops, bytes_accessed=w_gate.size * 12, transcendentals=0),
        compiler_params=pltpu.CompilerParams(collective_id=0, has_side_effects=True, vmem_limit_bytes=56 << 20),
    )(tokens, expert_ids.T, gate_weights.T, w_gate, w_up, w_down)


def capacity_of(rows, choices, experts):
    return rows * choices * 5 // (4 * experts)


def per_device(tokens, expert_ids, *rest):
    nodes, columns = lax.axis_size("node"), lax.axis_size("local") // 2
    count = tokens.shape[0]
    capacity = capacity_of(count, expert_ids.shape[1], nodes * columns)
    if nodes == 4 and columns == 4 and count <= LANES and capacity % 8 == 0:
        return by_rows(tokens, expert_ids, *rest)
    return by_slots(tokens, expert_ids, *rest)


def solution(mesh):
    placed = (
        P(("parts", "node", "local"), None),
        P(("parts", "node", "local"), None),
        P(("parts", "node", "local"), None),
        P(None, ("parts", "node", "local")),
        P(None, ("parts", "node", "local")),
        P(("parts", "node", "local"), None),
    )
    return jax.shard_map(
        per_device,
        mesh=mesh,
        in_specs=placed,
        out_specs=P(("parts", "node", "local"), None),
        check_vma=False,
    )
```

```python
import functools

import jax
import jax.numpy as jnp
from jax import lax
from jax.experimental import pallas as pl
from jax.experimental.pallas import tpu as pltpu
from jax.sharding import PartitionSpec as P

MESH = pl.DeviceIdType.MESH


def partner_2(value, axis, bit):
    mask = 2**bit
    pairs = [(source, source ^ mask) for source in range(lax.axis_size(axis))]
    return lax.ppermute(value, axis, pairs)


def by_slots(tokens, expert_ids, gate_weights, w_gate, w_up, w_down):
    node_count = lax.axis_size("node")
    local_count = lax.axis_size("local")
    devices = node_count * local_count
    experts = devices // 2
    tok_rows, top_count = expert_ids.shape
    width = tokens.shape[1]
    capacity = tok_rows * top_count * 5 // (4 * experts)
    flat_ids = expert_ids.reshape(-1)
    one_hot = (flat_ids[:, None] == jnp.arange(experts, dtype=jnp.int32)[None, :]).astype(jnp.int32)
    earlier = jnp.cumsum(one_hot, axis=0) - one_hot
    slot_rank = jnp.sum(earlier * one_hot, axis=1)
    slot_index = (flat_ids * capacity + slot_rank).reshape(tok_rows, top_count)
    slot_table = jnp.any(
        slot_index[None, :, :] == jnp.arange(experts * capacity, dtype=jnp.int32)[:, None, None],
        axis=2,
    ).astype(jnp.bfloat16)
    outgoing = jnp.dot(slot_table, tokens, preferred_element_type=jnp.float32).astype(jnp.bfloat16)
    outgoing = outgoing.reshape(devices, capacity // 2, width)
    partner = partner_2((w_gate, w_up, w_down), "local", 0)
    full_gate = jnp.concatenate([w_gate, partner[0]], axis=1)
    full_up = jnp.concatenate([w_up, partner[1]], axis=1)
    full_down = jnp.concatenate([w_down, partner[2]], axis=0)
    block = lax.all_to_all(outgoing, ("node", "local"), split_axis=0, concat_axis=0, tiled=True)
    rows = block.reshape(-1, width)
    gate = jnp.dot(rows, full_gate, preferred_element_type=jnp.float32)
    upper = jnp.dot(rows, full_up, preferred_element_type=jnp.float32)
    hidden = (jax.nn.silu(gate) * upper).astype(jnp.bfloat16)
    result = jnp.dot(hidden, full_down, preferred_element_type=jnp.float32).astype(jnp.bfloat16)
    processed = result.reshape(block.shape)
    returned = lax.all_to_all(processed, ("node", "local"), split_axis=0, concat_axis=0, tiled=True)
    results = returned.reshape(experts * capacity, width)
    chosen = results[slot_index]
    mixed = jnp.sum(gate_weights[:, :, None] * chosen.astype(jnp.float32), axis=1)
    return mixed.astype(jnp.bfloat16)


LANES = 128


def layer_kernel(
    nodes, columns, capacity, extra,
    rows_ref, ids_ref, weights_ref, gate_ref, up_ref, down_ref, out_ref,
    ids, weights, tables, shares, picks, spreads,
    first, second, dense, halves, packed, outs, passes, acts, hidden,
    results, relays, compacts, relayed, sums, totals, finals, output,
    edges, edge_picks, edge_spreads, dealt, gathered, merged, passed_edges, blended, edge_sums,
    load_sem, swap_send, swap_recv, line_recv, list_send, list_recv, half_recv, note_recv, pack_recv, pass_recv,
    far_recv, near_recv, sum_recv, end_recv, edge_recv, deal_recv, ship_recv, merge_recv, sent, ready,
):
    part, node, local = lax.axis_index("parts"), lax.axis_index("node"), lax.axis_index("local")
    column, core = local // 2, lax.rem(local, 2)
    high, low = node // 2, lax.rem(node, 2)
    count, width = rows_ref.shape
    hidden_half = gate_ref.shape[1]
    body_width = width - extra
    split = body_width // 2
    slots = 4
    bf16, f32 = jnp.bfloat16, jnp.float32
    inner = (column == 1) | (column == 2)

    def at(node_index, local_index):
        return (part, node_index, local_index)

    sides = (at(high * 2 + 1 - low, local), at((1 - high) * 2 + low, local))
    side_nodes = (high * 2 + 1 - low, (1 - high) * 2 + low)
    twin = at(node, column * 2 + 1 - core)
    low_flip = column + 1 - 2 * lax.rem(column, 2)
    beside = at(node, low_flip * 2 + core)
    across = at(node, (columns - 1 - column) * 2 + core)
    apart = at(node, (columns - 1 - low_flip) * 2 + core)
    later = jnp.where(inner, 2, 3)

    barrier = pltpu.get_barrier_semaphore()
    greeted = (*sides, twin, beside)
    for peer in greeted:
        pl.semaphore_signal(barrier, inc=1, device_id=peer, device_id_type=MESH)

    @pl.when(inner)
    def _():
        pl.semaphore_signal(barrier, inc=1, device_id=across, device_id_type=MESH)
        pl.semaphore_wait(barrier, len(greeted) + 1)
        pl.semaphore_signal(ready.at[0], inc=1, device_id=beside, device_id_type=MESH)
        pl.semaphore_signal(ready.at[1], inc=1, device_id=across, device_id_type=MESH)

    @pl.when(jnp.logical_not(inner))
    def _():
        pl.semaphore_wait(barrier, len(greeted))

    everything, inner_only = [], []

    def send(source, target, send_sem, recv_sem, peer):
        return pltpu.make_async_remote_copy(
            src_ref=source, dst_ref=target, send_sem=send_sem, recv_sem=recv_sem,
            device_id=peer, device_id_type=MESH,
        )

    def start(copy):
        copy.start()
        return copy

    def kept(copy):
        everything.append(copy)
        return start(copy)

    def columns_of(side):
        return pl.ds(side * split, split)

    def own(slot):
        return pl.ds(slot * capacity, capacity)

    body = pl.ds(0, body_width)
    edge = pl.ds(body_width, extra)
    edge_half = (pl.ds(0, extra // 2), pl.ds(extra // 2, extra // 2))

    half_in = {}
    line_in = {}
    list_in = {}
    note_in = {}
    pack_in = {}
    pass_in = {}

    def send_halves(step, source):
        for side in (0, 1):
            half_in[step, side] = start(send(source.at[:, columns_of(side)], halves.at[step, side], sent.at[SENT["half"]], half_recv.at[step, side], sides[side]))

    edge_in = {}
    for side in (0, 1):
        edge_in[side] = start(send(rows_ref.at[:, edge], edges.at[1 + side], sent.at[SENT["edge"]], edge_recv.at[side], sides[side]))
    send_halves(0, rows_ref)
    line_in[1] = start(send(rows_ref.at[:, body], dense.at[1], sent.at[SENT["line"]], line_recv.at[1], beside))
    to_across = send(rows_ref.at[:, body], dense.at[2], sent.at[SENT["line"]], line_recv.at[2], across)
    pass_across = send(dense.at[1], dense.at[3], sent.at[SENT["line"]], line_recv.at[3], across)
    pass_beside = (
        send(dense.at[2], dense.at[2], sent.at[SENT["line"]], line_recv.at[2], beside),
        send(dense.at[3], dense.at[3], sent.at[SENT["line"]], line_recv.at[3], beside),
    )
    line_in[2], line_in[3] = to_across, pass_across

    @pl.when(inner)
    def _():
        to_across.start()

    first_loads = [
        pltpu.make_async_copy(ids_ref, ids, load_sem.at[0]),
        pltpu.make_async_copy(weights_ref, weights, load_sem.at[1]),
        pltpu.make_async_copy(rows_ref.at[:, body], dense.at[0], load_sem.at[2]),
        pltpu.make_async_copy(rows_ref.at[:, edge], edges.at[0], load_sem.at[6]),
    ]
    for copy in first_loads:
        copy.start()

    def spot(target, index, by_rows, other):
        place = pl.ds((index + other) * hidden_half, hidden_half)
        return target.at[place] if by_rows else target.at[:, place]

    near = ((gate_ref, first, 0, False), (up_ref, first, 1, False), (down_ref, second, 0, True))
    swaps, loads = [], []
    for number, (source, target, index, by_rows) in enumerate(near):
        swaps.append(kept(send(source, spot(target, index, by_rows, 1 if by_rows else 2), swap_send.at[number], swap_recv.at[number], twin)))
        loads.append(pltpu.make_async_copy(source, spot(target, index, by_rows, 0), load_sem.at[3 + number]))
        loads[-1].start()

    for copy in first_loads[:2]:
        copy.wait()
    experts = nodes * columns
    expert_iota = lax.broadcasted_iota(jnp.int32, (experts, count), 0)
    listed = jnp.full((experts, count), -1.0, f32)
    for choice in range(ids.shape[0]):
        listed = jnp.where(ids[pl.ds(choice, 1), :] == expert_iota, weights[pl.ds(choice, 1), :], listed)
    tables[0, 0] = jnp.full((experts, LANES), -1.0, f32)
    tables[0, 0, :, pl.ds(0, count)] = listed

    list_in[1] = kept(send(tables.at[0, 0], tables.at[1, 0], list_send.at[0], list_recv.at[1], beside))
    list_across = send(tables.at[0, 0], tables.at[2, 0], list_send.at[1], list_recv.at[2], across)
    list_on = (
        send(tables.at[1, 0], tables.at[3, 0], list_send.at[2], list_recv.at[3], across),
        send(tables.at[2, 0], tables.at[2, 0], list_send.at[3], list_recv.at[2], beside),
        send(tables.at[3, 0], tables.at[3, 0], list_send.at[4], list_recv.at[3], beside),
    )
    list_in[2], list_in[3] = list_across, list_on[0]

    @pl.when(inner)
    def _():
        list_across.start()

    def send_notes(step):
        for side in (0, 1):
            note_in[step, side] = start(send(tables.at[step, 0], tables.at[step, 1 + side], sent.at[SENT["note"]], note_recv.at[step, side], sides[side]))

    before = (lax.broadcasted_iota(jnp.int32, (LANES, LANES), 0) < lax.broadcasted_iota(jnp.int32, (LANES, LANES), 1)).astype(bf16)
    places = lax.broadcasted_iota(jnp.int32, (capacity, LANES), 0).astype(f32)
    mirror = (lax.broadcasted_iota(jnp.int32, (count, LANES), 0) == lax.broadcasted_iota(jnp.int32, (count, LANES), 1)).astype(bf16)
    mine = node * columns + column
    near_experts = tuple(side_node * columns + column for side_node in side_nodes)
    line_experts = (mine, node * columns + low_flip, node * columns + (columns - 1 - column), node * columns + (columns - 1 - low_flip))

    def prepare(step, slot, wanted):
        table = tables[step, slot]
        rank = jnp.dot((table >= 0).astype(bf16), before, preferred_element_type=f32)
        rank = jnp.where(table >= 0, rank, -1.0)
        rows_iota = lax.broadcasted_iota(jnp.int32, table.shape, 0)
        for expert, index in wanted:
            chosen = rows_iota == expert
            row = jnp.sum(jnp.where(chosen, rank, 0.0), axis=0, keepdims=True)
            pick = (places == row).astype(f32)
            if index is None or index[1]:
                value = jnp.sum(jnp.where(chosen, table, 0.0), axis=0, keepdims=True)
                share = jnp.sum(pick * value, axis=1, keepdims=True)
                shares[step, own(slot)] = jnp.broadcast_to(share, (capacity, LANES))
            if index is not None:
                picked = pick.astype(bf16)
                picks[step, index[0], pl.ds(index[2] * capacity, capacity)] = picked
                spreads[step, index[0], index[2]] = lax.dot_general(
                    mirror, picked, (((1,), (1,)), ((), ())), preferred_element_type=f32).astype(bf16)

    tile = split

    def compress(step, index, source, targets):
        wanted = picks[step, index][:, :count]

        def body(number, carry):
            place = pl.ds(pl.multiple_of(number * tile, tile), tile)
            made = jnp.dot(wanted, source[:, place], preferred_element_type=f32).astype(bf16)
            for which, target in enumerate(targets):
                target[:, place] = made[which * capacity:(which + 1) * capacity]
            return carry

        lax.fori_loop(0, split // tile, body, 0)

    passed = {}

    def pass_on(step):
        passed[step] = True

        @pl.when(inner)
        def _():
            line_in[step].wait_recv()
            (pass_across, *pass_beside)[step - 1].start()
            list_in[step].wait_recv()
            list_on[step - 1].start()
            if step == 1:
                pl.semaphore_wait(ready.at[1], 1)
                pl.semaphore_signal(ready.at[1], inc=1, device_id=beside, device_id_type=MESH)

    def issue(step):
        if step:
            @pl.when(jnp.logical_not(inner) | (step not in passed))
            def _():
                line_in[step].wait_recv()
                list_in[step].wait_recv()

            send_halves(step, dense.at[step])
        send_notes(step)
        prepare(step, 0, ((near_experts[1], (0, False, 0)), (mine, (0, True, 1)), (near_experts[0], (1, False, 0))))
        picks[step, 1, pl.ds(capacity, capacity)] = picks[step, 0, pl.ds(capacity, capacity)]
        if not step:
            first_loads[2].wait()
        for half, side in ((0, 1), (1, 0)):
            compress(step, half, dense.at[step, :, columns_of(half)], (outs.at[step, side], packed.at[step, own(0), columns_of(half)]))
            pack_in[step, side] = start(send(outs.at[step, side], packed.at[step, own(1 + side), columns_of(half)], sent.at[SENT["pack"]], pack_recv.at[step], sides[side]))

    def spread_edges(step):
        for side in (0, 1):
            edge_in[side].wait_recv()
            part = edge_half[side]
            edge_in[2 + side] = start(send(edges.at[1 + side, :, part], edges.at[3, :, part], sent.at[SENT["edge"]], edge_recv.at[2 + side], sides[1 - side]))

    line_peers = {
        True: {1: (beside, 1), 2: (across, 2), 3: (apart, 3)},
        False: {1: (beside, 1), 2: (apart, 3), 3: (across, 2)},
    }

    def deal(step):
        first_loads[3].wait()
        note_in[0, 2].wait_recv()

        @pl.when(jnp.logical_not(inner))
        def _():
            pl.semaphore_wait(ready.at[0], 1)
            pl.semaphore_wait(ready.at[1], 1)

        for slot in range(slots):
            table = tables[0, slot]
            rank = jnp.dot((table >= 0).astype(bf16), before, preferred_element_type=f32)
            rank = jnp.where(table >= 0, rank, -1.0)
            rows_iota = lax.broadcasted_iota(jnp.int32, table.shape, 0)
            for index, expert in enumerate(line_experts):
                row = jnp.sum(jnp.where(rows_iota == expert, rank, 0.0), axis=0, keepdims=True)
                edge_picks[slot, own(index)] = (places == row).astype(bf16)
            edge_spreads[slot] = lax.dot_general(
                mirror, edge_picks[slot], (((1,), (1,)), ((), ())), preferred_element_type=f32).astype(bf16)
        for side in (0, 1):
            edge_in[2 + side].wait_recv()
        for slot in range(slots):
            made = jnp.dot(edge_picks[slot][:, :count], edges[slot], preferred_element_type=f32).astype(bf16)
            packed[0, own(slot), edge] = made[:capacity]
            for index in (1, 2, 3):
                dealt[index - 1, own(slot)] = made[index * capacity:(index + 1) * capacity]

    def deal_out(step):
        for inside, chosen in ((True, inner), (False, jnp.logical_not(inner))):
            @pl.when(chosen)
            def _(inside=inside):
                dealing(step, inside).start()

    def dealing(step, inside):
        peer, index = line_peers[inside][step]
        target = 1 if step == 1 else later
        return send(dealt.at[index - 1], packed.at[target, :, edge], sent.at[SENT["deal"]], deal_recv.at[target], peer)

    def relay(step):
        for side in (0, 1):
            other = 1 - side
            note_in[step, side].wait_recv()
            if not side:
                note_in[step, 2] = start(send(tables.at[step, 1], tables.at[step, 3], sent.at[SENT["note"]], note_recv.at[step, 2], sides[1]))
            prepare(step, 1 + side, ((near_experts[other], (2 + side, False, 0)), (mine, (2 + side, True, 1))))
            half_in[step, side].wait_recv()
            compress(step, 2 + side, halves.at[step, side], (passes.at[step, side], packed.at[step, own(1 + side), columns_of(side)]))
            pass_in[step, side] = start(send(passes.at[step, side], packed.at[step, own(3), columns_of(side)], sent.at[SENT["pass"]], pass_recv.at[step], sides[other]))

    def compute(step):
        if step:
            note_in[step, 2].wait_recv()
        prepare(step, 3, ((mine, None),))
        pltpu.make_async_copy(outs.at[step], outs.at[step], pack_recv.at[step]).wait()
        pltpu.make_async_copy(passes.at[step], passes.at[step], pass_recv.at[step]).wait()
        if step:
            pltpu.make_async_remote_copy(
                src_ref=dealt.at[0], dst_ref=packed.at[step, :, edge], send_sem=sent.at[SENT["deal"]], recv_sem=deal_recv.at[step],
                device_id=beside, device_id_type=MESH,
            ).wait_recv()
        if not step:
            for copy in swaps:
                copy.wait_recv()
            for copy in loads:
                copy.wait()
        for part in (0, 1):
            place = pl.ds(part * 2 * hidden_half, 2 * hidden_half)
            acts[:, place] = jnp.dot(packed[step], first[:, place], preferred_element_type=f32)
        for other in (0, 1):
            gate = acts[:, pl.ds(2 * other * hidden_half, hidden_half)]
            upper = acts[:, pl.ds((2 * other + 1) * hidden_half, hidden_half)]
            hidden[:, pl.ds(other * hidden_half, hidden_half)] = (gate / (1.0 + jnp.exp(-gate)) * upper).astype(bf16)
        share = shares[step][:, :1]
        wide = width // 4 if step else body_width // 2

        def out_of(number, carry):
            place = pl.ds(pl.multiple_of(number * wide, wide), wide)
            made = jnp.dot(hidden[...], second[:, place], preferred_element_type=f32)
            results[step, :, place] = (made * share).astype(bf16)
            return carry

        lax.fori_loop(0, body_width // wide if not step else width // wide, out_of, 0)
        if not step:
            made = (jnp.dot(hidden[...], second[:, edge], preferred_element_type=f32) * share).astype(bf16)
            for slot in range(slots):
                gathered[slot, pl.ds(0, capacity)] = made[slot * capacity:(slot + 1) * capacity]

    def shipment(step, slot, inside):
        peer, index = line_peers[inside][step]
        return send(results.at[step, own(slot), edge], gathered.at[slot, own(index)], sent.at[SENT["ship"]], ship_recv.at[slot], peer)

    def ship(step):
        for inside, chosen in ((True, inner), (False, jnp.logical_not(inner))):
            @pl.when(chosen)
            def _(inside=inside):
                for slot in range(slots):
                    shipment(step, slot, inside).start()

    def gather_edges(slot):
        others = gathered.at[slot, pl.ds(capacity, (columns - 1) * capacity)]
        pltpu.make_async_copy(others, others, ship_recv.at[slot]).wait()
        return jnp.dot(edge_spreads[slot], gathered[slot], preferred_element_type=f32)

    merge_in = {}

    def merge(step):
        merged[2] = gather_edges(3).astype(bf16)
        for side in (0, 1):
            merge_in["far", side] = start(send(merged.at[2, :, edge_half[side]], passed_edges.at[side], sent.at[SENT["merge"]], merge_recv.at[0, side], sides[side]))
        for side in (0, 1):
            merged[side] = gather_edges(1 + side).astype(bf16)
            part = edge_half[side]
            merge_in["near", side] = start(send(merged.at[side, :, part], edge_sums.at[side, :, part], sent.at[SENT["merge"]], merge_recv.at[1, side], sides[side]))

    def blend(step):
        for side in (0, 1):
            other = 1 - side
            part = edge_half[side]
            merge_in["far", side].wait_recv()
            blended[other] = (merged[other, :, part].astype(f32) + passed_edges[side].astype(f32)).astype(bf16)
            merge_in["sum", other] = start(send(blended.at[other], edge_sums.at[other, :, part], sent.at[SENT["merge"]], merge_recv.at[2, other], sides[other]))

    def finish(step):
        made = gather_edges(0)
        for side in (0, 1):
            merge_in["near", side].wait_recv()
            merge_in["sum", side].wait_recv()
            made += edge_sums[side].astype(f32)
        output[:, edge] = made.astype(bf16)
        hand_out(0, edge).start()

    far_in, near_in, sum_in = {}, {}, {}

    def hand_far(step):
        for side in (0, 1):
            far_in[step, side] = start(send(results.at[step, own(3), columns_of(side)], relays.at[step, side], sent.at[SENT["far"]], far_recv.at[step, side], sides[side]))

    def hand_near(step):
        for side in (0, 1):
            near_in[step, side] = start(send(results.at[step, own(1 + side), columns_of(side)], compacts.at[step, side], sent.at[SENT["near"]], near_recv.at[step, side], sides[side]))

    def combine(step):
        for side in (0, 1):
            other = 1 - side
            far_in[step, side].wait_recv()
            theirs = spreads[step, 2 + other, 0]
            ours = spreads[step, 2 + other, 1]

            def body(number, carry, side=side, other=other, theirs=theirs, ours=ours):
                place = pl.ds(pl.multiple_of(number * tile, tile), tile)
                shifted = pl.ds(pl.multiple_of(side * split + number * tile, tile), tile)
                made = jnp.dot(theirs, relays[step, side, :, place], preferred_element_type=f32)
                made += jnp.dot(ours, results[step, own(1 + other), shifted], preferred_element_type=f32)
                relayed[step, other, :, place] = made.astype(bf16)
                return carry

            lax.fori_loop(0, split // tile, body, 0)
            sum_in[step, other] = start(send(relayed.at[step, other], sums.at[step, other], sent.at[SENT["sum"]], sum_recv.at[step, other], sides[other]))

    FAR_SUM, BACK_SUM, LAST_SUM, BESIDE_SUM, ACROSS_SUM = range(5)
    routes = {
        True: {1: (beside, BESIDE_SUM), 2: (across, ACROSS_SUM), 3: (across, BACK_SUM)},
        False: {1: (beside, BESIDE_SUM), 2: (beside, LAST_SUM), 3: (beside, FAR_SUM)},
    }
    added = {
        True: {3: (FAR_SUM,), 2: (LAST_SUM,), 1: (BACK_SUM,), 0: (BESIDE_SUM, ACROSS_SUM)},
        False: {3: (), 2: (), 1: (), 0: (BESIDE_SUM,)},
    }

    cut = (split // LANES + 1) // 2 * LANES
    parts = ((0, cut), (cut, split - cut))

    def give(step, side, part, inside):
        peer, inbox = routes[inside][step]
        place = pl.ds(side * split + parts[part][0], parts[part][1])
        return send(
            totals.at[step - 1, :, place], finals.at[inbox, :, place], sent.at[SENT["end"]], end_recv.at[inbox, side, part], peer)

    def given(inbox, side, part):
        place = pl.ds(side * split + parts[part][0], parts[part][1])
        return send(
            totals.at[0, :, place], finals.at[inbox, :, place], sent.at[SENT["end"]], end_recv.at[inbox, side, part], beside)

    def hand_out(number, place):
        return pltpu.make_async_copy(output.at[:, place], out_ref.at[:, place], load_sem.at[number])

    def collect(step):
        for side in (0, 1):
            other = 1 - side
            near_in[step, side].wait_recv()
            sum_in[step, other].wait_recv()

            def total(inside, side=side, other=other):
                for part, (base, size) in enumerate(parts):
                    for inbox in added[inside][step]:
                        given(inbox, side, part).wait_recv()
                    place = pl.ds(base, size)
                    shifted = pl.ds(side * split + base, size)
                    made = jnp.dot(spreads[step, other, 0], compacts[step, side, :, place], preferred_element_type=f32)
                    made += jnp.dot(spreads[step, 0, 1], results[step, own(0), shifted], preferred_element_type=f32)
                    made += sums[step, other, :, place].astype(f32)
                    for inbox in added[inside][step]:
                        made += finals[inbox, :, shifted].astype(f32)
                    target = totals.at[step - 1] if step else output
                    target[:, shifted] = made.astype(bf16)
                    if step:
                        give(step, side, part, inside).start()
                    else:
                        hand_out(1 + 2 * side + part, shifted).start()

            @pl.when(inner)
            def _(total=total):
                total(True)

            @pl.when(jnp.logical_not(inner))
            def _(total=total):
                total(False)

    table = {
        "pass": pass_on, "issue": issue, "relay": relay, "compute": compute, "far": hand_far, "near": hand_near,
        "combine": combine, "collect": collect, "spread": spread_edges, "deal": deal, "dsend": deal_out, "ship": ship, "merge": merge,
        "blend": blend, "finish": finish,
    }
    def settle(name, held):
        pltpu.make_async_copy(held, held, sent.at[SENT[name]]).wait()

    for word in ORDER:
        if word == ORDER[-1]:
            for copy in everything:
                copy.wait_send()
            settle("half", halves)
            settle("note", tables.at[:, pl.ds(1, slots - 1)])
            settle("pack", outs)
            settle("pass", passes)
            settle("far", relays)
            settle("deal", dealt)
            settle("ship", gathered.at[:, pl.ds(capacity, (columns - 1) * capacity)])
            settle("edge", merged)

            @pl.when(inner)
            def _():
                settle("line", finals)
                for copy in (list_across, *list_on):
                    copy.wait_send()

            @pl.when(jnp.logical_not(inner))
            def _():
                settle("line", dense.at[1])
        table[word[:-1]](int(word[-1]))

    settle("near", compacts)
    settle("sum", sums)
    settle("end", totals)
    settle("merge", merged)
    hand_out(0, edge).wait()
    for side in (0, 1):
        for part, (base, size) in enumerate(parts):
            hand_out(1 + 2 * side + part, pl.ds(side * split + base, size)).wait()


NAMES = ("half", "note", "pack", "pass", "far", "near", "sum", "end", "edge", "deal", "ship", "merge", "line")
SENT = {name: number for number, name in enumerate(NAMES)}

ORDER = (
    "spread0", "issue0", "pass1", "issue1", "pass2", "relay0",
    "deal0", "relay1", "pass3", "issue2", "dsend2", "relay2",
    "issue3", "dsend1", "dsend3", "compute0", "relay3", "compute2",
    "ship2", "far2", "near2", "compute3", "far3", "ship3",
    "combine2", "near3", "compute1", "far1", "ship1", "combine3",
    "near1", "far0", "collect2", "combine1", "near0", "merge0",
    "collect3", "combine0", "collect1", "blend0", "collect0", "finish0",
)


def by_rows(tokens, expert_ids, gate_weights, w_gate, w_up, w_down):
    nodes, columns = lax.axis_size("node"), lax.axis_size("local") // 2
    experts = nodes * columns
    count, width = tokens.shape
    choices = expert_ids.shape[1]
    capacity = capacity_of(count, choices, experts)
    hidden_half = w_gate.shape[1]
    extra = width * 3 // 16
    body_width = width - extra
    split = body_width // 2
    dma = pltpu.SemaphoreType.DMA
    bf16, f32 = jnp.bfloat16, jnp.float32
    scratch = [
        pltpu.VMEM((choices, count), jnp.int32),
        pltpu.VMEM((choices, count), f32),
        pltpu.VMEM((columns, 4, experts, LANES), f32),
        pltpu.VMEM((columns, 4 * capacity, LANES), f32),
        pltpu.VMEM((columns, 4, 2 * capacity, LANES), bf16),
        pltpu.VMEM((columns, 4, 2, count, capacity), bf16),
        pltpu.VMEM((width, 4 * hidden_half), bf16),
        pltpu.VMEM((2 * hidden_half, width), bf16),
        pltpu.VMEM((columns, count, body_width), bf16),
        pltpu.VMEM((columns, 2, count, split), bf16),
        pltpu.VMEM((columns, 4 * capacity, width), bf16),
        pltpu.VMEM((columns, 2, capacity, split), bf16),
        pltpu.VMEM((columns, 2, capacity, split), bf16),
        pltpu.VMEM((4 * capacity, 4 * hidden_half), f32),
        pltpu.VMEM((4 * capacity, 2 * hidden_half), bf16),
        pltpu.VMEM((columns, 4 * capacity, width), bf16),
        pltpu.VMEM((columns, 2, capacity, split), bf16),
        pltpu.VMEM((columns, 2, capacity, split), bf16),
        pltpu.VMEM((columns, 2, count, split), bf16),
        pltpu.VMEM((columns, 2, count, split), bf16),
        pltpu.VMEM((columns - 1, count, body_width), bf16),
        pltpu.VMEM((5, count, body_width), bf16),
        pltpu.VMEM((count, width), bf16),
        pltpu.VMEM((4, count, extra), bf16),
        pltpu.VMEM((4, columns * capacity, LANES), bf16),
        pltpu.VMEM((4, count, columns * capacity), bf16),
        pltpu.VMEM((columns - 1, 4 * capacity, extra), bf16),
        pltpu.VMEM((4, columns * capacity, extra), bf16),
        pltpu.VMEM((3, count, extra), bf16),
        pltpu.VMEM((2, count, extra // 2), bf16),
        pltpu.VMEM((2, count, extra // 2), bf16),
        pltpu.VMEM((2, count, extra), bf16),
        dma((7,)), dma((3,)), dma((3,)), dma((columns,)), dma((5,)), dma((columns,)),
        dma((columns, 2)), dma((columns, 3)), dma((columns,)), dma((columns,)),
        dma((columns, 2)), dma((columns, 2)), dma((columns, 2)), dma((5, 2, 2)),
        dma((4,)), dma((columns,)), dma((4,)), dma((3, 2)),
        dma((len(SENT),)), pltpu.SemaphoreType.REGULAR((2,)),
    ]
    flops = 12 * experts * count * width * hidden_half
    return pl.pallas_call(
        functools.partial(layer_kernel, nodes, columns, capacity, extra),
        name="moe_layer",
        out_shape=pltpu.VMEM((count, width), bf16),
        in_specs=[pl.BlockSpec(memory_space=pl.ANY)] * 6,
        out_specs=pl.BlockSpec(memory_space=pl.ANY),
        scratch_shapes=scratch,
        cost_estimate=pl.CostEstimate(flops=flops, bytes_accessed=w_gate.size * 12, transcendentals=0),
        compiler_params=pltpu.CompilerParams(collective_id=0, has_side_effects=True, vmem_limit_bytes=56 << 20),
    )(tokens, expert_ids.T, gate_weights.T, w_gate, w_up, w_down)


def capacity_of(rows, choices, experts):
    return rows * choices * 5 // (4 * experts)


def per_device(tokens, expert_ids, *rest):
    nodes, columns = lax.axis_size("node"), lax.axis_size("local") // 2
    count = tokens.shape[0]
    capacity = capacity_of(count, expert_ids.shape[1], nodes * columns)
    if nodes == 4 and columns == 4 and count <= LANES and capacity % 8 == 0:
        return by_rows(tokens, expert_ids, *rest)
    return by_slots(tokens, expert_ids, *rest)


def solution(mesh):
    placed = (
        P(("parts", "node", "local"), None),
        P(("parts", "node", "local"), None),
        P(("parts", "node", "local"), None),
        P(None, ("parts", "node", "local")),
        P(None, ("parts", "node", "local")),
        P(("parts", "node", "local"), None),
    )
    return jax.shard_map(
        per_device,
        mesh=mesh,
        in_specs=placed,
        out_specs=P(("parts", "node", "local"), None),
        check_vma=False,
    )
```

```python
import functools

import jax
import jax.numpy as jnp
from jax import lax
from jax.experimental import pallas as pl
from jax.experimental.pallas import tpu as pltpu
from jax.sharding import PartitionSpec as P

MESH = pl.DeviceIdType.MESH


def partner_2(value, axis, bit):
    mask = 2**bit
    pairs = [(source, source ^ mask) for source in range(lax.axis_size(axis))]
    return lax.ppermute(value, axis, pairs)


def by_slots(tokens, expert_ids, gate_weights, w_gate, w_up, w_down):
    node_count = lax.axis_size("node")
    local_count = lax.axis_size("local")
    devices = node_count * local_count
    experts = devices // 2
    tok_rows, top_count = expert_ids.shape
    width = tokens.shape[1]
    capacity = tok_rows * top_count * 5 // (4 * experts)
    flat_ids = expert_ids.reshape(-1)
    one_hot = (flat_ids[:, None] == jnp.arange(experts, dtype=jnp.int32)[None, :]).astype(jnp.int32)
    earlier = jnp.cumsum(one_hot, axis=0) - one_hot
    slot_rank = jnp.sum(earlier * one_hot, axis=1)
    slot_index = (flat_ids * capacity + slot_rank).reshape(tok_rows, top_count)
    slot_table = jnp.any(
        slot_index[None, :, :] == jnp.arange(experts * capacity, dtype=jnp.int32)[:, None, None],
        axis=2,
    ).astype(jnp.bfloat16)
    outgoing = jnp.dot(slot_table, tokens, preferred_element_type=jnp.float32).astype(jnp.bfloat16)
    outgoing = outgoing.reshape(devices, capacity // 2, width)
    partner = partner_2((w_gate, w_up, w_down), "local", 0)
    full_gate = jnp.concatenate([w_gate, partner[0]], axis=1)
    full_up = jnp.concatenate([w_up, partner[1]], axis=1)
    full_down = jnp.concatenate([w_down, partner[2]], axis=0)
    block = lax.all_to_all(outgoing, ("node", "local"), split_axis=0, concat_axis=0, tiled=True)
    rows = block.reshape(-1, width)
    gate = jnp.dot(rows, full_gate, preferred_element_type=jnp.float32)
    upper = jnp.dot(rows, full_up, preferred_element_type=jnp.float32)
    hidden = (jax.nn.silu(gate) * upper).astype(jnp.bfloat16)
    result = jnp.dot(hidden, full_down, preferred_element_type=jnp.float32).astype(jnp.bfloat16)
    processed = result.reshape(block.shape)
    returned = lax.all_to_all(processed, ("node", "local"), split_axis=0, concat_axis=0, tiled=True)
    results = returned.reshape(experts * capacity, width)
    chosen = results[slot_index]
    mixed = jnp.sum(gate_weights[:, :, None] * chosen.astype(jnp.float32), axis=1)
    return mixed.astype(jnp.bfloat16)


LANES = 128


def layer_kernel(
    nodes, columns, capacity, extra,
    rows_ref, ids_ref, weights_ref, gate_ref, up_ref, down_ref, out_ref,
    ids, weights, tables, shares, picks, spreads,
    first, second, dense, halves, packed, outs, passes, acts, hidden,
    results, relays, compacts, relayed, sums, totals, finals, output,
    edges, edge_picks, edge_spreads, dealt, gathered, merged, passed_edges, blended, edge_sums,
    load_sem, swap_send, swap_recv, line_recv, list_send, list_recv, half_recv, note_recv, pack_recv, pass_recv,
    far_recv, near_recv, sum_recv, end_recv, edge_recv, deal_recv, ship_recv, merge_recv, sent, ready,
):
    part, node, local = lax.axis_index("parts"), lax.axis_index("node"), lax.axis_index("local")
    column, core = local // 2, lax.rem(local, 2)
    high, low = node // 2, lax.rem(node, 2)
    count, width = rows_ref.shape
    hidden_half = gate_ref.shape[1]
    body_width = width - extra
    split = body_width // 2
    slots = 4
    bf16, f32 = jnp.bfloat16, jnp.float32
    inner = (column == 1) | (column == 2)

    def at(node_index, local_index):
        return (part, node_index, local_index)

    sides = (at(high * 2 + 1 - low, local), at((1 - high) * 2 + low, local))
    side_nodes = (high * 2 + 1 - low, (1 - high) * 2 + low)
    twin = at(node, column * 2 + 1 - core)
    low_flip = column + 1 - 2 * lax.rem(column, 2)
    beside = at(node, low_flip * 2 + core)
    across = at(node, (columns - 1 - column) * 2 + core)
    apart = at(node, (columns - 1 - low_flip) * 2 + core)
    later = jnp.where(inner, 2, 3)

    barrier = pltpu.get_barrier_semaphore()
    greeted = (*sides, twin, beside)
    for peer in greeted:
        pl.semaphore_signal(barrier, inc=1, device_id=peer, device_id_type=MESH)

    @pl.when(inner)
    def _():
        pl.semaphore_signal(barrier, inc=1, device_id=across, device_id_type=MESH)
        pl.semaphore_wait(barrier, len(greeted) + 1)
        pl.semaphore_signal(ready.at[0], inc=1, device_id=beside, device_id_type=MESH)
        pl.semaphore_signal(ready.at[1], inc=1, device_id=across, device_id_type=MESH)

    @pl.when(jnp.logical_not(inner))
    def _():
        pl.semaphore_wait(barrier, len(greeted))

    everything, inner_only = [], []

    def send(source, target, send_sem, recv_sem, peer):
        return pltpu.make_async_remote_copy(
            src_ref=source, dst_ref=target, send_sem=send_sem, recv_sem=recv_sem,
            device_id=peer, device_id_type=MESH,
        )

    def start(copy):
        copy.start()
        return copy

    def kept(copy):
        everything.append(copy)
        return start(copy)

    def columns_of(side):
        return pl.ds(side * split, split)

    def own(slot):
        return pl.ds(slot * capacity, capacity)

    body = pl.ds(0, body_width)
    edge = pl.ds(body_width, extra)
    edge_half = (pl.ds(0, extra // 2), pl.ds(extra // 2, extra // 2))

    half_in = {}
    line_in = {}
    list_in = {}
    note_in = {}
    pack_in = {}
    pass_in = {}

    def send_halves(step, source):
        for side in (0, 1):
            half_in[step, side] = start(send(source.at[:, columns_of(side)], halves.at[step, side], sent.at[SENT["half"]], half_recv.at[step, side], sides[side]))

    edge_in = {}
    for side in (0, 1):
        edge_in[side] = start(send(rows_ref.at[:, edge], edges.at[1 + side], sent.at[SENT["edge"]], edge_recv.at[side], sides[side]))
    send_halves(0, rows_ref)
    line_in[1] = start(send(rows_ref.at[:, body], dense.at[1], sent.at[SENT["line"]], line_recv.at[1], beside))
    to_across = send(rows_ref.at[:, body], dense.at[2], sent.at[SENT["line"]], line_recv.at[2], across)
    pass_across = send(dense.at[1], dense.at[3], sent.at[SENT["line"]], line_recv.at[3], across)
    pass_beside = (
        send(dense.at[2], dense.at[2], sent.at[SENT["line"]], line_recv.at[2], beside),
        send(dense.at[3], dense.at[3], sent.at[SENT["line"]], line_recv.at[3], beside),
    )
    line_in[2], line_in[3] = to_across, pass_across

    @pl.when(inner)
    def _():
        to_across.start()

    first_loads = [
        pltpu.make_async_copy(ids_ref, ids, load_sem.at[0]),
        pltpu.make_async_copy(weights_ref, weights, load_sem.at[1]),
        pltpu.make_async_copy(rows_ref.at[:, body], dense.at[0], load_sem.at[2]),
        pltpu.make_async_copy(rows_ref.at[:, edge], edges.at[0], load_sem.at[6]),
    ]
    for copy in first_loads:
        copy.start()

    def spot(target, index, by_rows, other):
        place = pl.ds((index + other) * hidden_half, hidden_half)
        return target.at[place] if by_rows else target.at[:, place]

    near = ((gate_ref, first, 0, False), (up_ref, first, 1, False), (down_ref, second, 0, True))
    swaps, loads = [], []
    for number, (source, target, index, by_rows) in enumerate(near):
        swaps.append(kept(send(source, spot(target, index, by_rows, 1 if by_rows else 2), swap_send.at[number], swap_recv.at[number], twin)))
        loads.append(pltpu.make_async_copy(source, spot(target, index, by_rows, 0), load_sem.at[3 + number]))
        loads[-1].start()

    for copy in first_loads[:2]:
        copy.wait()
    experts = nodes * columns
    expert_iota = lax.broadcasted_iota(jnp.int32, (experts, count), 0)
    listed = jnp.full((experts, count), -1.0, f32)
    for choice in range(ids.shape[0]):
        listed = jnp.where(ids[pl.ds(choice, 1), :] == expert_iota, weights[pl.ds(choice, 1), :], listed)
    tables[0, 0] = jnp.full((experts, LANES), -1.0, f32)
    tables[0, 0, :, pl.ds(0, count)] = listed

    list_in[1] = kept(send(tables.at[0, 0], tables.at[1, 0], list_send.at[0], list_recv.at[1], beside))
    list_across = send(tables.at[0, 0], tables.at[2, 0], list_send.at[1], list_recv.at[2], across)
    list_on = (
        send(tables.at[1, 0], tables.at[3, 0], list_send.at[2], list_recv.at[3], across),
        send(tables.at[2, 0], tables.at[2, 0], list_send.at[3], list_recv.at[2], beside),
        send(tables.at[3, 0], tables.at[3, 0], list_send.at[4], list_recv.at[3], beside),
    )
    list_in[2], list_in[3] = list_across, list_on[0]

    @pl.when(inner)
    def _():
        list_across.start()

    def send_notes(step):
        for side in (0, 1):
            note_in[step, side] = start(send(tables.at[step, 0], tables.at[step, 1 + side], sent.at[SENT["note"]], note_recv.at[step, side], sides[side]))

    before = (lax.broadcasted_iota(jnp.int32, (LANES, LANES), 0) < lax.broadcasted_iota(jnp.int32, (LANES, LANES), 1)).astype(bf16)
    places = lax.broadcasted_iota(jnp.int32, (capacity, LANES), 0).astype(f32)
    mirror = (lax.broadcasted_iota(jnp.int32, (count, LANES), 0) == lax.broadcasted_iota(jnp.int32, (count, LANES), 1)).astype(bf16)
    mine = node * columns + column
    near_experts = tuple(side_node * columns + column for side_node in side_nodes)
    line_experts = (mine, node * columns + low_flip, node * columns + (columns - 1 - column), node * columns + (columns - 1 - low_flip))

    def prepare(step, slot, wanted):
        table = tables[step, slot]
        rank = jnp.dot((table >= 0).astype(bf16), before, preferred_element_type=f32)
        rank = jnp.where(table >= 0, rank, -1.0)
        rows_iota = lax.broadcasted_iota(jnp.int32, table.shape, 0)
        for expert, index in wanted:
            chosen = rows_iota == expert
            row = jnp.sum(jnp.where(chosen, rank, 0.0), axis=0, keepdims=True)
            pick = (places == row).astype(f32)
            if index is None or index[1]:
                value = jnp.sum(jnp.where(chosen, table, 0.0), axis=0, keepdims=True)
                share = jnp.sum(pick * value, axis=1, keepdims=True)
                shares[step, own(slot)] = jnp.broadcast_to(share, (capacity, LANES))
            if index is not None:
                picked = pick.astype(bf16)
                picks[step, index[0], pl.ds(index[2] * capacity, capacity)] = picked
                spreads[step, index[0], index[2]] = lax.dot_general(
                    mirror, picked, (((1,), (1,)), ((), ())), preferred_element_type=f32).astype(bf16)

    tile = split

    def compress(step, index, source, targets):
        wanted = picks[step, index][:, :count]

        def body(number, carry):
            place = pl.ds(pl.multiple_of(number * tile, tile), tile)
            made = jnp.dot(wanted, source[:, place], preferred_element_type=f32).astype(bf16)
            for which, target in enumerate(targets):
                target[:, place] = made[which * capacity:(which + 1) * capacity]
            return carry

        lax.fori_loop(0, split // tile, body, 0)

    passed = {}

    def pass_on(step):
        passed[step] = True

        @pl.when(inner)
        def _():
            line_in[step].wait_recv()
            (pass_across, *pass_beside)[step - 1].start()
            list_in[step].wait_recv()
            list_on[step - 1].start()
            if step == 1:
                pl.semaphore_wait(ready.at[1], 1)
                pl.semaphore_signal(ready.at[1], inc=1, device_id=beside, device_id_type=MESH)

    def issue(step):
        if step:
            @pl.when(jnp.logical_not(inner) | (step not in passed))
            def _():
                line_in[step].wait_recv()
                list_in[step].wait_recv()

            send_halves(step, dense.at[step])
        send_notes(step)
        prepare(step, 0, ((near_experts[1], (0, False, 0)), (mine, (0, True, 1)), (near_experts[0], (1, False, 0))))
        picks[step, 1, pl.ds(capacity, capacity)] = picks[step, 0, pl.ds(capacity, capacity)]
        if not step:
            first_loads[2].wait()
        for half, side in ((0, 1), (1, 0)):
            compress(step, half, dense.at[step, :, columns_of(half)], (outs.at[step, side], packed.at[step, own(0), columns_of(half)]))
            pack_in[step, side] = start(send(outs.at[step, side], packed.at[step, own(1 + side), columns_of(half)], sent.at[SENT["pack"]], pack_recv.at[step], sides[side]))

    def spread_edges(step):
        for side in (0, 1):
            edge_in[side].wait_recv()
            part = edge_half[side]
            edge_in[2 + side] = start(send(edges.at[1 + side, :, part], edges.at[3, :, part], sent.at[SENT["edge"]], edge_recv.at[2 + side], sides[1 - side]))

    line_peers = {
        True: {1: (beside, 1), 2: (across, 2), 3: (apart, 3)},
        False: {1: (beside, 1), 2: (apart, 3), 3: (across, 2)},
    }

    def deal(step):
        first_loads[3].wait()
        note_in[0, 2].wait_recv()

        @pl.when(jnp.logical_not(inner))
        def _():
            pl.semaphore_wait(ready.at[0], 1)
            pl.semaphore_wait(ready.at[1], 1)

        for slot in range(slots):
            table = tables[0, slot]
            rank = jnp.dot((table >= 0).astype(bf16), before, preferred_element_type=f32)
            rank = jnp.where(table >= 0, rank, -1.0)
            rows_iota = lax.broadcasted_iota(jnp.int32, table.shape, 0)
            for index, expert in enumerate(line_experts):
                row = jnp.sum(jnp.where(rows_iota == expert, rank, 0.0), axis=0, keepdims=True)
                edge_picks[slot, own(index)] = (places == row).astype(bf16)
            edge_spreads[slot] = lax.dot_general(
                mirror, edge_picks[slot], (((1,), (1,)), ((), ())), preferred_element_type=f32).astype(bf16)
        for side in (0, 1):
            edge_in[2 + side].wait_recv()
        for slot in range(slots):
            made = jnp.dot(edge_picks[slot][:, :count], edges[slot], preferred_element_type=f32).astype(bf16)
            packed[0, own(slot), edge] = made[:capacity]
            for index in (1, 2, 3):
                dealt[index - 1, own(slot)] = made[index * capacity:(index + 1) * capacity]

    def deal_out(step):
        for inside, chosen in ((True, inner), (False, jnp.logical_not(inner))):
            @pl.when(chosen)
            def _(inside=inside):
                dealing(step, inside).start()

    def dealing(step, inside):
        peer, index = line_peers[inside][step]
        target = 1 if step == 1 else later
        return send(dealt.at[index - 1], packed.at[target, :, edge], sent.at[SENT["deal"]], deal_recv.at[target], peer)

    def relay(step):
        for side in (0, 1):
            other = 1 - side
            note_in[step, side].wait_recv()
            if not side:
                note_in[step, 2] = start(send(tables.at[step, 1], tables.at[step, 3], sent.at[SENT["note"]], note_recv.at[step, 2], sides[1]))
            prepare(step, 1 + side, ((near_experts[other], (2 + side, False, 0)), (mine, (2 + side, True, 1))))
            half_in[step, side].wait_recv()
            compress(step, 2 + side, halves.at[step, side], (passes.at[step, side], packed.at[step, own(1 + side), columns_of(side)]))
            pass_in[step, side] = start(send(passes.at[step, side], packed.at[step, own(3), columns_of(side)], sent.at[SENT["pass"]], pass_recv.at[step], sides[other]))

    def compute(step):
        if step:
            note_in[step, 2].wait_recv()
        prepare(step, 3, ((mine, None),))
        pltpu.make_async_copy(outs.at[step], outs.at[step], pack_recv.at[step]).wait()
        pltpu.make_async_copy(passes.at[step], passes.at[step], pass_recv.at[step]).wait()
        if step:
            pltpu.make_async_remote_copy(
                src_ref=dealt.at[0], dst_ref=packed.at[step, :, edge], send_sem=sent.at[SENT["deal"]], recv_sem=deal_recv.at[step],
                device_id=beside, device_id_type=MESH,
            ).wait_recv()
        if not step:
            for copy in swaps:
                copy.wait_recv()
            for copy in loads:
                copy.wait()
        for part in (0, 1):
            place = pl.ds(part * 2 * hidden_half, 2 * hidden_half)
            acts[:, place] = jnp.dot(packed[step], first[:, place], preferred_element_type=f32)
        for other in (0, 1):
            gate = acts[:, pl.ds(2 * other * hidden_half, hidden_half)]
            upper = acts[:, pl.ds((2 * other + 1) * hidden_half, hidden_half)]
            hidden[:, pl.ds(other * hidden_half, hidden_half)] = (gate / (1.0 + jnp.exp(-gate)) * upper).astype(bf16)
        share = shares[step][:, :1]
        wide = width // 4 if step else body_width // 2

        def out_of(number, carry):
            place = pl.ds(pl.multiple_of(number * wide, wide), wide)
            made = jnp.dot(hidden[...], second[:, place], preferred_element_type=f32)
            results[step, :, place] = (made * share).astype(bf16)
            return carry

        lax.fori_loop(0, body_width // wide if not step else width // wide, out_of, 0)
        if not step:
            made = (jnp.dot(hidden[...], second[:, edge], preferred_element_type=f32) * share).astype(bf16)
            for slot in range(slots):
                gathered[slot, pl.ds(0, capacity)] = made[slot * capacity:(slot + 1) * capacity]

    def shipment(step, slot, inside):
        peer, index = line_peers[inside][step]
        return send(results.at[step, own(slot), edge], gathered.at[slot, own(index)], sent.at[SENT["ship"]], ship_recv.at[slot], peer)

    def ship(step):
        for inside, chosen in ((True, inner), (False, jnp.logical_not(inner))):
            @pl.when(chosen)
            def _(inside=inside):
                for slot in range(slots):
                    shipment(step, slot, inside).start()

    def gather_edges(slot):
        others = gathered.at[slot, pl.ds(capacity, (columns - 1) * capacity)]
        pltpu.make_async_copy(others, others, ship_recv.at[slot]).wait()
        return jnp.dot(edge_spreads[slot], gathered[slot], preferred_element_type=f32)

    merge_in = {}

    def merge(step):
        merged[2] = gather_edges(3).astype(bf16)
        for side in (0, 1):
            merge_in["far", side] = start(send(merged.at[2, :, edge_half[side]], passed_edges.at[side], sent.at[SENT["merge"]], merge_recv.at[0, side], sides[side]))
        for side in (0, 1):
            merged[side] = gather_edges(1 + side).astype(bf16)
            part = edge_half[side]
            merge_in["near", side] = start(send(merged.at[side, :, part], edge_sums.at[side, :, part], sent.at[SENT["merge"]], merge_recv.at[1, side], sides[side]))

    def blend(step):
        for side in (0, 1):
            other = 1 - side
            part = edge_half[side]
            merge_in["far", side].wait_recv()
            blended[other] = (merged[other, :, part].astype(f32) + passed_edges[side].astype(f32)).astype(bf16)
            merge_in["sum", other] = start(send(blended.at[other], edge_sums.at[other, :, part], sent.at[SENT["merge"]], merge_recv.at[2, other], sides[other]))

    def finish(step):
        made = gather_edges(0)
        for side in (0, 1):
            merge_in["near", side].wait_recv()
            merge_in["sum", side].wait_recv()
            made += edge_sums[side].astype(f32)
        output[:, edge] = made.astype(bf16)
        hand_out(0, edge).start()

    far_in, near_in, sum_in = {}, {}, {}

    def hand_far(step):
        for side in (0, 1):
            far_in[step, side] = start(send(results.at[step, own(3), columns_of(side)], relays.at[step, side], sent.at[SENT["far"]], far_recv.at[step, side], sides[side]))

    def hand_near(step):
        for side in (0, 1):
            near_in[step, side] = start(send(results.at[step, own(1 + side), columns_of(side)], compacts.at[step, side], sent.at[SENT["near"]], near_recv.at[step, side], sides[side]))

    def combine(step):
        for side in (0, 1):
            other = 1 - side
            far_in[step, side].wait_recv()
            theirs = spreads[step, 2 + other, 0]
            ours = spreads[step, 2 + other, 1]

            def body(number, carry, side=side, other=other, theirs=theirs, ours=ours):
                place = pl.ds(pl.multiple_of(number * tile, tile), tile)
                shifted = pl.ds(pl.multiple_of(side * split + number * tile, tile), tile)
                made = jnp.dot(theirs, relays[step, side, :, place], preferred_element_type=f32)
                made += jnp.dot(ours, results[step, own(1 + other), shifted], preferred_element_type=f32)
                relayed[step, other, :, place] = made.astype(bf16)
                return carry

            lax.fori_loop(0, split // tile, body, 0)
            sum_in[step, other] = start(send(relayed.at[step, other], sums.at[step, other], sent.at[SENT["sum"]], sum_recv.at[step, other], sides[other]))

    FAR_SUM, BACK_SUM, LAST_SUM, BESIDE_SUM, ACROSS_SUM = range(5)
    routes = {
        True: {1: (beside, BESIDE_SUM), 2: (across, ACROSS_SUM), 3: (across, BACK_SUM)},
        False: {1: (beside, BESIDE_SUM), 2: (beside, LAST_SUM), 3: (beside, FAR_SUM)},
    }
    added = {
        True: {3: (FAR_SUM,), 2: (LAST_SUM,), 1: (BACK_SUM,), 0: (BESIDE_SUM, ACROSS_SUM)},
        False: {3: (), 2: (), 1: (), 0: (BESIDE_SUM,)},
    }

    cut = (split // LANES + 1) // 2 * LANES
    parts = ((0, cut), (cut, split - cut))

    def give(step, side, part, inside):
        peer, inbox = routes[inside][step]
        place = pl.ds(side * split + parts[part][0], parts[part][1])
        return send(
            totals.at[step - 1, :, place], finals.at[inbox, :, place], sent.at[SENT["end"]], end_recv.at[inbox, side, part], peer)

    def given(inbox, side, part):
        place = pl.ds(side * split + parts[part][0], parts[part][1])
        return send(
            totals.at[0, :, place], finals.at[inbox, :, place], sent.at[SENT["end"]], end_recv.at[inbox, side, part], beside)

    def hand_out(number, place):
        return pltpu.make_async_copy(output.at[:, place], out_ref.at[:, place], load_sem.at[number])

    def collect(step):
        for side in (0, 1):
            other = 1 - side
            near_in[step, side].wait_recv()
            sum_in[step, other].wait_recv()

            def total(inside, side=side, other=other):
                for part, (base, size) in enumerate(parts):
                    for inbox in added[inside][step]:
                        given(inbox, side, part).wait_recv()
                    place = pl.ds(base, size)
                    shifted = pl.ds(side * split + base, size)
                    made = jnp.dot(spreads[step, other, 0], compacts[step, side, :, place], preferred_element_type=f32)
                    made += jnp.dot(spreads[step, 0, 1], results[step, own(0), shifted], preferred_element_type=f32)
                    made += sums[step, other, :, place].astype(f32)
                    for inbox in added[inside][step]:
                        made += finals[inbox, :, shifted].astype(f32)
                    target = totals.at[step - 1] if step else output
                    target[:, shifted] = made.astype(bf16)
                    if step:
                        give(step, side, part, inside).start()
                    else:
                        hand_out(1 + 2 * side + part, shifted).start()

            @pl.when(inner)
            def _(total=total):
                total(True)

            @pl.when(jnp.logical_not(inner))
            def _(total=total):
                total(False)

    table = {
        "pass": pass_on, "issue": issue, "relay": relay, "compute": compute, "far": hand_far, "near": hand_near,
        "combine": combine, "collect": collect, "spread": spread_edges, "deal": deal, "dsend": deal_out, "ship": ship, "merge": merge,
        "blend": blend, "finish": finish,
    }
    def settle(name, held):
        pltpu.make_async_copy(held, held, sent.at[SENT[name]]).wait()

    for word in ORDER:
        if word == ORDER[-1]:
            for copy in everything:
                copy.wait_send()
            settle("half", halves)
            settle("note", tables.at[:, pl.ds(1, slots - 1)])
            settle("pack", outs)
            settle("pass", passes)
            settle("far", relays)
            settle("deal", dealt)
            settle("ship", gathered.at[:, pl.ds(capacity, (columns - 1) * capacity)])
            settle("edge", merged)

            @pl.when(inner)
            def _():
                settle("line", finals)
                for copy in (list_across, *list_on):
                    copy.wait_send()

            @pl.when(jnp.logical_not(inner))
            def _():
                settle("line", dense.at[1])
        table[word[:-1]](int(word[-1]))

    settle("near", compacts)
    settle("sum", sums)
    settle("end", totals)
    settle("merge", merged)
    hand_out(0, edge).wait()
    for side in (0, 1):
        for part, (base, size) in enumerate(parts):
            hand_out(1 + 2 * side + part, pl.ds(side * split + base, size)).wait()


NAMES = ("half", "note", "pack", "pass", "far", "near", "sum", "end", "edge", "deal", "ship", "merge", "line")
SENT = {name: number for number, name in enumerate(NAMES)}

ORDER = (
    "spread0", "issue0", "relay0", "pass2", "pass1", "deal0",
    "issue1", "compute0", "relay1", "issue2", "dsend2", "pass3",
    "relay2", "issue3", "dsend1", "dsend3", "relay3", "compute2",
    "far2", "ship2", "near2", "compute3", "far3", "ship3",
    "combine2", "compute1", "ship1", "far1", "near3", "combine3",
    "near1", "far0", "collect2", "combine1", "merge0", "near0",
    "collect3", "combine0", "collect1", "blend0", "collect0", "finish0",
)


def by_rows(tokens, expert_ids, gate_weights, w_gate, w_up, w_down):
    nodes, columns = lax.axis_size("node"), lax.axis_size("local") // 2
    experts = nodes * columns
    count, width = tokens.shape
    choices = expert_ids.shape[1]
    capacity = capacity_of(count, choices, experts)
    hidden_half = w_gate.shape[1]
    extra = width * 3 // 16
    body_width = width - extra
    split = body_width // 2
    dma = pltpu.SemaphoreType.DMA
    bf16, f32 = jnp.bfloat16, jnp.float32
    scratch = [
        pltpu.VMEM((choices, count), jnp.int32),
        pltpu.VMEM((choices, count), f32),
        pltpu.VMEM((columns, 4, experts, LANES), f32),
        pltpu.VMEM((columns, 4 * capacity, LANES), f32),
        pltpu.VMEM((columns, 4, 2 * capacity, LANES), bf16),
        pltpu.VMEM((columns, 4, 2, count, capacity), bf16),
        pltpu.VMEM((width, 4 * hidden_half), bf16),
        pltpu.VMEM((2 * hidden_half, width), bf16),
        pltpu.VMEM((columns, count, body_width), bf16),
        pltpu.VMEM((columns, 2, count, split), bf16),
        pltpu.VMEM((columns, 4 * capacity, width), bf16),
        pltpu.VMEM((columns, 2, capacity, split), bf16),
        pltpu.VMEM((columns, 2, capacity, split), bf16),
        pltpu.VMEM((4 * capacity, 4 * hidden_half), f32),
        pltpu.VMEM((4 * capacity, 2 * hidden_half), bf16),
        pltpu.VMEM((columns, 4 * capacity, width), bf16),
        pltpu.VMEM((columns, 2, capacity, split), bf16),
        pltpu.VMEM((columns, 2, capacity, split), bf16),
        pltpu.VMEM((columns, 2, count, split), bf16),
        pltpu.VMEM((columns, 2, count, split), bf16),
        pltpu.VMEM((columns - 1, count, body_width), bf16),
        pltpu.VMEM((5, count, body_width), bf16),
        pltpu.VMEM((count, width), bf16),
        pltpu.VMEM((4, count, extra), bf16),
        pltpu.VMEM((4, columns * capacity, LANES), bf16),
        pltpu.VMEM((4, count, columns * capacity), bf16),
        pltpu.VMEM((columns - 1, 4 * capacity, extra), bf16),
        pltpu.VMEM((4, columns * capacity, extra), bf16),
        pltpu.VMEM((3, count, extra), bf16),
        pltpu.VMEM((2, count, extra // 2), bf16),
        pltpu.VMEM((2, count, extra // 2), bf16),
        pltpu.VMEM((2, count, extra), bf16),
        dma((7,)), dma((3,)), dma((3,)), dma((columns,)), dma((5,)), dma((columns,)),
        dma((columns, 2)), dma((columns, 3)), dma((columns,)), dma((columns,)),
        dma((columns, 2)), dma((columns, 2)), dma((columns, 2)), dma((5, 2, 2)),
        dma((4,)), dma((columns,)), dma((4,)), dma((3, 2)),
        dma((len(SENT),)), pltpu.SemaphoreType.REGULAR((2,)),
    ]
    flops = 12 * experts * count * width * hidden_half
    return pl.pallas_call(
        functools.partial(layer_kernel, nodes, columns, capacity, extra),
        name="moe_layer",
        out_shape=pltpu.VMEM((count, width), bf16),
        in_specs=[pl.BlockSpec(memory_space=pl.ANY)] * 6,
        out_specs=pl.BlockSpec(memory_space=pl.ANY),
        scratch_shapes=scratch,
        cost_estimate=pl.CostEstimate(flops=flops, bytes_accessed=w_gate.size * 12, transcendentals=0),
        compiler_params=pltpu.CompilerParams(collective_id=0, has_side_effects=True, vmem_limit_bytes=56 << 20),
    )(tokens, expert_ids.T, gate_weights.T, w_gate, w_up, w_down)


def capacity_of(rows, choices, experts):
    return rows * choices * 5 // (4 * experts)


def per_device(tokens, expert_ids, *rest):
    nodes, columns = lax.axis_size("node"), lax.axis_size("local") // 2
    count = tokens.shape[0]
    capacity = capacity_of(count, expert_ids.shape[1], nodes * columns)
    if nodes == 4 and columns == 4 and count <= LANES and capacity % 8 == 0:
        return by_rows(tokens, expert_ids, *rest)
    return by_slots(tokens, expert_ids, *rest)


def solution(mesh):
    placed = (
        P(("parts", "node", "local"), None),
        P(("parts", "node", "local"), None),
        P(("parts", "node", "local"), None),
        P(None, ("parts", "node", "local")),
        P(None, ("parts", "node", "local")),
        P(("parts", "node", "local"), None),
    )
    return jax.shard_map(
        per_device,
        mesh=mesh,
        in_specs=placed,
        out_specs=P(("parts", "node", "local"), None),
        check_vma=False,
    )
```

```python
import functools

import jax
import jax.numpy as jnp
from jax import lax
from jax.experimental import pallas as pl
from jax.experimental.pallas import tpu as pltpu
from jax.sharding import PartitionSpec as P

MESH = pl.DeviceIdType.MESH


def partner_2(value, axis, bit):
    mask = 2**bit
    pairs = [(source, source ^ mask) for source in range(lax.axis_size(axis))]
    return lax.ppermute(value, axis, pairs)


def by_slots(tokens, expert_ids, gate_weights, w_gate, w_up, w_down):
    node_count = lax.axis_size("node")
    local_count = lax.axis_size("local")
    devices = node_count * local_count
    experts = devices // 2
    tok_rows, top_count = expert_ids.shape
    width = tokens.shape[1]
    capacity = tok_rows * top_count * 5 // (4 * experts)
    flat_ids = expert_ids.reshape(-1)
    one_hot = (flat_ids[:, None] == jnp.arange(experts, dtype=jnp.int32)[None, :]).astype(jnp.int32)
    earlier = jnp.cumsum(one_hot, axis=0) - one_hot
    slot_rank = jnp.sum(earlier * one_hot, axis=1)
    slot_index = (flat_ids * capacity + slot_rank).reshape(tok_rows, top_count)
    slot_table = jnp.any(
        slot_index[None, :, :] == jnp.arange(experts * capacity, dtype=jnp.int32)[:, None, None],
        axis=2,
    ).astype(jnp.bfloat16)
    outgoing = jnp.dot(slot_table, tokens, preferred_element_type=jnp.float32).astype(jnp.bfloat16)
    outgoing = outgoing.reshape(devices, capacity // 2, width)
    partner = partner_2((w_gate, w_up, w_down), "local", 0)
    full_gate = jnp.concatenate([w_gate, partner[0]], axis=1)
    full_up = jnp.concatenate([w_up, partner[1]], axis=1)
    full_down = jnp.concatenate([w_down, partner[2]], axis=0)
    block = lax.all_to_all(outgoing, ("node", "local"), split_axis=0, concat_axis=0, tiled=True)
    rows = block.reshape(-1, width)
    gate = jnp.dot(rows, full_gate, preferred_element_type=jnp.float32)
    upper = jnp.dot(rows, full_up, preferred_element_type=jnp.float32)
    hidden = (jax.nn.silu(gate) * upper).astype(jnp.bfloat16)
    result = jnp.dot(hidden, full_down, preferred_element_type=jnp.float32).astype(jnp.bfloat16)
    processed = result.reshape(block.shape)
    returned = lax.all_to_all(processed, ("node", "local"), split_axis=0, concat_axis=0, tiled=True)
    results = returned.reshape(experts * capacity, width)
    chosen = results[slot_index]
    mixed = jnp.sum(gate_weights[:, :, None] * chosen.astype(jnp.float32), axis=1)
    return mixed.astype(jnp.bfloat16)


LANES = 128


def layer_kernel(
    nodes, columns, capacity, extra,
    rows_ref, ids_ref, weights_ref, gate_ref, up_ref, down_ref, out_ref,
    ids, weights, tables, shares, picks, spreads,
    first, second, dense, halves, packed, outs, passes, acts, hidden,
    results, relays, compacts, relayed, sums, totals, finals, output,
    edges, edge_picks, edge_spreads, dealt, gathered, merged, passed_edges, blended, edge_sums,
    load_sem, swap_send, swap_recv, line_recv, list_send, list_recv, half_recv, note_recv, pack_recv, pass_recv,
    far_recv, near_recv, sum_recv, end_recv, edge_recv, deal_recv, ship_recv, merge_recv, sent, ready,
):
    part, node, local = lax.axis_index("parts"), lax.axis_index("node"), lax.axis_index("local")
    column, core = local // 2, lax.rem(local, 2)
    high, low = node // 2, lax.rem(node, 2)
    count, width = rows_ref.shape
    hidden_half = gate_ref.shape[1]
    body_width = width - extra
    split = body_width // 2
    slots = 4
    bf16, f32 = jnp.bfloat16, jnp.float32
    inner = (column == 1) | (column == 2)

    def at(node_index, local_index):
        return (part, node_index, local_index)

    sides = (at(high * 2 + 1 - low, local), at((1 - high) * 2 + low, local))
    side_nodes = (high * 2 + 1 - low, (1 - high) * 2 + low)
    twin = at(node, column * 2 + 1 - core)
    low_flip = column + 1 - 2 * lax.rem(column, 2)
    beside = at(node, low_flip * 2 + core)
    across = at(node, (columns - 1 - column) * 2 + core)
    apart = at(node, (columns - 1 - low_flip) * 2 + core)
    later = jnp.where(inner, 2, 3)

    barrier = pltpu.get_barrier_semaphore()
    greeted = (*sides, twin, beside)
    for peer in greeted:
        pl.semaphore_signal(barrier, inc=1, device_id=peer, device_id_type=MESH)

    @pl.when(inner)
    def _():
        pl.semaphore_signal(barrier, inc=1, device_id=across, device_id_type=MESH)
        pl.semaphore_wait(barrier, len(greeted) + 1)
        pl.semaphore_signal(ready.at[0], inc=1, device_id=beside, device_id_type=MESH)
        pl.semaphore_signal(ready.at[1], inc=1, device_id=across, device_id_type=MESH)

    @pl.when(jnp.logical_not(inner))
    def _():
        pl.semaphore_wait(barrier, len(greeted))

    everything, inner_only = [], []

    def send(source, target, send_sem, recv_sem, peer):
        return pltpu.make_async_remote_copy(
            src_ref=source, dst_ref=target, send_sem=send_sem, recv_sem=recv_sem,
            device_id=peer, device_id_type=MESH,
        )

    def start(copy):
        copy.start()
        return copy

    def kept(copy):
        everything.append(copy)
        return start(copy)

    def columns_of(side):
        return pl.ds(side * split, split)

    def own(slot):
        return pl.ds(slot * capacity, capacity)

    body = pl.ds(0, body_width)
    edge = pl.ds(body_width, extra)
    edge_half = (pl.ds(0, extra // 2), pl.ds(extra // 2, extra // 2))

    half_in = {}
    line_in = {}
    list_in = {}
    note_in = {}
    pack_in = {}
    pass_in = {}

    def send_halves(step, source):
        for side in (0, 1):
            half_in[step, side] = start(send(source.at[:, columns_of(side)], halves.at[step, side], sent.at[SENT["half"]], half_recv.at[step, side], sides[side]))

    edge_in = {}
    for side in (0, 1):
        edge_in[side] = start(send(rows_ref.at[:, edge], edges.at[1 + side], sent.at[SENT["edge"]], edge_recv.at[side], sides[side]))
    send_halves(0, rows_ref)
    line_in[1] = start(send(rows_ref.at[:, body], dense.at[1], sent.at[SENT["line"]], line_recv.at[1], beside))
    to_across = send(rows_ref.at[:, body], dense.at[2], sent.at[SENT["line"]], line_recv.at[2], across)
    pass_across = send(dense.at[1], dense.at[3], sent.at[SENT["line"]], line_recv.at[3], across)
    pass_beside = (
        send(dense.at[2], dense.at[2], sent.at[SENT["line"]], line_recv.at[2], beside),
        send(dense.at[3], dense.at[3], sent.at[SENT["line"]], line_recv.at[3], beside),
    )
    line_in[2], line_in[3] = to_across, pass_across

    @pl.when(inner)
    def _():
        to_across.start()

    first_loads = [
        pltpu.make_async_copy(ids_ref, ids, load_sem.at[0]),
        pltpu.make_async_copy(weights_ref, weights, load_sem.at[1]),
        pltpu.make_async_copy(rows_ref.at[:, body], dense.at[0], load_sem.at[2]),
        pltpu.make_async_copy(rows_ref.at[:, edge], edges.at[0], load_sem.at[6]),
    ]
    for copy in first_loads:
        copy.start()

    def spot(target, index, by_rows, other):
        place = pl.ds((index + other) * hidden_half, hidden_half)
        return target.at[place] if by_rows else target.at[:, place]

    near = ((gate_ref, first, 0, False), (up_ref, first, 1, False), (down_ref, second, 0, True))
    swaps, loads = [], []
    for number, (source, target, index, by_rows) in enumerate(near):
        swaps.append(kept(send(source, spot(target, index, by_rows, 1 if by_rows else 2), swap_send.at[number], swap_recv.at[number], twin)))
        loads.append(pltpu.make_async_copy(source, spot(target, index, by_rows, 0), load_sem.at[3 + number]))
        loads[-1].start()

    for copy in first_loads[:2]:
        copy.wait()
    experts = nodes * columns
    expert_iota = lax.broadcasted_iota(jnp.int32, (experts, count), 0)
    listed = jnp.full((experts, count), -1.0, f32)
    for choice in range(ids.shape[0]):
        listed = jnp.where(ids[pl.ds(choice, 1), :] == expert_iota, weights[pl.ds(choice, 1), :], listed)
    tables[0, 0] = jnp.full((experts, LANES), -1.0, f32)
    tables[0, 0, :, pl.ds(0, count)] = listed

    list_in[1] = kept(send(tables.at[0, 0], tables.at[1, 0], list_send.at[0], list_recv.at[1], beside))
    list_across = send(tables.at[0, 0], tables.at[2, 0], list_send.at[1], list_recv.at[2], across)
    list_on = (
        send(tables.at[1, 0], tables.at[3, 0], list_send.at[2], list_recv.at[3], across),
        send(tables.at[2, 0], tables.at[2, 0], list_send.at[3], list_recv.at[2], beside),
        send(tables.at[3, 0], tables.at[3, 0], list_send.at[4], list_recv.at[3], beside),
    )
    list_in[2], list_in[3] = list_across, list_on[0]

    @pl.when(inner)
    def _():
        list_across.start()

    def send_notes(step):
        for side in (0, 1):
            note_in[step, side] = start(send(tables.at[step, 0], tables.at[step, 1 + side], sent.at[SENT["note"]], note_recv.at[step, side], sides[side]))

    before = (lax.broadcasted_iota(jnp.int32, (LANES, LANES), 0) < lax.broadcasted_iota(jnp.int32, (LANES, LANES), 1)).astype(bf16)
    places = lax.broadcasted_iota(jnp.int32, (capacity, LANES), 0).astype(f32)
    mirror = (lax.broadcasted_iota(jnp.int32, (count, LANES), 0) == lax.broadcasted_iota(jnp.int32, (count, LANES), 1)).astype(bf16)
    mine = node * columns + column
    near_experts = tuple(side_node * columns + column for side_node in side_nodes)
    line_experts = (mine, node * columns + low_flip, node * columns + (columns - 1 - column), node * columns + (columns - 1 - low_flip))

    def prepare(step, slot, wanted):
        table = tables[step, slot]
        rank = jnp.dot((table >= 0).astype(bf16), before, preferred_element_type=f32)
        rank = jnp.where(table >= 0, rank, -1.0)
        rows_iota = lax.broadcasted_iota(jnp.int32, table.shape, 0)
        for expert, index in wanted:
            chosen = rows_iota == expert
            row = jnp.sum(jnp.where(chosen, rank, 0.0), axis=0, keepdims=True)
            pick = (places == row).astype(f32)
            if index is None or index[1]:
                value = jnp.sum(jnp.where(chosen, table, 0.0), axis=0, keepdims=True)
                share = jnp.sum(pick * value, axis=1, keepdims=True)
                shares[step, own(slot)] = jnp.broadcast_to(share, (capacity, LANES))
            if index is not None:
                picked = pick.astype(bf16)
                picks[step, index[0], pl.ds(index[2] * capacity, capacity)] = picked
                spreads[step, index[0], index[2]] = lax.dot_general(
                    mirror, picked, (((1,), (1,)), ((), ())), preferred_element_type=f32).astype(bf16)

    tile = split

    def compress(step, index, source, targets):
        wanted = picks[step, index][:, :count]

        def body(number, carry):
            place = pl.ds(pl.multiple_of(number * tile, tile), tile)
            made = jnp.dot(wanted, source[:, place], preferred_element_type=f32).astype(bf16)
            for which, target in enumerate(targets):
                target[:, place] = made[which * capacity:(which + 1) * capacity]
            return carry

        lax.fori_loop(0, split // tile, body, 0)

    passed = {}

    def pass_on(step):
        passed[step] = True

        @pl.when(inner)
        def _():
            line_in[step].wait_recv()
            (pass_across, *pass_beside)[step - 1].start()
            list_in[step].wait_recv()
            list_on[step - 1].start()
            if step == 1:
                pl.semaphore_wait(ready.at[1], 1)
                pl.semaphore_signal(ready.at[1], inc=1, device_id=beside, device_id_type=MESH)

    def issue(step):
        if step:
            @pl.when(jnp.logical_not(inner) | (step not in passed))
            def _():
                line_in[step].wait_recv()
                list_in[step].wait_recv()

            send_halves(step, dense.at[step])
        send_notes(step)
        prepare(step, 0, ((near_experts[1], (0, False, 0)), (mine, (0, True, 1)), (near_experts[0], (1, False, 0))))
        picks[step, 1, pl.ds(capacity, capacity)] = picks[step, 0, pl.ds(capacity, capacity)]
        if not step:
            first_loads[2].wait()
        for half, side in ((0, 1), (1, 0)):
            compress(step, half, dense.at[step, :, columns_of(half)], (outs.at[step, side], packed.at[step, own(0), columns_of(half)]))
            pack_in[step, side] = start(send(outs.at[step, side], packed.at[step, own(1 + side), columns_of(half)], sent.at[SENT["pack"]], pack_recv.at[step], sides[side]))

    def spread_edges(step):
        for side in (0, 1):
            edge_in[side].wait_recv()
            part = edge_half[side]
            edge_in[2 + side] = start(send(edges.at[1 + side, :, part], edges.at[3, :, part], sent.at[SENT["edge"]], edge_recv.at[2 + side], sides[1 - side]))

    line_peers = {
        True: {1: (beside, 1), 2: (across, 2), 3: (apart, 3)},
        False: {1: (beside, 1), 2: (apart, 3), 3: (across, 2)},
    }

    def deal(step):
        first_loads[3].wait()
        note_in[0, 2].wait_recv()

        @pl.when(jnp.logical_not(inner))
        def _():
            pl.semaphore_wait(ready.at[0], 1)
            pl.semaphore_wait(ready.at[1], 1)

        for slot in range(slots):
            table = tables[0, slot]
            rank = jnp.dot((table >= 0).astype(bf16), before, preferred_element_type=f32)
            rank = jnp.where(table >= 0, rank, -1.0)
            rows_iota = lax.broadcasted_iota(jnp.int32, table.shape, 0)
            for index, expert in enumerate(line_experts):
                row = jnp.sum(jnp.where(rows_iota == expert, rank, 0.0), axis=0, keepdims=True)
                edge_picks[slot, own(index)] = (places == row).astype(bf16)
            edge_spreads[slot] = lax.dot_general(
                mirror, edge_picks[slot], (((1,), (1,)), ((), ())), preferred_element_type=f32).astype(bf16)
        for side in (0, 1):
            edge_in[2 + side].wait_recv()
        for slot in range(slots):
            made = jnp.dot(edge_picks[slot][:, :count], edges[slot], preferred_element_type=f32).astype(bf16)
            packed[0, own(slot), edge] = made[:capacity]
            for index in (1, 2, 3):
                dealt[index - 1, own(slot)] = made[index * capacity:(index + 1) * capacity]

    def deal_out(step):
        for inside, chosen in ((True, inner), (False, jnp.logical_not(inner))):
            @pl.when(chosen)
            def _(inside=inside):
                dealing(step, inside).start()

    def dealing(step, inside):
        peer, index = line_peers[inside][step]
        target = 1 if step == 1 else later
        return send(dealt.at[index - 1], packed.at[target, :, edge], sent.at[SENT["deal"]], deal_recv.at[target], peer)

    def relay(step):
        for side in (0, 1):
            other = 1 - side
            note_in[step, side].wait_recv()
            if not side:
                note_in[step, 2] = start(send(tables.at[step, 1], tables.at[step, 3], sent.at[SENT["note"]], note_recv.at[step, 2], sides[1]))
            prepare(step, 1 + side, ((near_experts[other], (2 + side, False, 0)), (mine, (2 + side, True, 1))))
            half_in[step, side].wait_recv()
            compress(step, 2 + side, halves.at[step, side], (passes.at[step, side], packed.at[step, own(1 + side), columns_of(side)]))
            pass_in[step, side] = start(send(passes.at[step, side], packed.at[step, own(3), columns_of(side)], sent.at[SENT["pass"]], pass_recv.at[step], sides[other]))

    def compute(step):
        if step:
            note_in[step, 2].wait_recv()
        prepare(step, 3, ((mine, None),))
        pltpu.make_async_copy(outs.at[step], outs.at[step], pack_recv.at[step]).wait()
        pltpu.make_async_copy(passes.at[step], passes.at[step], pass_recv.at[step]).wait()
        if step:
            pltpu.make_async_remote_copy(
                src_ref=dealt.at[0], dst_ref=packed.at[step, :, edge], send_sem=sent.at[SENT["deal"]], recv_sem=deal_recv.at[step],
                device_id=beside, device_id_type=MESH,
            ).wait_recv()
        if not step:
            for copy in swaps:
                copy.wait_recv()
            for copy in loads:
                copy.wait()
        for part in (0, 1):
            place = pl.ds(part * 2 * hidden_half, 2 * hidden_half)
            acts[:, place] = jnp.dot(packed[step], first[:, place], preferred_element_type=f32)
        for other in (0, 1):
            gate = acts[:, pl.ds(2 * other * hidden_half, hidden_half)]
            upper = acts[:, pl.ds((2 * other + 1) * hidden_half, hidden_half)]
            hidden[:, pl.ds(other * hidden_half, hidden_half)] = (gate / (1.0 + jnp.exp(-gate)) * upper).astype(bf16)
        share = shares[step][:, :1]
        wide = width // 2 if step else body_width // 2

        def out_of(number, carry):
            place = pl.ds(pl.multiple_of(number * wide, wide), wide)
            made = jnp.dot(hidden[...], second[:, place], preferred_element_type=f32)
            results[step, :, place] = (made * share).astype(bf16)
            return carry

        lax.fori_loop(0, body_width // wide if not step else width // wide, out_of, 0)
        if not step:
            made = (jnp.dot(hidden[...], second[:, edge], preferred_element_type=f32) * share).astype(bf16)
            for slot in range(slots):
                gathered[slot, pl.ds(0, capacity)] = made[slot * capacity:(slot + 1) * capacity]

    def shipment(step, slot, inside):
        peer, index = line_peers[inside][step]
        return send(results.at[step, own(slot), edge], gathered.at[slot, own(index)], sent.at[SENT["ship"]], ship_recv.at[slot], peer)

    def ship(step):
        for inside, chosen in ((True, inner), (False, jnp.logical_not(inner))):
            @pl.when(chosen)
            def _(inside=inside):
                for slot in range(slots):
                    shipment(step, slot, inside).start()

    def gather_edges(slot):
        others = gathered.at[slot, pl.ds(capacity, (columns - 1) * capacity)]
        pltpu.make_async_copy(others, others, ship_recv.at[slot]).wait()
        return jnp.dot(edge_spreads[slot], gathered[slot], preferred_element_type=f32)

    merge_in = {}

    def merge(step):
        merged[2] = gather_edges(3).astype(bf16)
        for side in (0, 1):
            merge_in["far", side] = start(send(merged.at[2, :, edge_half[side]], passed_edges.at[side], sent.at[SENT["merge"]], merge_recv.at[0, side], sides[side]))
        for side in (0, 1):
            merged[side] = gather_edges(1 + side).astype(bf16)
            part = edge_half[side]
            merge_in["near", side] = start(send(merged.at[side, :, part], edge_sums.at[side, :, part], sent.at[SENT["merge"]], merge_recv.at[1, side], sides[side]))

    def blend(step):
        for side in (0, 1):
            other = 1 - side
            part = edge_half[side]
            merge_in["far", side].wait_recv()
            blended[other] = (merged[other, :, part].astype(f32) + passed_edges[side].astype(f32)).astype(bf16)
            merge_in["sum", other] = start(send(blended.at[other], edge_sums.at[other, :, part], sent.at[SENT["merge"]], merge_recv.at[2, other], sides[other]))

    def finish(step):
        made = gather_edges(0)
        for side in (0, 1):
            merge_in["near", side].wait_recv()
            merge_in["sum", side].wait_recv()
            made += edge_sums[side].astype(f32)
        output[:, edge] = made.astype(bf16)
        hand_out(0, edge).start()

    far_in, near_in, sum_in = {}, {}, {}

    def hand_far(step):
        for side in (0, 1):
            far_in[step, side] = start(send(results.at[step, own(3), columns_of(side)], relays.at[step, side], sent.at[SENT["far"]], far_recv.at[step, side], sides[side]))

    def hand_near(step):
        for side in (0, 1):
            near_in[step, side] = start(send(results.at[step, own(1 + side), columns_of(side)], compacts.at[step, side], sent.at[SENT["near"]], near_recv.at[step, side], sides[side]))

    def combine(step):
        for side in (0, 1):
            other = 1 - side
            far_in[step, side].wait_recv()
            theirs = spreads[step, 2 + other, 0]
            ours = spreads[step, 2 + other, 1]

            def body(number, carry, side=side, other=other, theirs=theirs, ours=ours):
                place = pl.ds(pl.multiple_of(number * tile, tile), tile)
                shifted = pl.ds(pl.multiple_of(side * split + number * tile, tile), tile)
                made = jnp.dot(theirs, relays[step, side, :, place], preferred_element_type=f32)
                made += jnp.dot(ours, results[step, own(1 + other), shifted], preferred_element_type=f32)
                relayed[step, other, :, place] = made.astype(bf16)
                return carry

            lax.fori_loop(0, split // tile, body, 0)
            sum_in[step, other] = start(send(relayed.at[step, other], sums.at[step, other], sent.at[SENT["sum"]], sum_recv.at[step, other], sides[other]))

    FAR_SUM, BACK_SUM, LAST_SUM, BESIDE_SUM, ACROSS_SUM = range(5)
    routes = {
        True: {1: (beside, BESIDE_SUM), 2: (across, ACROSS_SUM), 3: (across, BACK_SUM)},
        False: {1: (beside, BESIDE_SUM), 2: (beside, LAST_SUM), 3: (beside, FAR_SUM)},
    }
    added = {
        True: {3: (FAR_SUM,), 2: (LAST_SUM,), 1: (BACK_SUM,), 0: (BESIDE_SUM, ACROSS_SUM)},
        False: {3: (), 2: (), 1: (), 0: (BESIDE_SUM,)},
    }

    cut = (split // LANES + 1) // 2 * LANES
    parts = ((0, cut), (cut, split - cut))

    def give(step, side, part, inside):
        peer, inbox = routes[inside][step]
        place = pl.ds(side * split + parts[part][0], parts[part][1])
        return send(
            totals.at[step - 1, :, place], finals.at[inbox, :, place], sent.at[SENT["end"]], end_recv.at[inbox, side, part], peer)

    def given(inbox, side, part):
        place = pl.ds(side * split + parts[part][0], parts[part][1])
        return send(
            totals.at[0, :, place], finals.at[inbox, :, place], sent.at[SENT["end"]], end_recv.at[inbox, side, part], beside)

    def hand_out(number, place):
        return pltpu.make_async_copy(output.at[:, place], out_ref.at[:, place], load_sem.at[number])

    def collect(step):
        for side in (0, 1):
            other = 1 - side
            near_in[step, side].wait_recv()
            sum_in[step, other].wait_recv()

            def total(inside, side=side, other=other):
                for part, (base, size) in enumerate(parts):
                    for inbox in added[inside][step]:
                        given(inbox, side, part).wait_recv()
                    place = pl.ds(base, size)
                    shifted = pl.ds(side * split + base, size)
                    made = jnp.dot(spreads[step, other, 0], compacts[step, side, :, place], preferred_element_type=f32)
                    made += jnp.dot(spreads[step, 0, 1], results[step, own(0), shifted], preferred_element_type=f32)
                    made += sums[step, other, :, place].astype(f32)
                    for inbox in added[inside][step]:
                        made += finals[inbox, :, shifted].astype(f32)
                    target = totals.at[step - 1] if step else output
                    target[:, shifted] = made.astype(bf16)
                    if step:
                        give(step, side, part, inside).start()
                    else:
                        hand_out(1 + 2 * side + part, shifted).start()

            @pl.when(inner)
            def _(total=total):
                total(True)

            @pl.when(jnp.logical_not(inner))
            def _(total=total):
                total(False)

    table = {
        "pass": pass_on, "issue": issue, "relay": relay, "compute": compute, "far": hand_far, "near": hand_near,
        "combine": combine, "collect": collect, "spread": spread_edges, "deal": deal, "dsend": deal_out, "ship": ship, "merge": merge,
        "blend": blend, "finish": finish,
    }
    def settle(name, held):
        pltpu.make_async_copy(held, held, sent.at[SENT[name]]).wait()

    for word in ORDER:
        if word == ORDER[-1]:
            for copy in everything:
                copy.wait_send()
            settle("half", halves)
            settle("note", tables.at[:, pl.ds(1, slots - 1)])
            settle("pack", outs)
            settle("pass", passes)
            settle("far", relays)
            settle("deal", dealt)
            settle("ship", gathered.at[:, pl.ds(capacity, (columns - 1) * capacity)])
            settle("edge", merged)

            @pl.when(inner)
            def _():
                settle("line", finals)
                for copy in (list_across, *list_on):
                    copy.wait_send()

            @pl.when(jnp.logical_not(inner))
            def _():
                settle("line", dense.at[1])
        table[word[:-1]](int(word[-1]))

    settle("near", compacts)
    settle("sum", sums)
    settle("end", totals)
    settle("merge", merged)
    hand_out(0, edge).wait()
    for side in (0, 1):
        for part, (base, size) in enumerate(parts):
            hand_out(1 + 2 * side + part, pl.ds(side * split + base, size)).wait()


NAMES = ("half", "note", "pack", "pass", "far", "near", "sum", "end", "edge", "deal", "ship", "merge", "line")
SENT = {name: number for number, name in enumerate(NAMES)}

ORDER = (
    "spread0", "issue0", "relay0", "pass2", "pass1", "deal0",
    "issue1", "compute0", "relay1", "issue2", "dsend2", "pass3",
    "relay2", "issue3", "dsend1", "dsend3", "relay3", "compute2",
    "far2", "ship2", "near2", "compute3", "far3", "ship3",
    "combine2", "compute1", "ship1", "far1", "near3", "combine3",
    "near1", "far0", "collect2", "combine1", "near0", "collect3",
    "merge0", "combine0", "collect1", "blend0", "collect0", "finish0",
)


def by_rows(tokens, expert_ids, gate_weights, w_gate, w_up, w_down):
    nodes, columns = lax.axis_size("node"), lax.axis_size("local") // 2
    experts = nodes * columns
    count, width = tokens.shape
    choices = expert_ids.shape[1]
    capacity = capacity_of(count, choices, experts)
    hidden_half = w_gate.shape[1]
    extra = width * 3 // 16
    body_width = width - extra
    split = body_width // 2
    dma = pltpu.SemaphoreType.DMA
    bf16, f32 = jnp.bfloat16, jnp.float32
    scratch = [
        pltpu.VMEM((choices, count), jnp.int32),
        pltpu.VMEM((choices, count), f32),
        pltpu.VMEM((columns, 4, experts, LANES), f32),
        pltpu.VMEM((columns, 4 * capacity, LANES), f32),
        pltpu.VMEM((columns, 4, 2 * capacity, LANES), bf16),
        pltpu.VMEM((columns, 4, 2, count, capacity), bf16),
        pltpu.VMEM((width, 4 * hidden_half), bf16),
        pltpu.VMEM((2 * hidden_half, width), bf16),
        pltpu.VMEM((columns, count, body_width), bf16),
        pltpu.VMEM((columns, 2, count, split), bf16),
        pltpu.VMEM((columns, 4 * capacity, width), bf16),
        pltpu.VMEM((columns, 2, capacity, split), bf16),
        pltpu.VMEM((columns, 2, capacity, split), bf16),
        pltpu.VMEM((4 * capacity, 4 * hidden_half), f32),
        pltpu.VMEM((4 * capacity, 2 * hidden_half), bf16),
        pltpu.VMEM((columns, 4 * capacity, width), bf16),
        pltpu.VMEM((columns, 2, capacity, split), bf16),
        pltpu.VMEM((columns, 2, capacity, split), bf16),
        pltpu.VMEM((columns, 2, count, split), bf16),
        pltpu.VMEM((columns, 2, count, split), bf16),
        pltpu.VMEM((columns - 1, count, body_width), bf16),
        pltpu.VMEM((5, count, body_width), bf16),
        pltpu.VMEM((count, width), bf16),
        pltpu.VMEM((4, count, extra), bf16),
        pltpu.VMEM((4, columns * capacity, LANES), bf16),
        pltpu.VMEM((4, count, columns * capacity), bf16),
        pltpu.VMEM((columns - 1, 4 * capacity, extra), bf16),
        pltpu.VMEM((4, columns * capacity, extra), bf16),
        pltpu.VMEM((3, count, extra), bf16),
        pltpu.VMEM((2, count, extra // 2), bf16),
        pltpu.VMEM((2, count, extra // 2), bf16),
        pltpu.VMEM((2, count, extra), bf16),
        dma((7,)), dma((3,)), dma((3,)), dma((columns,)), dma((5,)), dma((columns,)),
        dma((columns, 2)), dma((columns, 3)), dma((columns,)), dma((columns,)),
        dma((columns, 2)), dma((columns, 2)), dma((columns, 2)), dma((5, 2, 2)),
        dma((4,)), dma((columns,)), dma((4,)), dma((3, 2)),
        dma((len(SENT),)), pltpu.SemaphoreType.REGULAR((2,)),
    ]
    flops = 12 * experts * count * width * hidden_half
    return pl.pallas_call(
        functools.partial(layer_kernel, nodes, columns, capacity, extra),
        name="moe_layer",
        out_shape=pltpu.VMEM((count, width), bf16),
        in_specs=[pl.BlockSpec(memory_space=pl.ANY)] * 6,
        out_specs=pl.BlockSpec(memory_space=pl.ANY),
        scratch_shapes=scratch,
        cost_estimate=pl.CostEstimate(flops=flops, bytes_accessed=w_gate.size * 12, transcendentals=0),
        compiler_params=pltpu.CompilerParams(collective_id=0, has_side_effects=True, vmem_limit_bytes=56 << 20),
    )(tokens, expert_ids.T, gate_weights.T, w_gate, w_up, w_down)


def capacity_of(rows, choices, experts):
    return rows * choices * 5 // (4 * experts)


def per_device(tokens, expert_ids, *rest):
    nodes, columns = lax.axis_size("node"), lax.axis_size("local") // 2
    count = tokens.shape[0]
    capacity = capacity_of(count, expert_ids.shape[1], nodes * columns)
    if nodes == 4 and columns == 4 and count <= LANES and capacity % 8 == 0:
        return by_rows(tokens, expert_ids, *rest)
    return by_slots(tokens, expert_ids, *rest)


def solution(mesh):
    placed = (
        P(("parts", "node", "local"), None),
        P(("parts", "node", "local"), None),
        P(("parts", "node", "local"), None),
        P(None, ("parts", "node", "local")),
        P(None, ("parts", "node", "local")),
        P(("parts", "node", "local"), None),
    )
    return jax.shard_map(
        per_device,
        mesh=mesh,
        in_specs=placed,
        out_specs=P(("parts", "node", "local"), None),
        check_vma=False,
    )
```

```python
import functools

import jax
import jax.numpy as jnp
from jax import lax
from jax.experimental import pallas as pl
from jax.experimental.pallas import tpu as pltpu
from jax.sharding import PartitionSpec as P

MESH = pl.DeviceIdType.MESH


def partner_2(value, axis, bit):
    mask = 2**bit
    pairs = [(source, source ^ mask) for source in range(lax.axis_size(axis))]
    return lax.ppermute(value, axis, pairs)


def by_slots(tokens, expert_ids, gate_weights, w_gate, w_up, w_down):
    node_count = lax.axis_size("node")
    local_count = lax.axis_size("local")
    devices = node_count * local_count
    experts = devices // 2
    tok_rows, top_count = expert_ids.shape
    width = tokens.shape[1]
    capacity = tok_rows * top_count * 5 // (4 * experts)
    flat_ids = expert_ids.reshape(-1)
    one_hot = (flat_ids[:, None] == jnp.arange(experts, dtype=jnp.int32)[None, :]).astype(jnp.int32)
    earlier = jnp.cumsum(one_hot, axis=0) - one_hot
    slot_rank = jnp.sum(earlier * one_hot, axis=1)
    slot_index = (flat_ids * capacity + slot_rank).reshape(tok_rows, top_count)
    slot_table = jnp.any(
        slot_index[None, :, :] == jnp.arange(experts * capacity, dtype=jnp.int32)[:, None, None],
        axis=2,
    ).astype(jnp.bfloat16)
    outgoing = jnp.dot(slot_table, tokens, preferred_element_type=jnp.float32).astype(jnp.bfloat16)
    outgoing = outgoing.reshape(devices, capacity // 2, width)
    partner = partner_2((w_gate, w_up, w_down), "local", 0)
    full_gate = jnp.concatenate([w_gate, partner[0]], axis=1)
    full_up = jnp.concatenate([w_up, partner[1]], axis=1)
    full_down = jnp.concatenate([w_down, partner[2]], axis=0)
    block = lax.all_to_all(outgoing, ("node", "local"), split_axis=0, concat_axis=0, tiled=True)
    rows = block.reshape(-1, width)
    gate = jnp.dot(rows, full_gate, preferred_element_type=jnp.float32)
    upper = jnp.dot(rows, full_up, preferred_element_type=jnp.float32)
    hidden = (jax.nn.silu(gate) * upper).astype(jnp.bfloat16)
    result = jnp.dot(hidden, full_down, preferred_element_type=jnp.float32).astype(jnp.bfloat16)
    processed = result.reshape(block.shape)
    returned = lax.all_to_all(processed, ("node", "local"), split_axis=0, concat_axis=0, tiled=True)
    results = returned.reshape(experts * capacity, width)
    chosen = results[slot_index]
    mixed = jnp.sum(gate_weights[:, :, None] * chosen.astype(jnp.float32), axis=1)
    return mixed.astype(jnp.bfloat16)


LANES = 128


def layer_kernel(
    nodes, columns, capacity, extra,
    rows_ref, ids_ref, weights_ref, gate_ref, up_ref, down_ref, out_ref,
    ids, weights, tables, shares, picks, spreads,
    first, second, dense, halves, packed, outs, passes, acts, hidden,
    results, relays, compacts, relayed, sums, totals, finals, output,
    edges, edge_picks, edge_spreads, dealt, gathered, merged, passed_edges, blended, edge_sums,
    load_sem, swap_send, swap_recv, line_recv, list_send, list_recv, half_recv, note_recv, pack_recv, pass_recv,
    far_recv, near_recv, sum_recv, end_recv, edge_recv, deal_recv, ship_recv, merge_recv, sent, ready,
):
    part, node, local = lax.axis_index("parts"), lax.axis_index("node"), lax.axis_index("local")
    column, core = local // 2, lax.rem(local, 2)
    high, low = node // 2, lax.rem(node, 2)
    count, width = rows_ref.shape
    hidden_half = gate_ref.shape[1]
    body_width = width - extra
    split = body_width // 2
    slots = 4
    bf16, f32 = jnp.bfloat16, jnp.float32
    inner = (column == 1) | (column == 2)

    def at(node_index, local_index):
        return (part, node_index, local_index)

    sides = (at(high * 2 + 1 - low, local), at((1 - high) * 2 + low, local))
    side_nodes = (high * 2 + 1 - low, (1 - high) * 2 + low)
    twin = at(node, column * 2 + 1 - core)
    low_flip = column + 1 - 2 * lax.rem(column, 2)
    beside = at(node, low_flip * 2 + core)
    across = at(node, (columns - 1 - column) * 2 + core)
    apart = at(node, (columns - 1 - low_flip) * 2 + core)
    later = jnp.where(inner, 2, 3)

    barrier = pltpu.get_barrier_semaphore()
    greeted = (*sides, twin, beside)
    for peer in greeted:
        pl.semaphore_signal(barrier, inc=1, device_id=peer, device_id_type=MESH)

    @pl.when(inner)
    def _():
        pl.semaphore_signal(barrier, inc=1, device_id=across, device_id_type=MESH)
        pl.semaphore_wait(barrier, len(greeted) + 1)
        pl.semaphore_signal(ready.at[0], inc=1, device_id=beside, device_id_type=MESH)
        pl.semaphore_signal(ready.at[1], inc=1, device_id=across, device_id_type=MESH)

    @pl.when(jnp.logical_not(inner))
    def _():
        pl.semaphore_wait(barrier, len(greeted))

    everything, inner_only = [], []

    def send(source, target, send_sem, recv_sem, peer):
        return pltpu.make_async_remote_copy(
            src_ref=source, dst_ref=target, send_sem=send_sem, recv_sem=recv_sem,
            device_id=peer, device_id_type=MESH,
        )

    def start(copy):
        copy.start()
        return copy

    def kept(copy):
        everything.append(copy)
        return start(copy)

    def columns_of(side):
        return pl.ds(side * split, split)

    def own(slot):
        return pl.ds(slot * capacity, capacity)

    body = pl.ds(0, body_width)
    edge = pl.ds(body_width, extra)
    edge_half = (pl.ds(0, extra // 2), pl.ds(extra // 2, extra // 2))

    half_in = {}
    line_in = {}
    list_in = {}
    note_in = {}
    pack_in = {}
    pass_in = {}

    def send_halves(step, source):
        for side in (0, 1):
            half_in[step, side] = start(send(source.at[:, columns_of(side)], halves.at[step, side], sent.at[SENT["half"]], half_recv.at[step, side], sides[side]))

    edge_in = {}
    for side in (0, 1):
        edge_in[side] = start(send(rows_ref.at[:, edge], edges.at[1 + side], sent.at[SENT["edge"]], edge_recv.at[side], sides[side]))
    send_halves(0, rows_ref)
    line_in[1] = start(send(rows_ref.at[:, body], dense.at[1], sent.at[SENT["line"]], line_recv.at[1], beside))
    to_across = send(rows_ref.at[:, body], dense.at[2], sent.at[SENT["line"]], line_recv.at[2], across)
    pass_across = send(dense.at[1], dense.at[3], sent.at[SENT["line"]], line_recv.at[3], across)
    pass_beside = (
        send(dense.at[2], dense.at[2], sent.at[SENT["line"]], line_recv.at[2], beside),
        send(dense.at[3], dense.at[3], sent.at[SENT["line"]], line_recv.at[3], beside),
    )
    line_in[2], line_in[3] = to_across, pass_across

    @pl.when(inner)
    def _():
        to_across.start()

    first_loads = [
        pltpu.make_async_copy(ids_ref, ids, load_sem.at[0]),
        pltpu.make_async_copy(weights_ref, weights, load_sem.at[1]),
        pltpu.make_async_copy(rows_ref.at[:, body], dense.at[0], load_sem.at[2]),
        pltpu.make_async_copy(rows_ref.at[:, edge], edges.at[0], load_sem.at[6]),
    ]
    for copy in first_loads:
        copy.start()

    def spot(target, index, by_rows, other):
        place = pl.ds((index + other) * hidden_half, hidden_half)
        return target.at[place] if by_rows else target.at[:, place]

    near = ((gate_ref, first, 0, False), (up_ref, first, 1, False), (down_ref, second, 0, True))
    swaps, loads = [], []
    for number, (source, target, index, by_rows) in enumerate(near):
        swaps.append(kept(send(source, spot(target, index, by_rows, 1 if by_rows else 2), swap_send.at[number], swap_recv.at[number], twin)))
        loads.append(pltpu.make_async_copy(source, spot(target, index, by_rows, 0), load_sem.at[3 + number]))
        loads[-1].start()

    for copy in first_loads[:2]:
        copy.wait()
    experts = nodes * columns
    expert_iota = lax.broadcasted_iota(jnp.int32, (experts, count), 0)
    listed = jnp.full((experts, count), -1.0, f32)
    for choice in range(ids.shape[0]):
        listed = jnp.where(ids[pl.ds(choice, 1), :] == expert_iota, weights[pl.ds(choice, 1), :], listed)
    tables[0, 0] = jnp.full((experts, LANES), -1.0, f32)
    tables[0, 0, :, pl.ds(0, count)] = listed

    list_in[1] = kept(send(tables.at[0, 0], tables.at[1, 0], list_send.at[0], list_recv.at[1], beside))
    list_across = send(tables.at[0, 0], tables.at[2, 0], list_send.at[1], list_recv.at[2], across)
    list_on = (
        send(tables.at[1, 0], tables.at[3, 0], list_send.at[2], list_recv.at[3], across),
        send(tables.at[2, 0], tables.at[2, 0], list_send.at[3], list_recv.at[2], beside),
        send(tables.at[3, 0], tables.at[3, 0], list_send.at[4], list_recv.at[3], beside),
    )
    list_in[2], list_in[3] = list_across, list_on[0]

    @pl.when(inner)
    def _():
        list_across.start()

    def send_notes(step):
        for side in (0, 1):
            note_in[step, side] = start(send(tables.at[step, 0], tables.at[step, 1 + side], sent.at[SENT["note"]], note_recv.at[step, 0], sides[side]))

    before = (lax.broadcasted_iota(jnp.int32, (LANES, LANES), 0) < lax.broadcasted_iota(jnp.int32, (LANES, LANES), 1)).astype(bf16)
    places = lax.broadcasted_iota(jnp.int32, (capacity, LANES), 0).astype(f32)
    mirror = (lax.broadcasted_iota(jnp.int32, (count, LANES), 0) == lax.broadcasted_iota(jnp.int32, (count, LANES), 1)).astype(bf16)
    mine = node * columns + column
    near_experts = tuple(side_node * columns + column for side_node in side_nodes)
    line_experts = (mine, node * columns + low_flip, node * columns + (columns - 1 - column), node * columns + (columns - 1 - low_flip))

    def prepare(step, slot, wanted):
        table = tables[step, slot]
        rank = jnp.dot((table >= 0).astype(bf16), before, preferred_element_type=f32)
        rank = jnp.where(table >= 0, rank, -1.0)
        rows_iota = lax.broadcasted_iota(jnp.int32, table.shape, 0)
        for expert, index in wanted:
            chosen = rows_iota == expert
            row = jnp.sum(jnp.where(chosen, rank, 0.0), axis=0, keepdims=True)
            pick = (places == row).astype(f32)
            if index is None or index[1]:
                value = jnp.sum(jnp.where(chosen, table, 0.0), axis=0, keepdims=True)
                share = jnp.sum(pick * value, axis=1, keepdims=True)
                shares[step, own(slot)] = jnp.broadcast_to(share, (capacity, LANES))
            if index is not None:
                picked = pick.astype(bf16)
                picks[step, index[0], pl.ds(index[2] * capacity, capacity)] = picked
                spreads[step, index[0], index[2]] = lax.dot_general(
                    mirror, picked, (((1,), (1,)), ((), ())), preferred_element_type=f32).astype(bf16)

    tile = split

    def compress(step, index, source, targets):
        wanted = picks[step, index][:, :count]

        def body(number, carry):
            place = pl.ds(pl.multiple_of(number * tile, tile), tile)
            made = jnp.dot(wanted, source[:, place], preferred_element_type=f32).astype(bf16)
            for which, target in enumerate(targets):
                target[:, place] = made[which * capacity:(which + 1) * capacity]
            return carry

        lax.fori_loop(0, split // tile, body, 0)

    passed = {}

    def pass_on(step):
        passed[step] = True

        @pl.when(inner)
        def _():
            line_in[step].wait_recv()
            (pass_across, *pass_beside)[step - 1].start()
            list_in[step].wait_recv()
            list_on[step - 1].start()
            if step == 1:
                pl.semaphore_wait(ready.at[1], 1)
                pl.semaphore_signal(ready.at[1], inc=1, device_id=beside, device_id_type=MESH)

    def issue(step):
        if step:
            @pl.when(jnp.logical_not(inner) | (step not in passed))
            def _():
                line_in[step].wait_recv()
                list_in[step].wait_recv()

            send_halves(step, dense.at[step])
        send_notes(step)
        prepare(step, 0, ((near_experts[1], (0, False, 0)), (mine, (0, True, 1)), (near_experts[0], (1, False, 0))))
        picks[step, 1, pl.ds(capacity, capacity)] = picks[step, 0, pl.ds(capacity, capacity)]
        if not step:
            first_loads[2].wait()
        for half, side in ((0, 1), (1, 0)):
            compress(step, half, dense.at[step, :, columns_of(half)], (outs.at[step, side], packed.at[step, own(0), columns_of(half)]))
            pack_in[step, side] = start(send(outs.at[step, side], packed.at[step, own(1 + side), columns_of(half)], sent.at[SENT["pack"]], pack_recv.at[step], sides[side]))

    def spread_edges(step):
        for side in (0, 1):
            edge_in[side].wait_recv()
            part = edge_half[side]
            edge_in[2 + side] = start(send(edges.at[1 + side, :, part], edges.at[3, :, part], sent.at[SENT["edge"]], edge_recv.at[2 + side], sides[1 - side]))

    line_peers = {
        True: {1: (beside, 1), 2: (across, 2), 3: (apart, 3)},
        False: {1: (beside, 1), 2: (apart, 3), 3: (across, 2)},
    }

    def deal(step):
        first_loads[3].wait()
        note_in[0, 2].wait_recv()

        @pl.when(jnp.logical_not(inner))
        def _():
            pl.semaphore_wait(ready.at[0], 1)
            pl.semaphore_wait(ready.at[1], 1)

        for slot in range(slots):
            table = tables[0, slot]
            rank = jnp.dot((table >= 0).astype(bf16), before, preferred_element_type=f32)
            rank = jnp.where(table >= 0, rank, -1.0)
            rows_iota = lax.broadcasted_iota(jnp.int32, table.shape, 0)
            for index, expert in enumerate(line_experts):
                row = jnp.sum(jnp.where(rows_iota == expert, rank, 0.0), axis=0, keepdims=True)
                edge_picks[slot, own(index)] = (places == row).astype(bf16)
            edge_spreads[slot] = lax.dot_general(
                mirror, edge_picks[slot], (((1,), (1,)), ((), ())), preferred_element_type=f32).astype(bf16)
        for side in (0, 1):
            edge_in[2 + side].wait_recv()
        for slot in range(slots):
            made = jnp.dot(edge_picks[slot][:, :count], edges[slot], preferred_element_type=f32).astype(bf16)
            packed[0, own(slot), edge] = made[:capacity]
            for index in (1, 2, 3):
                dealt[index - 1, own(slot)] = made[index * capacity:(index + 1) * capacity]

    def deal_out(step):
        for inside, chosen in ((True, inner), (False, jnp.logical_not(inner))):
            @pl.when(chosen)
            def _(inside=inside):
                dealing(step, inside).start()

    def dealing(step, inside):
        peer, index = line_peers[inside][step]
        target = 1 if step == 1 else later
        return send(dealt.at[index - 1], packed.at[target, :, edge], sent.at[SENT["deal"]], deal_recv.at[target], peer)

    def relay(step):
        for side in (0, 1):
            other = 1 - side
            if not side:
                both = tables.at[step, pl.ds(1, 2)]
                pltpu.make_async_copy(both, both, note_recv.at[step, 0]).wait()
                note_in[step, 2] = start(send(tables.at[step, 1], tables.at[step, 3], sent.at[SENT["note"]], note_recv.at[step, 1], sides[1]))
            prepare(step, 1 + side, ((near_experts[other], (2 + side, False, 0)), (mine, (2 + side, True, 1))))
            half_in[step, side].wait_recv()
            compress(step, 2 + side, halves.at[step, side], (passes.at[step, side], packed.at[step, own(1 + side), columns_of(side)]))
            pass_in[step, side] = start(send(passes.at[step, side], packed.at[step, own(3), columns_of(side)], sent.at[SENT["pass"]], pass_recv.at[step], sides[other]))

    def compute(step):
        if step:
            note_in[step, 2].wait_recv()
        prepare(step, 3, ((mine, None),))
        pltpu.make_async_copy(outs.at[step], outs.at[step], pack_recv.at[step]).wait()
        pltpu.make_async_copy(passes.at[step], passes.at[step], pass_recv.at[step]).wait()
        if step:
            pltpu.make_async_remote_copy(
                src_ref=dealt.at[0], dst_ref=packed.at[step, :, edge], send_sem=sent.at[SENT["deal"]], recv_sem=deal_recv.at[step],
                device_id=beside, device_id_type=MESH,
            ).wait_recv()
        if not step:
            for copy in swaps:
                copy.wait_recv()
            for copy in loads:
                copy.wait()
        for part in (0, 1):
            place = pl.ds(part * 2 * hidden_half, 2 * hidden_half)
            acts[:, place] = jnp.dot(packed[step], first[:, place], preferred_element_type=f32)
        for other in (0, 1):
            gate = acts[:, pl.ds(2 * other * hidden_half, hidden_half)]
            upper = acts[:, pl.ds((2 * other + 1) * hidden_half, hidden_half)]
            hidden[:, pl.ds(other * hidden_half, hidden_half)] = (gate / (1.0 + jnp.exp(-gate)) * upper).astype(bf16)
        share = shares[step][:, :1]
        wide = width // 2 if step else body_width // 2

        def out_of(number, carry):
            place = pl.ds(pl.multiple_of(number * wide, wide), wide)
            made = jnp.dot(hidden[...], second[:, place], preferred_element_type=f32)
            results[step, :, place] = (made * share).astype(bf16)
            return carry

        lax.fori_loop(0, body_width // wide if not step else width // wide, out_of, 0)
        if not step:
            made = (jnp.dot(hidden[...], second[:, edge], preferred_element_type=f32) * share).astype(bf16)
            for slot in range(slots):
                gathered[slot, pl.ds(0, capacity)] = made[slot * capacity:(slot + 1) * capacity]

    def shipment(step, slot, inside):
        peer, index = line_peers[inside][step]
        return send(results.at[step, own(slot), edge], gathered.at[slot, own(index)], sent.at[SENT["ship"]], ship_recv.at[slot], peer)

    def ship(step):
        for inside, chosen in ((True, inner), (False, jnp.logical_not(inner))):
            @pl.when(chosen)
            def _(inside=inside):
                for slot in range(slots):
                    shipment(step, slot, inside).start()

    def gather_edges(slot):
        others = gathered.at[slot, pl.ds(capacity, (columns - 1) * capacity)]
        pltpu.make_async_copy(others, others, ship_recv.at[slot]).wait()
        return jnp.dot(edge_spreads[slot], gathered[slot], preferred_element_type=f32)

    merge_in = {}

    def merge(step):
        merged[2] = gather_edges(3).astype(bf16)
        for side in (0, 1):
            merge_in["far", side] = start(send(merged.at[2, :, edge_half[side]], passed_edges.at[side], sent.at[SENT["merge"]], merge_recv.at[0, side], sides[side]))
        for side in (0, 1):
            merged[side] = gather_edges(1 + side).astype(bf16)
            part = edge_half[side]
            merge_in["near", side] = start(send(merged.at[side, :, part], edge_sums.at[side, :, part], sent.at[SENT["merge"]], merge_recv.at[1, side], sides[side]))

    def blend(step):
        for side in (0, 1):
            other = 1 - side
            part = edge_half[side]
            merge_in["far", side].wait_recv()
            blended[other] = (merged[other, :, part].astype(f32) + passed_edges[side].astype(f32)).astype(bf16)
            merge_in["sum", other] = start(send(blended.at[other], edge_sums.at[other, :, part], sent.at[SENT["merge"]], merge_recv.at[2, other], sides[other]))

    def finish(step):
        made = gather_edges(0)
        for side in (0, 1):
            merge_in["near", side].wait_recv()
            merge_in["sum", side].wait_recv()
            made += edge_sums[side].astype(f32)
        output[:, edge] = made.astype(bf16)
        hand_out(0, edge).start()

    far_in, near_in, sum_in = {}, {}, {}

    def hand_far(step):
        for side in (0, 1):
            far_in[step, side] = start(send(results.at[step, own(3), columns_of(side)], relays.at[step, side], sent.at[SENT["far"]], far_recv.at[step, side], sides[side]))

    def hand_near(step):
        for side in (0, 1):
            near_in[step, side] = start(send(results.at[step, own(1 + side), columns_of(side)], compacts.at[step, side], sent.at[SENT["near"]], near_recv.at[step, side], sides[side]))

    def combine(step):
        for side in (0, 1):
            other = 1 - side
            far_in[step, side].wait_recv()
            theirs = spreads[step, 2 + other, 0]
            ours = spreads[step, 2 + other, 1]

            def body(number, carry, side=side, other=other, theirs=theirs, ours=ours):
                place = pl.ds(pl.multiple_of(number * tile, tile), tile)
                shifted = pl.ds(pl.multiple_of(side * split + number * tile, tile), tile)
                made = jnp.dot(theirs, relays[step, side, :, place], preferred_element_type=f32)
                made += jnp.dot(ours, results[step, own(1 + other), shifted], preferred_element_type=f32)
                relayed[step, other, :, place] = made.astype(bf16)
                return carry

            lax.fori_loop(0, split // tile, body, 0)
            sum_in[step, other] = start(send(relayed.at[step, other], sums.at[step, other], sent.at[SENT["sum"]], sum_recv.at[step, other], sides[other]))

    FAR_SUM, BACK_SUM, LAST_SUM, BESIDE_SUM, ACROSS_SUM = range(5)
    routes = {
        True: {1: (beside, BESIDE_SUM), 2: (across, ACROSS_SUM), 3: (across, BACK_SUM)},
        False: {1: (beside, BESIDE_SUM), 2: (beside, LAST_SUM), 3: (beside, FAR_SUM)},
    }
    added = {
        True: {3: (FAR_SUM,), 2: (LAST_SUM,), 1: (BACK_SUM,), 0: (BESIDE_SUM, ACROSS_SUM)},
        False: {3: (), 2: (), 1: (), 0: (BESIDE_SUM,)},
    }

    cut = (split // LANES + 1) // 2 * LANES
    parts = ((0, cut), (cut, split - cut))

    def give(step, side, part, inside):
        peer, inbox = routes[inside][step]
        place = pl.ds(side * split + parts[part][0], parts[part][1])
        return send(
            totals.at[step - 1, :, place], finals.at[inbox, :, place], sent.at[SENT["end"]], end_recv.at[inbox, side, part], peer)

    def given(inbox, side, part):
        place = pl.ds(side * split + parts[part][0], parts[part][1])
        return send(
            totals.at[0, :, place], finals.at[inbox, :, place], sent.at[SENT["end"]], end_recv.at[inbox, side, part], beside)

    def hand_out(number, place):
        return pltpu.make_async_copy(output.at[:, place], out_ref.at[:, place], load_sem.at[number])

    def collect(step):
        for side in (0, 1):
            other = 1 - side
            near_in[step, side].wait_recv()
            sum_in[step, other].wait_recv()

            def total(inside, side=side, other=other):
                for part, (base, size) in enumerate(parts):
                    for inbox in added[inside][step]:
                        given(inbox, side, part).wait_recv()
                    place = pl.ds(base, size)
                    shifted = pl.ds(side * split + base, size)
                    made = jnp.dot(spreads[step, other, 0], compacts[step, side, :, place], preferred_element_type=f32)
                    made += jnp.dot(spreads[step, 0, 1], results[step, own(0), shifted], preferred_element_type=f32)
                    made += sums[step, other, :, place].astype(f32)
                    for inbox in added[inside][step]:
                        made += finals[inbox, :, shifted].astype(f32)
                    target = totals.at[step - 1] if step else output
                    target[:, shifted] = made.astype(bf16)
                    if step:
                        give(step, side, part, inside).start()
                    else:
                        hand_out(1 + 2 * side + part, shifted).start()

            @pl.when(inner)
            def _(total=total):
                total(True)

            @pl.when(jnp.logical_not(inner))
            def _(total=total):
                total(False)

    table = {
        "pass": pass_on, "issue": issue, "relay": relay, "compute": compute, "far": hand_far, "near": hand_near,
        "combine": combine, "collect": collect, "spread": spread_edges, "deal": deal, "dsend": deal_out, "ship": ship, "merge": merge,
        "blend": blend, "finish": finish,
    }
    def settle(name, held):
        pltpu.make_async_copy(held, held, sent.at[SENT[name]]).wait()

    for word in ORDER:
        if word == ORDER[-1]:
            for copy in everything:
                copy.wait_send()
            settle("half", halves)
            settle("note", tables.at[:, pl.ds(1, slots - 1)])
            settle("pack", outs)
            settle("pass", passes)
            settle("far", relays)
            settle("deal", dealt)
            settle("ship", gathered.at[:, pl.ds(capacity, (columns - 1) * capacity)])
            settle("edge", merged)

            @pl.when(inner)
            def _():
                settle("line", finals)
                for copy in (list_across, *list_on):
                    copy.wait_send()

            @pl.when(jnp.logical_not(inner))
            def _():
                settle("line", dense.at[1])
        table[word[:-1]](int(word[-1]))

    settle("near", compacts)
    settle("sum", sums)
    settle("end", totals)
    settle("merge", merged)
    hand_out(0, edge).wait()
    for side in (0, 1):
        for part, (base, size) in enumerate(parts):
            hand_out(1 + 2 * side + part, pl.ds(side * split + base, size)).wait()


NAMES = ("half", "note", "pack", "pass", "far", "near", "sum", "end", "edge", "deal", "ship", "merge", "line")
SENT = {name: number for number, name in enumerate(NAMES)}

ORDER = (
    "spread0", "issue0", "relay0", "pass2", "pass1", "deal0",
    "issue1", "compute0", "relay1", "issue2", "dsend2", "pass3",
    "relay2", "issue3", "dsend1", "dsend3", "relay3", "compute2",
    "far2", "ship2", "near2", "compute3", "far3", "ship3",
    "combine2", "compute1", "ship1", "far1", "near3", "combine3",
    "near1", "far0", "collect2", "combine1", "near0", "collect3",
    "merge0", "combine0", "collect1", "blend0", "collect0", "finish0",
)


def by_rows(tokens, expert_ids, gate_weights, w_gate, w_up, w_down):
    nodes, columns = lax.axis_size("node"), lax.axis_size("local") // 2
    experts = nodes * columns
    count, width = tokens.shape
    choices = expert_ids.shape[1]
    capacity = capacity_of(count, choices, experts)
    hidden_half = w_gate.shape[1]
    extra = width * 3 // 16
    body_width = width - extra
    split = body_width // 2
    dma = pltpu.SemaphoreType.DMA
    bf16, f32 = jnp.bfloat16, jnp.float32
    scratch = [
        pltpu.VMEM((choices, count), jnp.int32),
        pltpu.VMEM((choices, count), f32),
        pltpu.VMEM((columns, 4, experts, LANES), f32),
        pltpu.VMEM((columns, 4 * capacity, LANES), f32),
        pltpu.VMEM((columns, 4, 2 * capacity, LANES), bf16),
        pltpu.VMEM((columns, 4, 2, count, capacity), bf16),
        pltpu.VMEM((width, 4 * hidden_half), bf16),
        pltpu.VMEM((2 * hidden_half, width), bf16),
        pltpu.VMEM((columns, count, body_width), bf16),
        pltpu.VMEM((columns, 2, count, split), bf16),
        pltpu.VMEM((columns, 4 * capacity, width), bf16),
        pltpu.VMEM((columns, 2, capacity, split), bf16),
        pltpu.VMEM((columns, 2, capacity, split), bf16),
        pltpu.VMEM((4 * capacity, 4 * hidden_half), f32),
        pltpu.VMEM((4 * capacity, 2 * hidden_half), bf16),
        pltpu.VMEM((columns, 4 * capacity, width), bf16),
        pltpu.VMEM((columns, 2, capacity, split), bf16),
        pltpu.VMEM((columns, 2, capacity, split), bf16),
        pltpu.VMEM((columns, 2, count, split), bf16),
        pltpu.VMEM((columns, 2, count, split), bf16),
        pltpu.VMEM((columns - 1, count, body_width), bf16),
        pltpu.VMEM((5, count, body_width), bf16),
        pltpu.VMEM((count, width), bf16),
        pltpu.VMEM((4, count, extra), bf16),
        pltpu.VMEM((4, columns * capacity, LANES), bf16),
        pltpu.VMEM((4, count, columns * capacity), bf16),
        pltpu.VMEM((columns - 1, 4 * capacity, extra), bf16),
        pltpu.VMEM((4, columns * capacity, extra), bf16),
        pltpu.VMEM((3, count, extra), bf16),
        pltpu.VMEM((2, count, extra // 2), bf16),
        pltpu.VMEM((2, count, extra // 2), bf16),
        pltpu.VMEM((2, count, extra), bf16),
        dma((7,)), dma((3,)), dma((3,)), dma((columns,)), dma((5,)), dma((columns,)),
        dma((columns, 2)), dma((columns, 2)), dma((columns,)), dma((columns,)),
        dma((columns, 2)), dma((columns, 2)), dma((columns, 2)), dma((5, 2, 2)),
        dma((4,)), dma((columns,)), dma((4,)), dma((3, 2)),
        dma((len(SENT),)), pltpu.SemaphoreType.REGULAR((2,)),
    ]
    flops = 12 * experts * count * width * hidden_half
    return pl.pallas_call(
        functools.partial(layer_kernel, nodes, columns, capacity, extra),
        name="moe_layer",
        out_shape=pltpu.VMEM((count, width), bf16),
        in_specs=[pl.BlockSpec(memory_space=pl.ANY)] * 6,
        out_specs=pl.BlockSpec(memory_space=pl.ANY),
        scratch_shapes=scratch,
        cost_estimate=pl.CostEstimate(flops=flops, bytes_accessed=w_gate.size * 12, transcendentals=0),
        compiler_params=pltpu.CompilerParams(collective_id=0, has_side_effects=True, vmem_limit_bytes=56 << 20),
    )(tokens, expert_ids.T, gate_weights.T, w_gate, w_up, w_down)


def capacity_of(rows, choices, experts):
    return rows * choices * 5 // (4 * experts)


def per_device(tokens, expert_ids, *rest):
    nodes, columns = lax.axis_size("node"), lax.axis_size("local") // 2
    count = tokens.shape[0]
    capacity = capacity_of(count, expert_ids.shape[1], nodes * columns)
    if nodes == 4 and columns == 4 and count <= LANES and capacity % 8 == 0:
        return by_rows(tokens, expert_ids, *rest)
    return by_slots(tokens, expert_ids, *rest)


def solution(mesh):
    placed = (
        P(("parts", "node", "local"), None),
        P(("parts", "node", "local"), None),
        P(("parts", "node", "local"), None),
        P(None, ("parts", "node", "local")),
        P(None, ("parts", "node", "local")),
        P(("parts", "node", "local"), None),
    )
    return jax.shard_map(
        per_device,
        mesh=mesh,
        in_specs=placed,
        out_specs=P(("parts", "node", "local"), None),
        check_vma=False,
    )
```
